32 devices in a mesh: dp: 16 (over z, y, x), mp: 2 (over core).
Axes of the slice: x: 2, y: 2, z: 4, core: 2. Of those that a mesh axis runs over, the one named last changes fastest.
Arguments:
- text: bfloat16 [16000, 768], P('dp', 'mp'), may hold values from -6 to 6
- patches: bfloat16 [400, 145, 1024], P('dp'), may hold values from -6 to 6
- segment_ids: int32 [400, 40], P('dp'), may hold values from 0 to 4, never falling along the last dimension, each value on 1 to 20 neighbouring positions
- row_image: int32 [400], P('dp'), may hold values from 0 to 399, as said below
- self_qkv: bfloat16 [3, 768, 768], P(None, None, 'mp'), may hold values from -0.21875 to 0.21875
- self_bias: bfloat16 [2, 768], P(None, 'mp'), may hold values from -3 to 3
- self_out: bfloat16 [768, 768], P('mp'), may hold values from -0.4375 to 0.4375
- cross_query: bfloat16 [768, 768], P(None, 'mp'), may hold values from -0.21875 to 0.21875
- cross_bias: bfloat16 [2, 768], P(None, 'mp'), may hold values from -3 to 3
- cross_kv: bfloat16 [2, 1024, 768], P(None, None, 'mp'), may hold values from -0.1875 to 0.1875
- cross_out: bfloat16 [768, 768], P('mp'), may hold values from -1.25 to 1.25
- ffn_in: bfloat16 [768, 3072], P(None, 'mp'), may hold values from -0.21875 to 0.21875
- ffn_in_bias: bfloat16 [3072], P('mp'), may hold values from -3 to 3
- ffn_out: bfloat16 [3072, 768], P('mp'), may hold values from -0.109375 to 0.109375
- branch_bias: bfloat16 [3, 768], P(None, 'mp'), may hold values from -3 to 3
- norm_gain: bfloat16 [3, 768], P(None, 'mp'), may hold values from 0.25 to 1.75
- norm_bias: bfloat16 [3, 768], P(None, 'mp'), may hold values from -3 to 3
- cotangent: bfloat16 [16000, 768], P('dp', 'mp'), may hold values from -6 to 6
Outputs:
- joined: float32 [16000, 768], P('dp', 'mp')
- text_grad: float32 [16000, 768], P('dp', 'mp')
- patch_grad: float32 [400, 145, 1024], P('dp', None, 'mp')
- grad_self_qkv: float32 [3, 768, 768], P(None, 'dp', 'mp')
- grad_self_bias: float32 [2, 768], P(None, 'mp')
- grad_self_out: float32 [768, 768], P('mp', 'dp')
- grad_cross_query: float32 [768, 768], P('dp', 'mp')
- grad_cross_bias: float32 [2, 768], P(None, 'mp')
- grad_cross_kv: float32 [2, 1024, 768], P(None, 'dp', 'mp')
- grad_cross_out: float32 [768, 768], P('mp', 'dp')
- grad_ffn_in: float32 [768, 3072], P('dp', 'mp')
- grad_ffn_in_bias: float32 [3072], P('mp')
- grad_ffn_out: float32 [3072, 768], P('mp', 'dp')
- grad_branch_bias: float32 [3, 768], P(None, 'mp')
- grad_norm_gain: float32 [3, 768], P(None, 'mp')
- grad_norm_bias: float32 [3, 768], P(None, 'mp')
The draws below stay inside these ranges and needn't reach their ends.
Inputs may be any that keep to these rules, and one draw needn't show every extreme that they name: `segment_ids`: within a row the ids never fall; a token attends only to tokens of its own row with its own id. `row_image`: the image of row r lies among the 25 images that start at r // 25 * 25.
All inputs are finite; a program needn't handle non-finite values.
Results may differ from the reference program's by a relative error of at most 0.024.
Values may be sent and summed in bfloat16 or wider, within the bound.
A program may use at most 256 MiB of HBM per device.

```python
import math
import jax
import jax.numpy as jnp
import numpy as np
from jax import lax

D = 768
HEADS = 12
HD = 64
FF = 3072
DV = 1024
PATCH = 145
SEQ = 40
ROWS_DEV = 25
IMG_DEV = 25
ROWS = 400
TOKENS = 16000
IMAGES = 400
N_DP = 16


def draw_row_image(key, part):
    key_pick = jax.random.fold_in(key, 11)
    key_first = jax.random.fold_in(key, 12)
    key_last = jax.random.fold_in(key, 13)
    block = jnp.arange(ROWS, dtype=jnp.int32) // ROWS_DEV
    pick = jax.random.randint(key_pick, (ROWS,), 0, IMG_DEV, dtype=jnp.int32)
    first = jax.random.randint(key_first, (), 0, ROWS_DEV, dtype=jnp.int32)
    last = ROWS - ROWS_DEV + jax.random.randint(key_last, (), 0, ROWS_DEV, dtype=jnp.int32)
    pick = pick.at[first].set(0).at[last].set(IMG_DEV - 1)
    return block * IMG_DEV + pick


def strengthened(drawn, own_key, source, target, parts, factor):
    def block_of(axis_at):
        return (jnp.arange(drawn.shape[axis_at]) // (drawn.shape[axis_at] // parts)).reshape((-1,) + (1,) * (drawn.ndim - 1 - axis_at))

    one_side = jax.random.permutation(own_key, parts)[block_of(target)]
    second = (block_of(target) + parts // 2) % parts
    return jnp.where((block_of(source) == one_side) | (block_of(source) == second), factor * drawn, drawn)


def block_levels(rng, extent, pieces, low, largest):
    def one(position, parts):
        draws = jax.random.uniform(jax.random.fold_in(jax.random.fold_in(rng, 6), position), (parts,), jnp.float32, low / len(pieces), largest / len(pieces))
        return jnp.repeat(jnp.exp(draws), extent[position] // parts).reshape((-1,) + (1,) * (len(extent) - position - 1))

    factor_of = one(*pieces[0])
    for cut in pieces[1:]:
        factor_of = factor_of * one(*cut)
    return factor_of


def profile(count, total, bound, slope):
    weights = [(1 << 20) // math.isqrt(grade ** slope) + 1 for grade in range(2, count + 1)]
    rest, holding = total - bound - (count - 1), [1] * (count - 1)
    while rest > 0:
        free = [i for i in range(count - 1) if holding[i] < bound]
        whole, left = sum([weights[i] for i in free]), rest
        for i in free:
            extra = min(bound - holding[i], max(1, left * weights[i] // whole), rest)
            holding[i] = holding[i] + extra
            rest = rest - extra
    return np.array([bound] + holding)


def uneven_parts(stream_key, number_of, total, reach, lean):
    if number_of == 2:
        one = jax.random.randint(stream_key, (), max(1, total - reach), min(reach, total - 1) + 1)
        return jnp.stack([one, total - one])
    tallies = jnp.asarray(profile(number_of, total, reach, lean), jnp.int32)
    twos = (number_of - 1) // 2
    source_of, receiver = tallies[1:1 + 2 * twos:2], tallies[2:2 + 2 * twos:2]
    margin = jnp.minimum(source_of - 1, reach - receiver)
    shifted = jax.random.randint(jax.random.fold_in(stream_key, 1), (twos,), 0, 1 << 20) % (margin + 1)
    tallies = tallies.at[1:1 + 2 * twos:2].set(source_of - shifted).at[2:2 + 2 * twos:2].set(receiver + shifted)
    return tallies[jax.random.permutation(jax.random.fold_in(stream_key, 2), number_of)]


def noise(rng, dims, spread, limit, shards=(), kind=jnp.bfloat16):
    loudness = block_levels(rng, dims, shards, -0.22, 0.18) if shards else 1.0
    array = jax.random.normal(rng, dims, jnp.float32) * spread * loudness
    return jnp.minimum(jnp.maximum(array, -limit), limit).astype(kind)


def bell_draw_with(own_key, extent, spread, bound, shards, heavy, kind=jnp.bfloat16):
    entries = spread * jax.random.normal(own_key, extent, jnp.float32)
    if shards:
        entries = entries * block_levels(own_key, extent, shards, -0.22, 0.18)
    return jnp.clip(strengthened(entries, jax.random.fold_in(own_key, 3), *heavy), -bound, bound).astype(kind)


def setup_inputs(seed: int = 0) -> dict:
    streams_of = jax.random.split(jax.random.key(seed), 19)
    return {
        "text": noise(streams_of[0], (TOKENS, D), 1.0, 6.0, ((0, 16), (1, 2))),
        "patches": noise(streams_of[1], (IMAGES, PATCH, DV), 1.0, 6.0, ((0, 16),)),
        "segment_ids": jax.vmap(lambda own: jnp.searchsorted(jnp.cumsum(uneven_parts(own, SEQ // 8, SEQ, SEQ // 2, 1)), jnp.arange(SEQ), side="right"))(jax.random.split(streams_of[2], ROWS)).reshape((ROWS, SEQ)).astype(jnp.int32),
        "row_image": draw_row_image(jax.random.fold_in(streams_of[18], 71), 0),
        "self_qkv": noise(streams_of[4], (3, D, D), D ** -0.5, 0.21875, ((2, 2),)),
        "self_bias": noise(streams_of[5], (2, D), 0.5, 3.0, ((1, 2),)),
        "self_out": noise(streams_of[6], (D, D), (D // 4) ** -0.5, 0.4375, ((0, 2),)),
        "cross_query": noise(streams_of[7], (D, D), D ** -0.5, 0.21875, ((1, 2),)),
        "cross_bias": noise(streams_of[8], (2, D), 0.5, 3.0, ((1, 2),)),
        "cross_kv": noise(streams_of[9], (2, DV, D), DV ** -0.5, 0.1875, ((2, 2),)),
        "cross_out": noise(streams_of[10], (D, D), (D // 32) ** -0.5, 1.25, ((0, 2),)),
        "ffn_in": noise(streams_of[11], (D, FF), D ** -0.5, 0.21875, ((1, 2),)),
        "ffn_in_bias": noise(streams_of[12], (FF,), 0.5, 3.0, ((0, 2),)),
        "ffn_out": noise(streams_of[13], (FF, D), FF ** -0.5, 0.109375, ((0, 2),)),
        "branch_bias": noise(streams_of[14], (3, D), 0.5, 3.0, ((1, 2),)),
        "norm_gain": jnp.clip(1.0 + 0.15 * jax.random.normal(streams_of[15], (3, D), jnp.float32), 0.25, 1.75).astype(jnp.bfloat16),
        "norm_bias": noise(streams_of[16], (3, D), 0.5, 3.0, ((1, 2),)),
        "cotangent": bell_draw_with(streams_of[17], (TOKENS, D), 1.0, 6.0, ((0, 16), (1, 2)), (0, 1, 16, 2.0)),
    }


EPS = 1e-06
BIG_NEG = -1000000000.0
HIGH = lax.Precision.HIGHEST

@jax.custom_vjp
def low(v):
    return lax.optimization_barrier(v.astype(jnp.bfloat16)).astype(jnp.float32)

@jax.custom_vjp
def low_back(v):
    return v

def low_keep(v):
    return (low(v), None)

def low_pass(kept, grad):
    return (grad,)

def back_keep(v):
    return (v, None)

def back_low(kept, grad):
    return (low(grad),)
low.defvjp(low_keep, low_pass)
low_back.defvjp(back_keep, back_low)

def both_ways(value):
    return low(low_back(value))

def dense(left, right):
    return jnp.dot(left, right, precision=HIGH)

def layer_norm(resid, gain, shift):
    mean = lax.optimization_barrier(jnp.mean(resid, axis=-1, keepdims=True))
    square = lax.optimization_barrier(jnp.mean(resid * resid, axis=-1, keepdims=True))
    return (resid - mean) * lax.rsqrt(square - mean * mean + EPS) * gain + shift

def softmax_rows(scores):
    peak = lax.optimization_barrier(jnp.max(scores, axis=-1, keepdims=True))
    weight = jnp.exp(scores - peak)
    return weight / lax.optimization_barrier(jnp.sum(weight, axis=-1, keepdims=True))

def self_block(block):
    query, keys, values, segments = block
    scores = low_back(jnp.einsum('rqhd,rkhd->rhqk', query, keys, precision=HIGH) * 0.125)
    allowed = (segments[:, :, None] == segments[:, None, :])[:, None]
    probs = softmax_rows(jnp.where(allowed, scores, BIG_NEG))
    return jnp.einsum('rhqk,rkhd->rqhd', low(probs), values, precision=HIGH)

def cross_block(block):
    query, keys, values, picks = block
    row_keys = jnp.take(keys, picks, axis=0)
    row_values = jnp.take(values, picks, axis=0)
    scores = low_back(jnp.einsum('rqhd,rkhd->rhqk', query, row_keys, precision=HIGH) * 0.125)
    probs = softmax_rows(scores)
    return jnp.einsum('rhqk,rkhd->rqhd', low(probs), row_values, precision=HIGH)

def reference(text, patches, segment_ids, row_image, self_qkv, self_bias, self_out, cross_query, cross_bias, cross_kv, cross_out, ffn_in, ffn_in_bias, ffn_out, branch_bias, norm_gain, norm_bias, cotangent):
    picks = row_image.reshape(N_DP, ROWS_DEV) - (jnp.arange(N_DP, dtype=jnp.int32) * IMG_DEV)[:, None]
    segments = segment_ids.reshape(N_DP, ROWS_DEV, SEQ)

    def split_heads(block, count):
        return block.reshape(N_DP, count, -1, HEADS, HD)

    def forward(text, patches, self_qkv, self_bias, self_out, cross_query, cross_bias, cross_kv, cross_out, ffn_in, ffn_in_bias, ffn_out, branch_bias, norm_gain, norm_bias):
        query = low(low_back(dense(text, self_qkv[0])) + self_bias[0])
        keys = low(low_back(dense(text, self_qkv[1])))
        values = low(low_back(dense(text, self_qkv[2])) + self_bias[1])
        context = lax.map(jax.checkpoint(self_block), (split_heads(query, ROWS_DEV), split_heads(keys, ROWS_DEV), split_heads(values, ROWS_DEV), segments))
        context = both_ways(context.reshape(TOKENS, D))
        first = text + low_back(dense(context, self_out)) + branch_bias[0]
        middle = layer_norm(first, norm_gain[0], norm_bias[0])
        cross_q = low(low_back(dense(low(middle), cross_query)) + cross_bias[0])
        patch_rows = patches.reshape(IMAGES * PATCH, DV)
        cross_k = low(low_back(dense(patch_rows, cross_kv[0])))
        cross_v = low(low_back(dense(patch_rows, cross_kv[1])) + cross_bias[1])
        cross_context = lax.map(jax.checkpoint(cross_block), (split_heads(cross_q, ROWS_DEV), split_heads(cross_k, IMG_DEV), split_heads(cross_v, IMG_DEV), picks))
        cross_context = both_ways(cross_context.reshape(TOKENS, D))
        second = middle + low_back(dense(cross_context, cross_out)) + branch_bias[1]
        later = layer_norm(second, norm_gain[1], norm_bias[1])
        hidden = low_back(dense(low(later), ffn_in)) + ffn_in_bias
        activated = both_ways(jax.nn.gelu(hidden, approximate=False))
        third = later + low_back(dense(activated, ffn_out)) + branch_bias[2]
        return layer_norm(third, norm_gain[2], norm_bias[2])
    floats = tuple((value.astype(jnp.float32) for value in (text, patches, self_qkv, self_bias, self_out, cross_query, cross_bias, cross_kv, cross_out, ffn_in, ffn_in_bias, ffn_out, branch_bias, norm_gain, norm_bias)))
    joined, pull = jax.vjp(forward, *floats)
    grads = pull(cotangent.astype(jnp.float32))
    return (joined, grads[0], grads[1], grads[2], grads[3], grads[4], grads[5], grads[6], grads[7], grads[8], grads[9], grads[10], grads[11], grads[12], grads[13], grads[14])
```

```python
import math
from functools import partial

import jax
import jax.numpy as jnp
from jax import lax
from jax.experimental import pallas as pl
from jax.experimental.pallas import tpu as pltpu
from jax.sharding import PartitionSpec as P

HD = 64
EPS = 1e-06
BIG_NEG = -1000000000.0
SCALE = 0.125
BF = jnp.bfloat16
F32 = jnp.float32
MIB = 1 << 20


def nn(a, b):
    return lax.dot_general(a, b, (((1,), (0,)), ((), ())), preferred_element_type=F32)


def nt(a, b):
    return lax.dot_general(a, b, (((1,), (1,)), ((), ())), preferred_element_type=F32)


def tn(a, b):
    return lax.dot_general(a, b, (((0,), (0,)), ((), ())), preferred_element_type=F32)


def head_mask(width, head, dtype):
    lane = lax.broadcasted_iota(jnp.int32, (1, width), 1)
    return ((lane >= head * HD) & (lane < (head + 1) * HD)).astype(F32).astype(dtype)


def whole(shape):
    zeros = (0,) * len(shape)
    return pl.BlockSpec(shape, lambda i, *_: zeros, pipeline_mode=pl.Buffered(1))


def tiled(shape):
    zeros = (0,) * (len(shape) - 1)
    return pl.BlockSpec(shape, lambda i, *_: (i,) + zeros)


def call(body, name, grid, ins, outs, scratch, flops, nbytes, scalars=0, vmem=60):
    return pl.pallas_call(
        body,
        name=name,
        out_shape=[jax.ShapeDtypeStruct(s, d) for s, d, _ in outs],
        grid_spec=pltpu.PrefetchScalarGridSpec(
            num_scalar_prefetch=scalars,
            grid=(grid,),
            in_specs=ins,
            out_specs=[spec for _, _, spec in outs],
            scratch_shapes=scratch,
        ),
        compiler_params=pltpu.CompilerParams(
            dimension_semantics=("arbitrary",), vmem_limit_bytes=vmem * MIB
        ),
        cost_estimate=pl.CostEstimate(flops=flops, bytes_accessed=nbytes, transcendentals=0),
    )


def norm(z):
    mu = jnp.mean(z, axis=1, keepdims=True)
    sq = jnp.mean(z * z, axis=1, keepdims=True)
    r = lax.rsqrt(sq - mu * mu + EPS)
    return (z - mu) * r, r


def norm_back(e, n, r, gain):
    a = e * gain
    ma = jnp.mean(a, axis=1, keepdims=True)
    mn = jnp.mean(a * n, axis=1, keepdims=True)
    return r * (a - ma - n * mn)


def colsum(v):
    return jnp.sum(v, axis=0, keepdims=True)


def softmax_cols(s):
    e = jnp.exp(s - jnp.max(s, axis=0, keepdims=True))
    return e * (1.0 / jnp.sum(e, axis=0, keepdims=True))


def softmax_rows(s):
    e = jnp.exp(s - jnp.max(s, axis=1, keepdims=True))
    return e * (1.0 / jnp.sum(e, axis=1, keepdims=True))


def project_patches(patches, cross_kv, bias, padded):
    images, count, visual = patches.shape
    width = cross_kv.shape[2]
    group = 5

    def body(p_ref, w_ref, b_ref, k_ref, v_ref, rows, wcat):
        @pl.when(pl.program_id(0) == 0)
        def _():
            wcat[:, :width] = w_ref[0]
            wcat[:, width:] = w_ref[1]
            rows[...] = jnp.zeros_like(rows)

        for i in range(group):
            rows[padded * i : padded * i + count, :] = p_ref[i]
        out = nn(rows[...], wcat[...])
        k_ref[...] = out[:, :width].astype(BF)
        v_ref[...] = (out[:, width:] + b_ref[1:2, :].astype(F32)).astype(BF)

    tall = (images * padded, width)
    return call(
        body,
        "project_patches",
        images // group,
        [tiled((group, count, visual)), whole(cross_kv.shape), whole(bias.shape)],
        [(tall, BF, tiled((group * padded, width)))] * 2,
        [pltpu.VMEM((group * padded, visual), BF), pltpu.VMEM((visual, 2 * width), BF)],
        2 * images * padded * visual * 2 * width,
        patches.size * 2 + cross_kv.size * 2 + 4 * images * padded * width,
    )(patches, cross_kv, bias)


def self_forward(text, qkv_w, qkv_b, out_w, ids_col, ids_row, tile):
    tokens, width = text.shape
    here = out_w.shape[0]

    def body(x_ref, w_ref, b_ref, o_ref, ic_ref, ir_ref, qkv_ref, c_ref, part_ref, wcat):
        @pl.when(pl.program_id(0) == 0)
        def _():
            for s in range(3):
                wcat[:, s * here : (s + 1) * here] = w_ref[s]

        qkv = (nn(x_ref[...], wcat[...]) + b_ref[...]).astype(BF)
        qkv_ref[...] = qkv
        same = ic_ref[...] == ir_ref[0]
        parts = []
        for p in range(here // 128):
            q = qkv[:, 128 * p : 128 * p + 128]
            k = qkv[:, here + 128 * p : here + 128 * p + 128]
            v = qkv[:, 2 * here + 128 * p : 2 * here + 128 * p + 128]
            total = None
            for a in range(2):
                mask = head_mask(128, a, BF)
                s = jnp.where(same, nt(q * mask, k) * SCALE, BIG_NEG)
                o = nn(softmax_rows(s).astype(BF), v * mask)
                total = o if total is None else total + o
            parts.append(total)
        c = jnp.concatenate(parts, axis=1).astype(BF)
        c_ref[...] = c
        part_ref[...] = nn(c, o_ref[...]).astype(BF)

    return call(
        body,
        "self_forward",
        tokens // tile,
        [
            tiled((tile, width)),
            whole(qkv_w.shape),
            whole(qkv_b.shape),
            whole(out_w.shape),
            tiled((tile, 1)),
            tiled((1, 1, tile)),
        ],
        [
            ((tokens, 3 * here), BF, tiled((tile, 3 * here))),
            ((tokens, here), BF, tiled((tile, here))),
            ((tokens, width), BF, tiled((tile, width))),
        ],
        [pltpu.VMEM((width, 3 * here), BF)],
        2 * tokens * width * 4 * here,
        tokens * (width + 4 * here + width) * 2 + 4 * width * here * 2,
    )(text, qkv_w, qkv_b, out_w, ids_col, ids_row)


def quads(here):
    return [(at, min(256, here - at)) for at in range(0, here, 256)]


def stacked(rows, span):
    return jnp.concatenate(
        [rows * head_mask(span, h, F32) for h in range(span // HD)], axis=0
    ).astype(BF)


def unstacked(tall, span, length):
    total = None
    for h in range(span // HD):
        piece = tall[h * length : (h + 1) * length] * head_mask(span, h, F32)
        total = piece if total is None else total + piece
    return total


def cross_forward(picks, text, mine, other, params, query_w, query_b, keys, values, out_w,
                  tile, length, count, padded):
    tokens, width = text.shape
    here = out_w.shape[0]
    rows = tile // length

    def body(pick, x_ref, m_ref, t_ref, pr_ref, w_ref, b_ref, k_ref, v_ref, o_ref,
             n_ref, r_ref, y_ref, q_ref, c_ref, part_ref, q32, c32):
        h = x_ref[...].astype(F32) + (m_ref[...].astype(F32) + t_ref[...].astype(F32)) + pr_ref[0:1, :]
        n, r = norm(h)
        n_ref[...] = n
        r_ref[...] = r
        y = (n * pr_ref[3:4, :] + pr_ref[6:7, :]).astype(BF)
        y_ref[...] = y
        q = nn(y, w_ref[...]) + b_ref[0:1, :].astype(F32)
        q32[...] = q
        q_ref[...] = q.astype(BF)
        base = pl.program_id(0) * rows
        for j in range(rows):
            at = pl.multiple_of(pick[base + j] * padded, padded)
            for lo, span in quads(here):
                qs = stacked(q32[j * length : (j + 1) * length, lo : lo + span], span)
                s = nt(qs, k_ref[pl.ds(at, padded), lo : lo + span]) * SCALE
                live = lax.broadcasted_iota(jnp.int32, s.shape, 1) < count
                p = softmax_rows(jnp.where(live, s, -1e30))
                o = nn(p.astype(BF), v_ref[pl.ds(at, padded), lo : lo + span])
                c32[j * length : (j + 1) * length, lo : lo + span] = unstacked(o, span, length)
        c = c32[...].astype(BF)
        c_ref[...] = c
        part_ref[...] = nn(c, o_ref[...]).astype(BF)

    full = tiled((tile, width))
    half = tiled((tile, here))
    return call(
        body,
        "cross_forward",
        tokens // tile,
        [full, full, full, whole(params.shape), whole(query_w.shape), whole(query_b.shape),
         whole(keys.shape), whole(values.shape), whole(out_w.shape)],
        [
            ((tokens, width), F32, full),
            ((tokens, 1), F32, tiled((tile, 1))),
            ((tokens, width), BF, full),
            ((tokens, here), BF, half),
            ((tokens, here), BF, half),
            ((tokens, width), BF, full),
        ],
        [pltpu.VMEM((tile, here), F32)] * 2,
        2 * tokens * width * 2 * here + 4 * tokens * padded * here * 4,
        tokens * width * 14 + keys.size * 4,
        scalars=1,
    )(picks, text, mine, other, params, query_w, query_b, keys, values, out_w)


def ffn_forward(normed, mine, other, params, in_w, in_b, out_w, tile):
    tokens, width = normed.shape
    hidden = in_w.shape[1]

    def body(n1_ref, m_ref, t_ref, pr_ref, w_ref, b_ref, o_ref,
             n_ref, r_ref, y_ref, g_ref, d_ref, part_ref):
        h = (n1_ref[...] * pr_ref[3:4, :] + pr_ref[6:7, :]) + (
            m_ref[...].astype(F32) + t_ref[...].astype(F32)
        ) + pr_ref[1:2, :]
        n, r = norm(h)
        n_ref[...] = n
        r_ref[...] = r
        y = (n * pr_ref[4:5, :] + pr_ref[7:8, :]).astype(BF)
        y_ref[...] = y
        u = nn(y, w_ref[...]) + b_ref[...].astype(F32)
        phi = 0.5 * (1.0 + lax.erf(u * math.sqrt(0.5)))
        g = (u * phi).astype(BF)
        g_ref[...] = g
        density = jnp.exp(u * u * -0.5) * (1.0 / math.sqrt(2.0 * math.pi))
        d_ref[...] = (phi + u * density).astype(BF)
        part_ref[...] = nn(g, o_ref[...]).astype(BF)

    full = tiled((tile, width))
    wide = tiled((tile, hidden))
    return call(
        body,
        "ffn_forward",
        tokens // tile,
        [full, full, full, whole(params.shape), whole(in_w.shape), whole(in_b.shape),
         whole(out_w.shape)],
        [
            ((tokens, width), F32, full),
            ((tokens, 1), F32, tiled((tile, 1))),
            ((tokens, width), BF, full),
            ((tokens, hidden), BF, wide),
            ((tokens, hidden), BF, wide),
            ((tokens, width), BF, full),
        ],
        [],
        2 * tokens * width * 2 * hidden,
        tokens * width * 16 + tokens * hidden * 4 + width * hidden * 4,
    )(normed, mine, other, params, in_w, in_b, out_w)


def ffn_backward(side, normed, mine, other, params, cot, slope, in_w, out_w, tile):
    tokens, width = normed.shape
    hidden = in_w.shape[1]
    here = width // 2

    def body(side_ref, n2_ref, m_ref, t_ref, pr_ref, e_ref, d_ref, w_ref, o_ref,
             j_ref, dh_ref, dhb_ref, du_ref, part_ref, sum_ref, sumu_ref, wt, ot):
        @pl.when(pl.program_id(0) == 0)
        def _():
            wt[...] = w_ref[...].T
            ot[...] = o_ref[...].T
            sum_ref[...] = jnp.zeros_like(sum_ref)
            sumu_ref[...] = jnp.zeros_like(sumu_ref)

        h = (n2_ref[...] * pr_ref[4:5, :] + pr_ref[7:8, :]) + (
            m_ref[...].astype(F32) + t_ref[...].astype(F32)
        ) + pr_ref[2:3, :]
        n, r = norm(h)
        joined = n * pr_ref[5:6, :] + pr_ref[8:9, :]
        j_ref[...] = jnp.where(side_ref[0] == 0, joined[:, :here], joined[:, here:])
        e = e_ref[...].astype(F32)
        dh = norm_back(e, n, r, pr_ref[5:6, :])
        dh_ref[...] = dh
        dhb = dh.astype(BF)
        dhb_ref[...] = dhb
        sum_ref[0:1, :] += colsum(e * n)
        sum_ref[1:2, :] += colsum(e)
        sum_ref[2:3, :] += colsum(dh)
        dg = nn(dhb, ot[...]).astype(BF)
        du = dg.astype(F32) * d_ref[...].astype(F32)
        sumu_ref[0:1, :] += colsum(du)
        dub = du.astype(BF)
        du_ref[...] = dub
        part_ref[...] = nn(dub, wt[...]).astype(BF)

    full = tiled((tile, width))
    wide = tiled((tile, hidden))
    return call(
        body,
        "ffn_backward",
        tokens // tile,
        [full, full, full, whole(params.shape), full, wide, whole(in_w.shape), whole(out_w.shape)],
        [
            ((tokens, here), F32, tiled((tile, here))),
            ((tokens, width), F32, full),
            ((tokens, width), BF, full),
            ((tokens, hidden), BF, wide),
            ((tokens, width), BF, full),
            ((8, width), F32, whole((8, width))),
            ((8, hidden), F32, whole((8, hidden))),
        ],
        [pltpu.VMEM((hidden, width), BF), pltpu.VMEM((width, hidden), BF)],
        2 * tokens * width * 2 * hidden,
        tokens * width * 22 + tokens * hidden * 4 + width * hidden * 4,
        scalars=1,
    )(side, normed, mine, other, params, cot, slope, in_w, out_w)


def cross_backward(picks, grad, mine, other, params, normed, spread, query, keys, values,
                   query_w, out_w, tile, length, count, padded):
    tokens, width = grad.shape
    here = out_w.shape[0]
    rows = tile // length
    steps = tokens // tile
    tall = keys.shape[0]

    def body(pick, g_ref, m_ref, t_ref, pr_ref, n_ref, r_ref, q_ref, k_ref, v_ref, w_ref, o_ref,
             dh_ref, dhb_ref, dq_ref, part_ref, kv_ref, sum_ref,
             wt, ot, q32, c32, dq32, dk_acc, dv_acc):
        @pl.when(pl.program_id(0) == 0)
        def _():
            wt[...] = w_ref[...].T
            ot[...] = o_ref[...].T
            sum_ref[...] = jnp.zeros_like(sum_ref)
            dk_acc[...] = jnp.zeros_like(dk_acc)
            dv_acc[...] = jnp.zeros_like(dv_acc)

        e = g_ref[...] + (m_ref[...].astype(F32) + t_ref[...].astype(F32))
        n = n_ref[...]
        dh = norm_back(e, n, r_ref[...], pr_ref[4:5, :])
        dh_ref[...] = dh
        dhb = dh.astype(BF)
        dhb_ref[...] = dhb
        sum_ref[0:1, :] += colsum(e * n)
        sum_ref[1:2, :] += colsum(e)
        sum_ref[2:3, :] += colsum(dh)
        c32[...] = nn(dhb, ot[...])
        q32[...] = q_ref[...].astype(F32)
        base = pl.program_id(0) * rows
        for j in range(rows):
            at = pl.multiple_of(pick[base + j] * padded, padded)
            for lo, span in quads(here):
                here_rows = slice(j * length, (j + 1) * length)
                cols = slice(lo, lo + span)
                qs = stacked(q32[here_rows, cols], span)
                cs = stacked(c32[here_rows, cols], span)
                k = k_ref[pl.ds(at, padded), cols]
                s = nt(k, qs) * SCALE
                live = lax.broadcasted_iota(jnp.int32, s.shape, 0) < count
                p = softmax_cols(jnp.where(live, s, -1e30))
                dp = nt(v_ref[pl.ds(at, padded), cols], cs)
                ds = (p * (dp - jnp.sum(dp * p, axis=0, keepdims=True))).astype(BF)
                dv_acc[pl.ds(at, padded), cols] += nn(p.astype(BF), cs)
                dk_acc[pl.ds(at, padded), cols] += nn(ds, qs) * SCALE
                dq32[here_rows, cols] = unstacked(tn(ds, k), span, length) * SCALE
        dq = dq32[...]
        sum_ref[3:4, :here] += colsum(dq)
        dqb = dq.astype(BF)
        dq_ref[...] = dqb
        part_ref[...] = nn(dqb, wt[...]).astype(BF)

        @pl.when(pl.program_id(0) == steps - 1)
        def _():
            def step(i, total):
                at = pl.ds(pl.multiple_of(i * padded, padded), padded)
                kv_ref[at, :here] = dk_acc[at, :].astype(BF)
                dv = dv_acc[at, :]
                kv_ref[at, here:] = dv.astype(BF)
                return total + colsum(dv)

            total = lax.fori_loop(0, tall // padded, step, jnp.zeros((1, here), F32))
            sum_ref[3:4, here:] = total

    full = tiled((tile, width))
    half = tiled((tile, here))
    return call(
        body,
        "cross_backward",
        steps,
        [full, full, full, whole(params.shape), full, tiled((tile, 1)), half, whole(keys.shape),
         whole(values.shape), whole(query_w.shape), whole(out_w.shape)],
        [
            ((tokens, width), F32, full),
            ((tokens, width), BF, full),
            ((tokens, here), BF, half),
            ((tokens, width), BF, full),
            ((tall, 2 * here), BF, whole((tall, 2 * here))),
            ((8, width), F32, whole((8, width))),
        ],
        [pltpu.VMEM((here, width), BF), pltpu.VMEM((width, here), BF)]
        + [pltpu.VMEM((tile, here), F32)] * 3
        + [pltpu.VMEM((tall, here), F32)] * 2,
        2 * tokens * width * 2 * here + 10 * tokens * padded * here * 4,
        tokens * width * 20 + keys.size * 8,
        scalars=1,
    )(picks, grad, mine, other, params, normed, spread, query, keys, values, query_w, out_w)


def self_backward(side, grad, mine, other, params, normed, spread, qkv, qkv_w, out_w,
                  ids_col, ids_row, tile):
    tokens, width = grad.shape
    here = out_w.shape[0]

    def body(side_ref, g_ref, m_ref, t_ref, pr_ref, n_ref, r_ref, q_ref, w_ref, o_ref,
             ic_ref, ir_ref, dhb_ref, dq_ref, keep_ref, send_ref, sum_ref, wt, ot):
        @pl.when(pl.program_id(0) == 0)
        def _():
            for s in range(3):
                wt[s * here : (s + 1) * here, :] = w_ref[s].T
            ot[...] = o_ref[...].T
            sum_ref[...] = jnp.zeros_like(sum_ref)

        e = g_ref[...] + (m_ref[...].astype(F32) + t_ref[...].astype(F32))
        n = n_ref[...]
        dh = norm_back(e, n, r_ref[...], pr_ref[3:4, :])
        dhb = dh.astype(BF)
        dhb_ref[...] = dhb
        sum_ref[0:1, :] += colsum(e * n)
        sum_ref[1:2, :] += colsum(e)
        sum_ref[2:3, :] += colsum(dh)
        dc = nn(dhb, ot[...]).astype(BF)
        same = ic_ref[...] == ir_ref[0]
        grads = [[], [], []]
        for p in range(here // 128):
            q = q_ref[:, 128 * p : 128 * p + 128]
            k = q_ref[:, here + 128 * p : here + 128 * p + 128]
            v = q_ref[:, 2 * here + 128 * p : 2 * here + 128 * p + 128]
            c = dc[:, 128 * p : 128 * p + 128]
            sums = [None, None, None]
            for a in range(2):
                mask = head_mask(128, a, BF)
                qm = q * mask
                cm = c * mask
                s = jnp.where(same, nt(k, qm) * SCALE, BIG_NEG)
                pt = softmax_cols(s)
                dp = nt(v, cm)
                ds = (pt * (dp - jnp.sum(dp * pt, axis=0, keepdims=True))).astype(BF)
                new = (tn(ds, k * mask), nn(ds, qm), nn(pt.astype(BF), cm))
                sums = [b if a_ is None else a_ + b for a_, b in zip(sums, new)]
            grads[0].append(sums[0] * SCALE)
            grads[1].append(sums[1] * SCALE)
            grads[2].append(sums[2])
        dq, dk, dv = (jnp.concatenate(g, axis=1) for g in grads)
        sum_ref[3:4, :here] += colsum(dq)
        sum_ref[3:4, here:] += colsum(dv)
        dqkv = jnp.concatenate((dq, dk, dv), axis=1).astype(BF)
        dq_ref[...] = dqkv
        part = nn(dqkv, wt[...])
        first = side_ref[0] == 0
        keep_ref[...] = jnp.where(
            first, dh[:, :here] + part[:, :here], dh[:, here:] + part[:, here:]
        )
        send_ref[...] = jnp.where(first, part[:, here:], part[:, :here]).astype(BF)

    full = tiled((tile, width))
    half = tiled((tile, here))
    return call(
        body,
        "self_backward",
        tokens // tile,
        [full, full, full, whole(params.shape), full, tiled((tile, 1)), tiled((tile, 3 * here)),
         whole(qkv_w.shape), whole(out_w.shape), tiled((tile, 1)), tiled((1, 1, tile))],
        [
            ((tokens, width), BF, full),
            ((tokens, 3 * here), BF, tiled((tile, 3 * here))),
            ((tokens, here), F32, half),
            ((tokens, here), BF, half),
            ((8, width), F32, whole((8, width))),
        ],
        [pltpu.VMEM((3 * here, width), BF), pltpu.VMEM((width, here), BF)],
        2 * tokens * width * 4 * here + 10 * tokens * tile * here,
        tokens * width * 16 + 8 * width * here,
        scalars=1,
    )(side, grad, mine, other, params, normed, spread, qkv, qkv_w, out_w, ids_col, ids_row)


def patch_send(side, pair, cross_kv, images, count, padded):
    width = cross_kv.shape[2]
    visual = cross_kv.shape[1]
    half = visual // 2
    group = 5

    def body(side_ref, p_ref, w_ref, s_ref, wt):
        @pl.when(pl.program_id(0) == 0)
        def _():
            wt[:width, :] = w_ref[0].T
            wt[width:, :] = w_ref[1].T

        out = nn(p_ref[...], wt[...])
        for i in range(group):
            s_ref[i] = out[padded * i : padded * i + count].astype(BF)

    return call(
        body,
        "patch_send",
        images // group,
        [
            tiled((group * padded, 2 * width)),
            pl.BlockSpec((2, half, width), lambda i, s: (0, 1 - s[0], 0), pipeline_mode=pl.Buffered(1)),
        ],
        [((images, count, half), BF, tiled((group, count, half)))],
        [pltpu.VMEM((2 * width, half), BF)],
        2 * images * padded * half * 2 * width,
        images * padded * (2 * width + half) * 2,
        scalars=1,
    )(side, pair, cross_kv)[0]


def patch_keep(side, pair, cross_kv, arrived, padded):
    images, count, half = arrived.shape
    width = cross_kv.shape[2]
    group = 5

    def body(side_ref, p_ref, w_ref, a_ref, o_ref, wt):
        @pl.when(pl.program_id(0) == 0)
        def _():
            wt[:width, :] = w_ref[0].T
            wt[width:, :] = w_ref[1].T

        out = nn(p_ref[...], wt[...])
        for i in range(group):
            o_ref[i] = out[padded * i : padded * i + count] + a_ref[i].astype(F32)

    return call(
        body,
        "patch_keep",
        images // group,
        [
            tiled((group * padded, 2 * width)),
            pl.BlockSpec((2, half, width), lambda i, s: (0, s[0], 0), pipeline_mode=pl.Buffered(1)),
            tiled((group, count, half)),
        ],
        [((images, count, half), F32, tiled((group, count, half)))],
        [pltpu.VMEM((2 * width, half), BF)],
        2 * images * padded * half * 2 * width,
        images * padded * (2 * width + half * 3) * 2,
        scalars=1,
    )(side, pair, cross_kv, arrived)[0]


def shards_of(bit, count):
    return [i for i in range(count) if not (i >> bit) & 1]


def split_rows(acc, send_ref, keep_ref, bits_ref, bit, shards, size):
    mine = bits_ref[bit]
    for slot, shard in enumerate(shards_of(bit, shards)):
        kept = pl.multiple_of((shard + (mine << bit)) * size, size)
        sent = pl.multiple_of((shard + ((1 - mine) << bit)) * size, size)
        keep_ref[slot] = acc[pl.ds(kept, size), :].astype(BF)
        send_ref[slot] = acc[pl.ds(sent, size), :].astype(BF)


def split_outside(full, bit, shards, bits):
    size = full.shape[0] // shards
    inner = 1 << bit
    view = full.reshape(shards // (2 * inner), 2, inner, size, full.shape[1])
    return [
        lax.dynamic_index_in_dim(view, at, 1, keepdims=False).reshape(
            shards // 2, size, full.shape[1]
        )
        for at in (1 - bits[bit], bits[bit])
    ]


def grad_weight(bits, groups, shards, name, tile):
    tokens, width = groups[0][1][0][0].shape
    size = width // shards
    inside = size % 16 == 0
    terms, specs, outs, operands = [], [], [], []
    at = 0
    for number, (bit, members) in enumerate(groups):
        first = at
        for left, right, column, columns in members:
            terms.append((at, columns // tile, number, bit))
            operands += [left, right]
            specs += [
                whole(left.shape),
                pl.BlockSpec(
                    (tokens, tile),
                    lambda i, *_, a=at, n=columns // tile, c=column // tile: (
                        0, c + jnp.clip(i - a, 0, n - 1)),
                ),
            ]
            at += columns // tile
        span = at - first
        if inside:
            for _ in range(2):
                outs.append((
                    (shards // 2, size, span * tile), BF,
                    pl.BlockSpec(
                        (shards // 2, size, tile),
                        lambda i, *_, a=first, n=span: (0, 0, jnp.clip(i - a, 0, n - 1)),
                    ),
                ))
        else:
            outs.append((
                (width, span * tile), BF,
                pl.BlockSpec(
                    (width, tile),
                    lambda i, *_, a=first, n=span: (0, jnp.clip(i - a, 0, n - 1)),
                ),
            ))
    total = at

    def body(bits_ref, *refs):
        ins = refs[: len(operands)]
        results = refs[len(operands) : -2]
        lt, acc = refs[-2:]
        step = pl.program_id(0)
        for which, (start, count, number, bit) in enumerate(terms):
            l_ref, r_ref = ins[2 * which : 2 * which + 2]

            if which == 0 or operands[2 * which] is not operands[2 * which - 2]:
                @pl.when(step == start)
                def _(l_ref=l_ref):
                    lt[...] = l_ref[...].T

            @pl.when((step >= start) & (step < start + count))
            def _(r_ref=r_ref, number=number, bit=bit):
                acc[...] = nn(lt[...], r_ref[...])
                if inside:
                    split_rows(acc, results[2 * number], results[2 * number + 1], bits_ref, bit,
                               shards, size)
                else:
                    results[number][...] = acc[...].astype(BF)

    made = call(
        body,
        name,
        total,
        specs,
        outs,
        [pltpu.VMEM((width, tokens), BF), pltpu.VMEM((width, tile), F32)],
        2 * tokens * width * total * tile,
        tokens * (width + total * tile) * 2 + width * total * tile * 2,
        scalars=1,
    )(bits, *operands)
    if inside:
        return [made[2 * i : 2 * i + 2] for i in range(len(groups))]
    return [split_outside(m, g[0], shards, bits) for m, g in zip(made, groups)]


def grad_weight_patches(bits, patches, pair, padded, shards, bit):
    images, count, visual = patches.shape
    size = visual // shards
    wide = pair.shape[1]
    group = 5
    steps = images // group
    inside = size % 16 == 0

    def body(bits_ref, p_ref, g_ref, *refs):
        rows, acc = refs[-2:]
        at = pl.program_id(0)

        @pl.when(at == 0)
        def _():
            rows[...] = jnp.zeros_like(rows)

        for i in range(group):
            rows[padded * i : padded * i + count, :] = p_ref[i]
        new = tn(rows[...], g_ref[...])

        @pl.when(at == 0)
        def _():
            acc[...] = new

        @pl.when(at > 0)
        def _():
            acc[...] += new

        @pl.when(at == steps - 1)
        def _():
            if inside:
                split_rows(acc, refs[0], refs[1], bits_ref, bit, shards, size)
            else:
                refs[0][...] = acc[...].astype(BF)

    half = (shards // 2, size, wide)
    full = (visual, wide)
    made = call(
        body,
        "grad_weight_patches",
        steps,
        [tiled((group, count, visual)), tiled((group * padded, wide))],
        [(half, BF, whole(half))] * 2 if inside else [(full, BF, whole(full))],
        [pltpu.VMEM((group * padded, visual), BF), pltpu.VMEM((visual, wide), F32)],
        2 * images * padded * visual * wide,
        patches.size * 2 + pair.size * 2 + visual * wide * 2,
        scalars=1,
    )(bits, patches, pair)
    return made if inside else split_outside(made[0], bit, shards, bits)


def swap_dp(value, bit, shards):
    return lax.ppermute(value, "dp", [(i, i ^ (1 << bit)) for i in range(shards)])


def add_pair(keep, arrived):
    return keep.astype(F32) + arrived.astype(F32)


def split_next(total, position, mine):
    lead = total.shape[0]
    inner = 1 << position
    view = total.reshape((lead // (2 * inner), 2, inner) + total.shape[1:])
    send = lax.dynamic_index_in_dim(view, 1 - mine, 1, keepdims=False)
    keep = lax.dynamic_index_in_dim(view, mine, 1, keepdims=False)
    shape = (lead // 2,) + total.shape[1:]
    return send.reshape(shape).astype(BF), keep.reshape(shape).astype(BF)


class Sum:
    def __init__(self, first, second, join, bits, shards):
        self.bits, self.shards, self.join = bits, shards, join
        self.keep = [first[1], second[1]]
        self.sent = [swap_dp(first[0], 0, shards), swap_dp(second[0], 1, shards)]
        self.bit = 1

    def step(self, *behind):
        arrived = after(self.sent, behind)
        totals = [add_pair(k, a) for k, a in zip(self.keep, arrived)]
        bit, bits, shards = self.bit, self.bits, self.shards
        if bit == 1:
            pairs = [split_next(t, 0, bits[b]) for t, b in zip(totals, (1, 0))]
            self.keep = [keep for _, keep in pairs]
            self.sent = [swap_dp(send, b, shards) for (send, _), b in zip(pairs, (1, 0))]
        else:
            total = totals[0]
            if bit == 2:
                total = jnp.concatenate(totals, axis=self.join)
            if total.shape[0] == 1:
                return total[0]
            send, keep = split_next(total, 0, bits[bit])
            self.keep, self.sent = [keep], [swap_dp(send, bit, shards)]
        self.bit += 1
        return None

    def finish(self):
        done = None
        while done is None:
            done = self.step()
        return done


def after(values, behind):
    if not behind:
        return values
    return lax.optimization_barrier((values, behind))[0]


def sum_dp(value, shards):
    bit = 0
    while (1 << bit) < shards:
        value = value + swap_dp(value, bit, shards)
        bit += 1
    return value


def swap_mp(value):
    return lax.ppermute(value, "mp", [(0, 1), (1, 0)])


def local(
    shards,
    text,
    patches,
    segment_ids,
    row_image,
    self_qkv,
    self_bias,
    self_out,
    cross_query,
    cross_bias,
    cross_kv,
    cross_out,
    ffn_in,
    ffn_in_bias,
    ffn_out,
    branch_bias,
    norm_gain,
    norm_bias,
    cotangent,
):
    rows, length = segment_ids.shape
    images, count, visual = patches.shape
    tokens, here = text.shape
    padded = -(-count // 32) * 32
    tile = 5 * length
    hidden = ffn_in.shape[1]
    dp_at = lax.axis_index("dp")
    mp_at = lax.axis_index("mp")
    side = mp_at.reshape(1).astype(jnp.int32)
    bit_count = max(2, shards.bit_length() - 1)
    bits = (dp_at >> jnp.arange(bit_count, dtype=jnp.int32)) & 1
    bits = bits.astype(jnp.int32)
    bit_at = [(dp_at >> b) & 1 for b in range(bit_count)]

    def both(own):
        other = swap_mp(own)
        return jnp.where(
            mp_at == 0,
            jnp.concatenate((own, other), axis=1),
            jnp.concatenate((other, own), axis=1),
        )

    text_full = both(text)
    params = both(jnp.concatenate((branch_bias, norm_gain, norm_bias), axis=0)).astype(F32)
    cot_full = both(cotangent)

    picks = (row_image - dp_at * images).astype(jnp.int32)
    ids = segment_ids + 32 * (jnp.arange(rows, dtype=jnp.int32) % (tile // length))[:, None]
    ids_col = ids.reshape(tokens, 1)
    ids_row = ids.reshape(tokens // tile, 1, tile)
    zero = jnp.zeros((here,), F32)
    qkv_b = jnp.concatenate((self_bias[0].astype(F32), zero, self_bias[1].astype(F32)))[None]

    keys, values = project_patches(patches, cross_kv, cross_bias, padded)
    qkv, context, part_one = self_forward(
        text_full, self_qkv, qkv_b, self_out, ids_col, ids_row, tile
    )
    n_one, r_one, y_one, query, cross_ctx, part_two = cross_forward(
        picks, text_full, part_one, swap_mp(part_one), params, cross_query, cross_bias,
        keys, values, cross_out, tile, length, count, padded,
    )
    n_two, r_two, y_two, act, slope, part_three = ffn_forward(
        n_one, part_two, swap_mp(part_two), params, ffn_in, ffn_in_bias[None], ffn_out, tile
    )
    joined, dh_three, dhb_three, du, part_four, sums_three, sums_hidden = ffn_backward(
        side, n_two, part_three, swap_mp(part_three), params, cot_full, slope, ffn_in, ffn_out,
        tile,
    )
    other_four = swap_mp(part_four)
    ffn_groups = grad_weight(
        bits,
        [(0, [(dhb_three, act, 0, hidden)]), (1, [(y_two, du, 0, hidden)])],
        shards, "grad_ffn", 512,
    )
    ffn_sum = Sum(*ffn_groups, 2, bit_at, shards)

    part_four, _ = after([part_four, other_four], tuple(g[0] for g in ffn_groups))
    dh_two, dhb_two, dq_cross, part_five, pair, sums_two = cross_backward(
        picks, dh_three, part_four, other_four, params, n_two, r_two, query, keys, values,
        cross_query, cross_out, tile, length, count, padded,
    )
    other_five = swap_mp(part_five)
    ffn_sum.step(part_five)
    (out_pair,) = grad_weight(
        bits,
        [(0, [(dhb_two, cross_ctx, 0, here), (y_one, dq_cross, 0, here)])],
        shards, "grad_cross", here,
    )
    kv_pair = grad_weight_patches(bits, patches, pair, padded, shards, 1)
    cross_sum = Sum(out_pair, kv_pair, 1, bit_at, shards)
    ffn_sum.step(kv_pair[0])

    part_five, _ = after([part_five, other_five], (kv_pair[0],))
    dhb_one, dqkv, text_keep, text_send, sums_one = self_backward(
        side, dh_two, part_five, other_five, params, n_one, r_one, qkv, self_qkv, self_out,
        ids_col, ids_row, tile,
    )
    text_other = swap_mp(text_send)
    cross_sum.step(dhb_one)
    ffn_sum.step(dhb_one)
    self_groups = grad_weight(
        bits,
        [
            (0, [(text_full, dqkv, 0, 2 * here)]),
            (1, [(text_full, dqkv, 2 * here, here), (dhb_one, context, 0, here)]),
        ],
        shards, "grad_self", here,
    )
    self_sum = Sum(*self_groups, 2, bit_at, shards)
    cross_sum.step(self_groups[0][0])
    sent = patch_send(side, after([pair], (self_groups[0][0],))[0], cross_kv, images, count, padded)
    ffn_shard = ffn_sum.finish()
    arrived = swap_mp(sent)
    self_sum.step(sent)
    patch_grad = patch_keep(side, pair, cross_kv, arrived, padded)
    cross_shard = cross_sum.finish()
    self_shard = self_sum.finish()
    text_grad = text_keep + text_other.astype(F32)

    def mine(block):
        return jnp.where(mp_at == 0, block[:, :here], block[:, here:])

    smalls = jnp.concatenate(
        (
            mine(sums_one[:3]),
            mine(sums_two[:3]),
            mine(sums_three[:3]),
            sums_one[3].reshape(2, here),
            sums_two[3].reshape(2, here),
            sums_hidden[0].reshape(-1, here),
        ),
        axis=0,
    )
    smalls = sum_dp(smalls, shards)
    block = self_shard.shape[0]
    self_grad = jnp.stack([self_shard[:, i * here : (i + 1) * here] for i in range(3)])
    return (
        joined,
        text_grad,
        patch_grad,
        self_grad,
        smalls[9:11],
        self_shard[:, 3 * here :].T,
        cross_shard[:block, here:],
        smalls[11:13],
        jnp.stack((cross_shard[block:, :here], cross_shard[block:, here:])),
        cross_shard[:block, :here].T,
        ffn_shard[:, hidden:],
        smalls[13:].reshape(-1),
        ffn_shard[:, :hidden].T,
        jnp.stack((smalls[2], smalls[5], smalls[8])),
        jnp.stack((smalls[0], smalls[3], smalls[6])),
        jnp.stack((smalls[1], smalls[4], smalls[7])),
    )


def solution(mesh):
    return jax.shard_map(
        partial(local, mesh.shape["dp"]),
        mesh=mesh,
        in_specs=(
            P("dp", "mp"),
            P("dp", None, None),
            P("dp", None),
            P("dp"),
            P(None, None, "mp"),
            P(None, "mp"),
            P("mp", None),
            P(None, "mp"),
            P(None, "mp"),
            P(None, None, "mp"),
            P("mp", None),
            P(None, "mp"),
            P("mp"),
            P("mp", None),
            P(None, "mp"),
            P(None, "mp"),
            P(None, "mp"),
            P("dp", "mp"),
        ),
        out_specs=(
            P("dp", "mp"),
            P("dp", "mp"),
            P("dp", None, "mp"),
            P(None, "dp", "mp"),
            P(None, "mp"),
            P("mp", "dp"),
            P("dp", "mp"),
            P(None, "mp"),
            P(None, "dp", "mp"),
            P("mp", "dp"),
            P("dp", "mp"),
            P("mp"),
            P("mp", "dp"),
            P(None, "mp"),
            P(None, "mp"),
            P(None, "mp"),
        ),
        check_vma=False,
    )
```

```python
import math
from functools import partial

import jax
import jax.numpy as jnp
from jax import lax
from jax.experimental import pallas as pl
from jax.experimental.pallas import tpu as pltpu
from jax.sharding import PartitionSpec as P

HD = 64
EPS = 1e-06
BIG_NEG = -1000000000.0
SCALE = 0.125
BF = jnp.bfloat16
F32 = jnp.float32
MIB = 1 << 20


def nn(a, b):
    return lax.dot_general(a, b, (((1,), (0,)), ((), ())), preferred_element_type=F32)


def nt(a, b):
    return lax.dot_general(a, b, (((1,), (1,)), ((), ())), preferred_element_type=F32)


def tn(a, b):
    return lax.dot_general(a, b, (((0,), (0,)), ((), ())), preferred_element_type=F32)


def head_mask(width, head, dtype):
    lane = lax.broadcasted_iota(jnp.int32, (1, width), 1)
    return ((lane >= head * HD) & (lane < (head + 1) * HD)).astype(F32).astype(dtype)


def whole(shape):
    zeros = (0,) * len(shape)
    return pl.BlockSpec(shape, lambda i, *_: zeros, pipeline_mode=pl.Buffered(1))


def tiled(shape):
    zeros = (0,) * (len(shape) - 1)
    return pl.BlockSpec(shape, lambda i, *_: (i,) + zeros)


def call(body, name, grid, ins, outs, scratch, flops, nbytes, scalars=0, vmem=60,
         collective=None):
    return pl.pallas_call(
        body,
        name=name,
        out_shape=[jax.ShapeDtypeStruct(s, d) for s, d, _ in outs],
        grid_spec=pltpu.PrefetchScalarGridSpec(
            num_scalar_prefetch=scalars,
            grid=(grid,),
            in_specs=ins,
            out_specs=[spec for _, _, spec in outs],
            scratch_shapes=scratch,
        ),
        compiler_params=pltpu.CompilerParams(
            dimension_semantics=("arbitrary",), vmem_limit_bytes=vmem * MIB,
            collective_id=collective, has_side_effects=collective is not None,
        ),
        cost_estimate=pl.CostEstimate(flops=flops, bytes_accessed=nbytes, transcendentals=0),
    )


def norm(z):
    mu = jnp.mean(z, axis=1, keepdims=True)
    sq = jnp.mean(z * z, axis=1, keepdims=True)
    r = lax.rsqrt(sq - mu * mu + EPS)
    return (z - mu) * r, r


def norm_back(e, n, r, gain):
    a = e * gain
    ma = jnp.mean(a, axis=1, keepdims=True)
    mn = jnp.mean(a * n, axis=1, keepdims=True)
    return r * (a - ma - n * mn)


def colsum(v):
    return jnp.sum(v, axis=0, keepdims=True)


def softmax_cols(s):
    e = jnp.exp(s - jnp.max(s, axis=0, keepdims=True))
    return e * (1.0 / jnp.sum(e, axis=0, keepdims=True))


def softmax_rows(s):
    e = jnp.exp(s - jnp.max(s, axis=1, keepdims=True))
    return e * (1.0 / jnp.sum(e, axis=1, keepdims=True))


def project_patches(patches, cross_kv, bias, padded):
    images, count, visual = patches.shape
    width = cross_kv.shape[2]
    group = 5

    def body(p_ref, w_ref, b_ref, k_ref, v_ref, rows, wcat):
        @pl.when(pl.program_id(0) == 0)
        def _():
            wcat[:, :width] = w_ref[0]
            wcat[:, width:] = w_ref[1]
            rows[...] = jnp.zeros_like(rows)

        for i in range(group):
            rows[padded * i : padded * i + count, :] = p_ref[i]
        out = nn(rows[...], wcat[...])
        k_ref[...] = out[:, :width].astype(BF)
        v_ref[...] = (out[:, width:] + b_ref[1:2, :].astype(F32)).astype(BF)

    tall = (images * padded, width)
    return call(
        body,
        "project_patches",
        images // group,
        [tiled((group, count, visual)), whole(cross_kv.shape), whole(bias.shape)],
        [(tall, BF, tiled((group * padded, width)))] * 2,
        [pltpu.VMEM((group * padded, visual), BF), pltpu.VMEM((visual, 2 * width), BF)],
        2 * images * padded * visual * 2 * width,
        patches.size * 2 + cross_kv.size * 2 + 4 * images * padded * width,
    )(patches, cross_kv, bias)


def self_forward(text, qkv_w, qkv_b, out_w, ids_col, ids_row, tile):
    tokens, width = text.shape
    here = out_w.shape[0]

    def body(x_ref, w_ref, b_ref, o_ref, ic_ref, ir_ref, qkv_ref, c_ref, part_ref, wcat):
        @pl.when(pl.program_id(0) == 0)
        def _():
            for s in range(3):
                wcat[:, s * here : (s + 1) * here] = w_ref[s]

        qkv = (nn(x_ref[...], wcat[...]) + b_ref[...]).astype(BF)
        qkv_ref[...] = qkv
        same = ic_ref[...] == ir_ref[0]
        parts = []
        for p in range(here // 128):
            q = qkv[:, 128 * p : 128 * p + 128]
            k = qkv[:, here + 128 * p : here + 128 * p + 128]
            v = qkv[:, 2 * here + 128 * p : 2 * here + 128 * p + 128]
            total = None
            for a in range(2):
                mask = head_mask(128, a, BF)
                s = jnp.where(same, nt(q * mask, k) * SCALE, BIG_NEG)
                o = nn(softmax_rows(s).astype(BF), v * mask)
                total = o if total is None else total + o
            parts.append(total)
        c = jnp.concatenate(parts, axis=1).astype(BF)
        c_ref[...] = c
        part_ref[...] = nn(c, o_ref[...]).astype(BF)

    return call(
        body,
        "self_forward",
        tokens // tile,
        [
            tiled((tile, width)),
            whole(qkv_w.shape),
            whole(qkv_b.shape),
            whole(out_w.shape),
            tiled((tile, 1)),
            tiled((1, 1, tile)),
        ],
        [
            ((tokens, 3 * here), BF, tiled((tile, 3 * here))),
            ((tokens, here), BF, tiled((tile, here))),
            ((tokens, width), BF, tiled((tile, width))),
        ],
        [pltpu.VMEM((width, 3 * here), BF)],
        2 * tokens * width * 4 * here,
        tokens * (width + 4 * here + width) * 2 + 4 * width * here * 2,
    )(text, qkv_w, qkv_b, out_w, ids_col, ids_row)


def quads(here):
    return [(at, min(256, here - at)) for at in range(0, here, 256)]


def stacked(rows, span):
    return jnp.concatenate(
        [rows * head_mask(span, h, F32) for h in range(span // HD)], axis=0
    ).astype(BF)


def unstacked(tall, span, length):
    total = None
    for h in range(span // HD):
        piece = tall[h * length : (h + 1) * length] * head_mask(span, h, F32)
        total = piece if total is None else total + piece
    return total


def cross_forward(picks, text, mine, other, params, query_w, query_b, keys, values, out_w,
                  tile, length, count, padded):
    tokens, width = text.shape
    here = out_w.shape[0]
    rows = tile // length

    def body(pick, x_ref, m_ref, t_ref, pr_ref, w_ref, b_ref, k_ref, v_ref, o_ref,
             n_ref, r_ref, y_ref, q_ref, c_ref, part_ref, q32, c32):
        h = x_ref[...].astype(F32) + (m_ref[...].astype(F32) + t_ref[...].astype(F32)) + pr_ref[0:1, :]
        n, r = norm(h)
        n_ref[...] = n
        r_ref[...] = r
        y = (n * pr_ref[3:4, :] + pr_ref[6:7, :]).astype(BF)
        y_ref[...] = y
        q = nn(y, w_ref[...]) + b_ref[0:1, :].astype(F32)
        q32[...] = q
        q_ref[...] = q.astype(BF)
        base = pl.program_id(0) * rows
        for j in range(rows):
            at = pl.multiple_of(pick[base + j] * padded, padded)
            for lo, span in quads(here):
                qs = stacked(q32[j * length : (j + 1) * length, lo : lo + span], span)
                s = nt(qs, k_ref[pl.ds(at, padded), lo : lo + span]) * SCALE
                live = lax.broadcasted_iota(jnp.int32, s.shape, 1) < count
                p = softmax_rows(jnp.where(live, s, -1e30))
                o = nn(p.astype(BF), v_ref[pl.ds(at, padded), lo : lo + span])
                c32[j * length : (j + 1) * length, lo : lo + span] = unstacked(o, span, length)
        c = c32[...].astype(BF)
        c_ref[...] = c
        part_ref[...] = nn(c, o_ref[...]).astype(BF)

    full = tiled((tile, width))
    half = tiled((tile, here))
    return call(
        body,
        "cross_forward",
        tokens // tile,
        [full, full, full, whole(params.shape), whole(query_w.shape), whole(query_b.shape),
         whole(keys.shape), whole(values.shape), whole(out_w.shape)],
        [
            ((tokens, width), F32, full),
            ((tokens, 1), F32, tiled((tile, 1))),
            ((tokens, width), BF, full),
            ((tokens, here), BF, half),
            ((tokens, here), BF, half),
            ((tokens, width), BF, full),
        ],
        [pltpu.VMEM((tile, here), F32)] * 2,
        2 * tokens * width * 2 * here + 4 * tokens * padded * here * 4,
        tokens * width * 14 + keys.size * 4,
        scalars=1,
    )(picks, text, mine, other, params, query_w, query_b, keys, values, out_w)


def ffn_forward(normed, mine, other, params, in_w, in_b, out_w, tile):
    tokens, width = normed.shape
    hidden = in_w.shape[1]

    def body(n1_ref, m_ref, t_ref, pr_ref, w_ref, b_ref, o_ref,
             n_ref, r_ref, y_ref, g_ref, d_ref, part_ref):
        h = (n1_ref[...] * pr_ref[3:4, :] + pr_ref[6:7, :]) + (
            m_ref[...].astype(F32) + t_ref[...].astype(F32)
        ) + pr_ref[1:2, :]
        n, r = norm(h)
        n_ref[...] = n
        r_ref[...] = r
        y = (n * pr_ref[4:5, :] + pr_ref[7:8, :]).astype(BF)
        y_ref[...] = y
        u = nn(y, w_ref[...]) + b_ref[...].astype(F32)
        phi = 0.5 * (1.0 + lax.erf(u * math.sqrt(0.5)))
        g = (u * phi).astype(BF)
        g_ref[...] = g
        density = jnp.exp(u * u * -0.5) * (1.0 / math.sqrt(2.0 * math.pi))
        d_ref[...] = (phi + u * density).astype(BF)
        part_ref[...] = nn(g, o_ref[...]).astype(BF)

    full = tiled((tile, width))
    wide = tiled((tile, hidden))
    return call(
        body,
        "ffn_forward",
        tokens // tile,
        [full, full, full, whole(params.shape), whole(in_w.shape), whole(in_b.shape),
         whole(out_w.shape)],
        [
            ((tokens, width), F32, full),
            ((tokens, 1), F32, tiled((tile, 1))),
            ((tokens, width), BF, full),
            ((tokens, hidden), BF, wide),
            ((tokens, hidden), BF, wide),
            ((tokens, width), BF, full),
        ],
        [],
        2 * tokens * width * 2 * hidden,
        tokens * width * 16 + tokens * hidden * 4 + width * hidden * 4,
    )(normed, mine, other, params, in_w, in_b, out_w)


def ffn_backward(side, normed, mine, other, params, cot, slope, in_w, out_w, tile):
    tokens, width = normed.shape
    hidden = in_w.shape[1]
    here = width // 2

    def body(side_ref, n2_ref, m_ref, t_ref, pr_ref, e_ref, d_ref, w_ref, o_ref,
             j_ref, dh_ref, dhb_ref, du_ref, part_ref, sum_ref, wt, ot):
        @pl.when(pl.program_id(0) == 0)
        def _():
            wt[...] = w_ref[...].T
            ot[...] = o_ref[...].T
            sum_ref[...] = jnp.zeros_like(sum_ref)

        h = (n2_ref[...] * pr_ref[4:5, :] + pr_ref[7:8, :]) + (
            m_ref[...].astype(F32) + t_ref[...].astype(F32)
        ) + pr_ref[2:3, :]
        n, r = norm(h)
        joined = n * pr_ref[5:6, :] + pr_ref[8:9, :]
        j_ref[...] = jnp.where(side_ref[0] == 0, joined[:, :here], joined[:, here:])
        e = e_ref[...].astype(F32)
        dh = norm_back(e, n, r, pr_ref[5:6, :])
        dh_ref[...] = dh
        dhb = dh.astype(BF)
        dhb_ref[...] = dhb
        sum_ref[0:1, :] += colsum(e * n)
        sum_ref[1:2, :] += colsum(e)
        sum_ref[2:3, :] += colsum(dh)
        dg = nn(dhb, ot[...]).astype(BF)
        du = dg.astype(F32) * d_ref[...].astype(F32)
        total = colsum(du)
        sum_ref[4:5, :] += total[:, :width]
        sum_ref[5:6, :] += total[:, width:]
        dub = du.astype(BF)
        du_ref[...] = dub
        part_ref[...] = nn(dub, wt[...]).astype(BF)

    full = tiled((tile, width))
    wide = tiled((tile, hidden))
    return call(
        body,
        "ffn_backward",
        tokens // tile,
        [full, full, full, whole(params.shape), full, wide, whole(in_w.shape), whole(out_w.shape)],
        [
            ((tokens, here), F32, tiled((tile, here))),
            ((tokens, width), F32, full),
            ((tokens, width), BF, full),
            ((tokens, hidden), BF, wide),
            ((tokens, width), BF, full),
            ((8, width), F32, whole((8, width))),
        ],
        [pltpu.VMEM((hidden, width), BF), pltpu.VMEM((width, hidden), BF)],
        2 * tokens * width * 2 * hidden,
        tokens * width * 22 + tokens * hidden * 4 + width * hidden * 4,
        scalars=1,
    )(side, normed, mine, other, params, cot, slope, in_w, out_w)


def cross_backward(picks, grad, mine, other, params, normed, spread, query, keys, values,
                   query_w, out_w, tile, length, count, padded):
    tokens, width = grad.shape
    here = out_w.shape[0]
    rows = tile // length
    steps = tokens // tile
    tall = keys.shape[0]

    def body(pick, g_ref, m_ref, t_ref, pr_ref, n_ref, r_ref, q_ref, k_ref, v_ref, w_ref, o_ref,
             dh_ref, dhb_ref, dq_ref, part_ref, kv_ref, sum_ref,
             wt, ot, q32, c32, dq32, dk_acc, dv_acc):
        @pl.when(pl.program_id(0) == 0)
        def _():
            wt[...] = w_ref[...].T
            ot[...] = o_ref[...].T
            sum_ref[...] = jnp.zeros_like(sum_ref)
            dk_acc[...] = jnp.zeros_like(dk_acc)
            dv_acc[...] = jnp.zeros_like(dv_acc)

        e = g_ref[...] + (m_ref[...].astype(F32) + t_ref[...].astype(F32))
        n = n_ref[...]
        dh = norm_back(e, n, r_ref[...], pr_ref[4:5, :])
        dh_ref[...] = dh
        dhb = dh.astype(BF)
        dhb_ref[...] = dhb
        sum_ref[0:1, :] += colsum(e * n)
        sum_ref[1:2, :] += colsum(e)
        sum_ref[2:3, :] += colsum(dh)
        c32[...] = nn(dhb, ot[...])
        q32[...] = q_ref[...].astype(F32)
        base = pl.program_id(0) * rows
        for j in range(rows):
            at = pl.multiple_of(pick[base + j] * padded, padded)
            for lo, span in quads(here):
                here_rows = slice(j * length, (j + 1) * length)
                cols = slice(lo, lo + span)
                qs = stacked(q32[here_rows, cols], span)
                cs = stacked(c32[here_rows, cols], span)
                k = k_ref[pl.ds(at, padded), cols]
                s = nt(k, qs) * SCALE
                live = lax.broadcasted_iota(jnp.int32, s.shape, 0) < count
                p = softmax_cols(jnp.where(live, s, -1e30))
                dp = nt(v_ref[pl.ds(at, padded), cols], cs)
                ds = (p * (dp - jnp.sum(dp * p, axis=0, keepdims=True))).astype(BF)
                dv_acc[pl.ds(at, padded), cols] += nn(p.astype(BF), cs)
                dk_acc[pl.ds(at, padded), cols] += nn(ds, qs) * SCALE
                dq32[here_rows, cols] = unstacked(tn(ds, k), span, length) * SCALE
        dq = dq32[...]
        sum_ref[3:4, :here] += colsum(dq)
        dqb = dq.astype(BF)
        dq_ref[...] = dqb
        part_ref[...] = nn(dqb, wt[...]).astype(BF)

        @pl.when(pl.program_id(0) == steps - 1)
        def _():
            def step(i, total):
                at = pl.ds(pl.multiple_of(i * padded, padded), padded)
                kv_ref[at, :here] = dk_acc[at, :].astype(BF)
                dv = dv_acc[at, :]
                kv_ref[at, here:] = dv.astype(BF)
                return total + colsum(dv)

            total = lax.fori_loop(0, tall // padded, step, jnp.zeros((1, here), F32))
            sum_ref[3:4, here:] = total

    full = tiled((tile, width))
    half = tiled((tile, here))
    return call(
        body,
        "cross_backward",
        steps,
        [full, full, full, whole(params.shape), full, tiled((tile, 1)), half, whole(keys.shape),
         whole(values.shape), whole(query_w.shape), whole(out_w.shape)],
        [
            ((tokens, width), F32, full),
            ((tokens, width), BF, full),
            ((tokens, here), BF, half),
            ((tokens, width), BF, full),
            ((tall, 2 * here), BF, whole((tall, 2 * here))),
            ((8, width), F32, whole((8, width))),
        ],
        [pltpu.VMEM((here, width), BF), pltpu.VMEM((width, here), BF)]
        + [pltpu.VMEM((tile, here), F32)] * 3
        + [pltpu.VMEM((tall, here), F32)] * 2,
        2 * tokens * width * 2 * here + 10 * tokens * padded * here * 4,
        tokens * width * 20 + keys.size * 8,
        scalars=1,
    )(picks, grad, mine, other, params, normed, spread, query, keys, values, query_w, out_w)


def self_tile(grad, mine, other, pr_ref, n, r, q_ref, wt, ot, same, sum_ref, keep_ref, send_ref,
              first, here):
    e = grad + (mine.astype(F32) + other.astype(F32))
    dh = norm_back(e, n, r, pr_ref[3:4, :])
    dhb = dh.astype(BF)
    sum_ref[0:1, :] += colsum(e * n)
    sum_ref[1:2, :] += colsum(e)
    sum_ref[2:3, :] += colsum(dh)
    dc = nn(dhb, ot[...]).astype(BF)
    grads = [[], [], []]
    for p in range(here // 128):
        q = q_ref[:, 128 * p : 128 * p + 128]
        k = q_ref[:, here + 128 * p : here + 128 * p + 128]
        v = q_ref[:, 2 * here + 128 * p : 2 * here + 128 * p + 128]
        c = dc[:, 128 * p : 128 * p + 128]
        sums = [None, None, None]
        for a in range(2):
            mask = head_mask(128, a, BF)
            qm = q * mask
            cm = c * mask
            pt = softmax_cols(jnp.where(same, nt(k, qm) * SCALE, BIG_NEG))
            dp = nt(v, cm)
            ds = (pt * (dp - jnp.sum(dp * pt, axis=0, keepdims=True))).astype(BF)
            new = (tn(ds, k * mask), nn(ds, qm), nn(pt.astype(BF), cm))
            sums = [b if a_ is None else a_ + b for a_, b in zip(sums, new)]
        grads[0].append(sums[0] * SCALE)
        grads[1].append(sums[1] * SCALE)
        grads[2].append(sums[2])
    dq, dk, dv = (jnp.concatenate(g, axis=1) for g in grads)
    sum_ref[3:4, :here] += colsum(dq)
    sum_ref[3:4, here:] += colsum(dv)
    dqkv = jnp.concatenate((dq, dk, dv), axis=1).astype(BF)
    part = nn(dqkv, wt[...])
    keep_ref[...] = jnp.where(first, dh[:, :here] + part[:, :here], dh[:, here:] + part[:, here:])
    send_ref[...] = jnp.where(first, part[:, here:], part[:, :here]).astype(BF)
    return dhb, dqkv


def self_backward(side, grad, mine, other, params, normed, spread, qkv, qkv_w, out_w,
                  ids_col, ids_row, tile):
    tokens, width = grad.shape
    here = out_w.shape[0]

    def body(side_ref, g_ref, m_ref, t_ref, pr_ref, n_ref, r_ref, q_ref, w_ref, o_ref,
             ic_ref, ir_ref, dhb_ref, dq_ref, keep_ref, send_ref, sum_ref, wt, ot):
        @pl.when(pl.program_id(0) == 0)
        def _():
            for s in range(3):
                wt[s * here : (s + 1) * here, :] = w_ref[s].T
            ot[...] = o_ref[...].T
            sum_ref[...] = jnp.zeros_like(sum_ref)

        dhb, dqkv = self_tile(
            g_ref[...], m_ref[...], t_ref[...], pr_ref, n_ref[...], r_ref[...], q_ref, wt, ot,
            ic_ref[...] == ir_ref[0], sum_ref, keep_ref, send_ref, side_ref[0] == 0, here,
        )
        dhb_ref[...] = dhb
        dq_ref[...] = dqkv

    full = tiled((tile, width))
    half = tiled((tile, here))
    return call(
        body,
        "self_backward",
        tokens // tile,
        [full, full, full, whole(params.shape), full, tiled((tile, 1)), tiled((tile, 3 * here)),
         whole(qkv_w.shape), whole(out_w.shape), tiled((tile, 1)), tiled((1, 1, tile))],
        [
            ((tokens, width), BF, full),
            ((tokens, 3 * here), BF, tiled((tile, 3 * here))),
            ((tokens, here), F32, half),
            ((tokens, here), BF, half),
            ((8, width), F32, whole((8, width))),
        ],
        [pltpu.VMEM((3 * here, width), BF), pltpu.VMEM((width, here), BF)],
        2 * tokens * width * 4 * here + 10 * tokens * tile * here,
        tokens * width * 16 + 8 * width * here,
        scalars=1,
    )(side, grad, mine, other, params, normed, spread, qkv, qkv_w, out_w, ids_col, ids_row)


def patch_send(side, pair, cross_kv, images, count, padded):
    width = cross_kv.shape[2]
    visual = cross_kv.shape[1]
    half = visual // 2
    group = 5

    def body(side_ref, p_ref, w_ref, s_ref, wt):
        @pl.when(pl.program_id(0) == 0)
        def _():
            wt[:width, :] = w_ref[0].T
            wt[width:, :] = w_ref[1].T

        out = nn(p_ref[...], wt[...])
        for i in range(group):
            s_ref[i] = out[padded * i : padded * i + count].astype(BF)

    return call(
        body,
        "patch_send",
        images // group,
        [
            tiled((group * padded, 2 * width)),
            pl.BlockSpec((2, half, width), lambda i, s: (0, 1 - s[0], 0), pipeline_mode=pl.Buffered(1)),
        ],
        [((images, count, half), BF, tiled((group, count, half)))],
        [pltpu.VMEM((2 * width, half), BF)],
        2 * images * padded * half * 2 * width,
        images * padded * (2 * width + half) * 2,
        scalars=1,
    )(side, pair, cross_kv)[0]


def patch_keep(side, pair, cross_kv, arrived, padded):
    images, count, half = arrived.shape
    width = cross_kv.shape[2]
    group = 5

    def body(side_ref, p_ref, w_ref, a_ref, o_ref, wt):
        @pl.when(pl.program_id(0) == 0)
        def _():
            wt[:width, :] = w_ref[0].T
            wt[width:, :] = w_ref[1].T

        out = nn(p_ref[...], wt[...])
        for i in range(group):
            o_ref[i] = out[padded * i : padded * i + count] + a_ref[i].astype(F32)

    return call(
        body,
        "patch_keep",
        images // group,
        [
            tiled((group * padded, 2 * width)),
            pl.BlockSpec((2, half, width), lambda i, s: (0, s[0], 0), pipeline_mode=pl.Buffered(1)),
            tiled((group, count, half)),
        ],
        [((images, count, half), F32, tiled((group, count, half)))],
        [pltpu.VMEM((2 * width, half), BF)],
        2 * images * padded * half * 2 * width,
        images * padded * (2 * width + half * 3) * 2,
        scalars=1,
    )(side, pair, cross_kv, arrived)[0]


def shards_of(bit, count):
    return [i for i in range(count) if not (i >> bit) & 1]


def split_rows(acc, send_ref, keep_ref, bits_ref, bit, shards, size):
    mine = bits_ref[bit]
    for slot, shard in enumerate(shards_of(bit, shards)):
        kept = pl.multiple_of((shard + (mine << bit)) * size, size)
        sent = pl.multiple_of((shard + ((1 - mine) << bit)) * size, size)
        keep_ref[slot] = acc[pl.ds(kept, size), :].astype(BF)
        send_ref[slot] = acc[pl.ds(sent, size), :].astype(BF)


def split_outside(full, bit, shards, bits):
    size = full.shape[0] // shards
    inner = 1 << bit
    view = full.reshape(shards // (2 * inner), 2, inner, size, full.shape[1])
    return [
        lax.dynamic_index_in_dim(view, at, 1, keepdims=False).reshape(
            shards // 2, size, full.shape[1]
        )
        for at in (1 - bits[bit], bits[bit])
    ]


def grad_weight(bits, groups, shards, name, tile):
    tokens, width = groups[0][1][0][0].shape
    size = width // shards
    inside = size % 16 == 0
    terms, specs, outs, operands = [], [], [], []
    at = 0
    for number, (bit, members) in enumerate(groups):
        first = at
        for left, right, column, columns in members:
            terms.append((at, columns // tile, number, bit))
            operands += [left, right]
            specs += [
                whole(left.shape),
                pl.BlockSpec(
                    (tokens, tile),
                    lambda i, *_, a=at, n=columns // tile, c=column // tile: (
                        0, c + jnp.clip(i - a, 0, n - 1)),
                ),
            ]
            at += columns // tile
        span = at - first
        if inside:
            for _ in range(2):
                outs.append((
                    (shards // 2, size, span * tile), BF,
                    pl.BlockSpec(
                        (shards // 2, size, tile),
                        lambda i, *_, a=first, n=span: (0, 0, jnp.clip(i - a, 0, n - 1)),
                    ),
                ))
        else:
            outs.append((
                (width, span * tile), BF,
                pl.BlockSpec(
                    (width, tile),
                    lambda i, *_, a=first, n=span: (0, jnp.clip(i - a, 0, n - 1)),
                ),
            ))
    total = at

    def body(bits_ref, *refs):
        ins = refs[: len(operands)]
        results = refs[len(operands) : -2]
        lt, acc = refs[-2:]
        step = pl.program_id(0)
        for which, (start, count, number, bit) in enumerate(terms):
            l_ref, r_ref = ins[2 * which : 2 * which + 2]

            if which == 0 or operands[2 * which] is not operands[2 * which - 2]:
                @pl.when(step == start)
                def _(l_ref=l_ref):
                    lt[...] = l_ref[...].T

            @pl.when((step >= start) & (step < start + count))
            def _(r_ref=r_ref, number=number, bit=bit):
                acc[...] = nn(lt[...], r_ref[...])
                if inside:
                    split_rows(acc, results[2 * number], results[2 * number + 1], bits_ref, bit,
                               shards, size)
                else:
                    results[number][...] = acc[...].astype(BF)

    made = call(
        body,
        name,
        total,
        specs,
        outs,
        [pltpu.VMEM((width, tokens), BF), pltpu.VMEM((width, tile), F32)],
        2 * tokens * width * total * tile,
        tokens * (width + total * tile) * 2 + width * total * tile * 2,
        scalars=1,
    )(bits, *operands)
    if inside:
        return [made[2 * i : 2 * i + 2] for i in range(len(groups))]
    return [split_outside(m, g[0], shards, bits) for m, g in zip(made, groups)]


def grad_weight_patches(bits, patches, pair, padded, shards, bit):
    images, count, visual = patches.shape
    size = visual // shards
    wide = pair.shape[1]
    group = 5
    steps = images // group
    inside = size % 16 == 0

    def body(bits_ref, p_ref, g_ref, *refs):
        rows, acc = refs[-2:]
        at = pl.program_id(0)

        @pl.when(at == 0)
        def _():
            rows[...] = jnp.zeros_like(rows)

        for i in range(group):
            rows[padded * i : padded * i + count, :] = p_ref[i]
        new = tn(rows[...], g_ref[...])

        @pl.when(at == 0)
        def _():
            acc[...] = new

        @pl.when(at > 0)
        def _():
            acc[...] += new

        @pl.when(at == steps - 1)
        def _():
            if inside:
                split_rows(acc, refs[0], refs[1], bits_ref, bit, shards, size)
            else:
                refs[0][...] = acc[...].astype(BF)

    half = (shards // 2, size, wide)
    full = (visual, wide)
    made = call(
        body,
        "grad_weight_patches",
        steps,
        [tiled((group, count, visual)), tiled((group * padded, wide))],
        [(half, BF, whole(half))] * 2 if inside else [(full, BF, whole(full))],
        [pltpu.VMEM((group * padded, visual), BF), pltpu.VMEM((visual, wide), F32)],
        2 * images * padded * visual * wide,
        patches.size * 2 + pair.size * 2 + visual * wide * 2,
        scalars=1,
    )(bits, patches, pair)
    return made if inside else split_outside(made[0], bit, shards, bits)


ORDERS = ((0, 1, 2, 3), (1, 2, 0, 3), (2, 0, 1, 3))
LINKS = (None, 0, 1, 2, 3)
MESH = pl.DeviceIdType.MESH


def digit(bit):
    return (lax.axis_index("dp") // (1 << bit)) % 2


def partner(bit):
    dp_at, mp_at = lax.axis_index("dp"), lax.axis_index("mp")
    if bit is None:
        return {"dp": dp_at, "mp": 1 - mp_at}
    return {"dp": dp_at + (1 << bit) - 2 * (1 << bit) * digit(bit), "mp": mp_at}


def remote(source, target, send_sem, got_sem, bit):
    return pltpu.make_async_remote_copy(
        src_ref=source, dst_ref=target, send_sem=send_sem, recv_sem=got_sem,
        device_id=partner(bit), device_id_type=MESH,
    )


def greet():
    barrier = pltpu.get_barrier_semaphore()
    for bit in LINKS:
        pl.semaphore_signal(barrier, inc=1, device_id=partner(bit), device_id_type=MESH)


def met():
    pl.semaphore_wait(pltpu.get_barrier_semaphore(), len(LINKS))


class Stream:
    def __init__(self, rows, columns, order, first=0, last=3):
        self.rows, self.columns, self.order = rows, columns, order
        self.first, self.last = first, last

    def shape(self, t):
        return (8 >> t, self.rows, self.columns)

    def position(self, t):
        return sorted(set(self.order) - set(self.order[:t])).index(self.order[t])

    def scratch(self, made):
        steps = range(self.first, self.last + 1)
        shapes = [pltpu.VMEM(self.shape(t), BF) for t in steps]
        for t in range(made, self.last + 1):
            shapes += [pltpu.VMEM(self.shape(t), BF)] * 2
        return shapes + [pltpu.SemaphoreType.DMA((4,))] * 2

    def bind(self, refs, made, given=None):
        size = len(self.scratch(made))
        mine, rest = refs[:size], refs[size:]
        steps = self.last + 1 - self.first
        self.got = {self.first + i: mine[i] for i in range(steps)}
        self.pairs = {}
        for i, t in enumerate(range(made, self.last + 1)):
            self.pairs[t] = mine[steps + 2 * i : steps + 2 * i + 2]
        if given is not None:
            self.pairs[made - 1] = given
        self.sems = mine[-2:]
        return rest

    def copy(self, t):
        return remote(self.pairs[t][0], self.got[t], self.sems[0].at[t], self.sems[1].at[t],
                      self.order[t])

    def start(self, t):
        self.copy(t).start()

    def total(self, t, shard):
        return self.pairs[t][1][shard].astype(F32) + self.got[t][shard].astype(F32)

    def fold(self, t, target):
        mine = digit(self.order[t + 1])
        low = 1 << self.position(t + 1)
        send, keep = target
        for j in range(8 >> (t + 1)):
            base = (j // low) * 2 * low + j % low
            send[j] = self.total(t, base + (1 - mine) * low).astype(BF)
            keep[j] = self.total(t, base + mine * low).astype(BF)

    def advance(self, t):
        self.copy(t).wait()
        self.fold(t, self.pairs[t + 1])
        self.start(t + 1)

    def finish(self):
        self.copy(3).wait()
        return self.total(3, 0)


def split_shards(full, columns, pair, bit, size):
    mine = digit(bit)
    for slot, shard in enumerate(shards_of(bit, 16)):
        kept = pl.multiple_of((shard + mine * (1 << bit)) * size, 16)
        sent = pl.multiple_of((shard + (1 - mine) * (1 << bit)) * size, 16)
        pair[1][slot] = full[pl.ds(kept, size), columns].astype(BF)
        pair[0][slot] = full[pl.ds(sent, size), columns].astype(BF)


def small_out(shape, dtype=F32):
    return (shape, dtype, whole(shape))


def rows_backward(ffn_kept, ffn_got, cross_terms, grad, part, params, normed, spread, qkv,
                  qkv_w, out_w, ids_col, ids_row, text, context, tile):
    tokens, width = grad.shape
    here = out_w.shape[0]
    tiles = tokens // tile
    size = width // 16
    third = 2 * here // 3
    ffn_cols = ffn_kept[0].shape[2]
    self_cols = 4 * here // 3
    dhb_two, cross_ctx, y_one, dq_cross = cross_terms
    begin = 2
    after_self = begin + tiles
    steps = after_self + 4
    ffn = [Stream(size, ffn_cols, order) for order in ORDERS]
    cross = [Stream(size, third, order, 0, 0) for order in ORDERS]
    self_streams = [Stream(size, self_cols, order) for order in ORDERS]

    def body(*refs):
        ffn_refs, refs = refs[:6], refs[6:]
        (l0_ref, r0_ref, l1_ref, r1_ref, g_ref, part_ref, mine_ref, pr_ref, n_ref, r_ref, q_ref,
         w_ref, o_ref, ic_ref, ir_ref, x_ref, c_ref) = refs[:17]
        keep_ref, send_ref, sum_ref, ffn_ref = refs[17:21]
        self_out, cross_out, rest = refs[21:27], refs[27:33], refs[33:]
        (lt, acc, wt, ot, other, dq_all, dhb_all, full, part_sems) = rest[:9]
        ffn_local, ffn_sems, rest = rest[9:15], rest[15], rest[16:]
        for which, stream in enumerate(ffn):
            rest = stream.bind(rest, 1)
            stream.pairs[0] = (None, ffn_local[2 * which])
            stream.got[0] = ffn_local[2 * which + 1]
        for stream in cross:
            rest = stream.bind(rest, 0)
        at = pl.program_id(0)
        side = lax.axis_index("mp")
        loads = [
            pltpu.make_async_copy(ffn_refs[i], ffn_local[i], ffn_sems.at[i]) for i in range(6)
        ]
        part_copy = remote(part_ref, other, part_sems.at[0], part_sems.at[1], None)

        @pl.when(at == 0)
        def _():
            greet()
            for load in loads:
                load.start()
            lt[...] = l0_ref[...].T
            sum_ref[...] = jnp.zeros_like(sum_ref)
            met()
            part_copy.start()
            acc[...] = nn(lt[...], r0_ref[...])
            full[:, :here] = acc[...].astype(BF)
            for load in loads:
                load.wait()
            for stream in ffn:
                stream.fold(0, stream.pairs[1])
                stream.start(1)

        @pl.when(at == 1)
        def _():
            lt[...] = l1_ref[...].T
            acc[...] = nn(lt[...], r1_ref[...])
            full[:, here : 2 * here] = acc[...].astype(BF)
            for which, stream in enumerate(cross):
                split_shards(full, slice(which * third, (which + 1) * third), stream.pairs[0],
                             stream.order[0], size)
            for s in range(3):
                wt[s * here : (s + 1) * here, :] = w_ref[s].T
            ot[...] = o_ref[...].T
            part_copy.wait()

        @pl.when(at == begin + 2)
        def _():
            for stream in ffn:
                stream.advance(1)

        @pl.when(at == begin + 4)
        def _():
            for stream in ffn:
                stream.advance(2)
            for stream in cross:
                stream.start(0)

        @pl.when((at >= begin) & (at < after_self))
        def _():
            i = at - begin
            dhb, dqkv = self_tile(
                g_ref[...], mine_ref[...], other[i], pr_ref, n_ref[...], r_ref[...], q_ref,
                wt, ot, ic_ref[...] == ir_ref[0], sum_ref, keep_ref, send_ref, side == 0, here,
            )
            for j in range(tiles):
                @pl.when(i == j)
                def _(j=j):
                    dq_all[j * tile : (j + 1) * tile, :] = dqkv
                    dhb_all[j * tile : (j + 1) * tile, :] = dhb

        for j in range(4):
            @pl.when(at == after_self + j)
            def _(j=j):
                if j == 0:
                    lt[...] = x_ref[...].T
                if j == 3:
                    lt[...] = dhb_all[...].T
                right = c_ref[...] if j == 3 else dq_all[:, j * here : (j + 1) * here]
                acc[...] = nn(lt[...], right)
                full[:, j * here : (j + 1) * here] = acc[...].astype(BF)
                if j == 3:
                    for which, stream in enumerate(self_streams):
                        split_shards(
                            full, slice(which * self_cols, (which + 1) * self_cols),
                            self_out[2 * which : 2 * which + 2], stream.order[0], size,
                        )
                    for which, stream in enumerate(cross):
                        stream.copy(0).wait()
                        stream.fold(0, cross_out[2 * which : 2 * which + 2])
                    for which, stream in enumerate(ffn):
                        ffn_ref[:, which * ffn_cols : (which + 1) * ffn_cols] = stream.finish()

    anywhere = pl.BlockSpec(memory_space=pl.ANY)

    def rows(columns):
        return pl.BlockSpec((tile, columns), lambda i: (jnp.clip(i - begin, 0, tiles - 1), 0))

    ids_spec = pl.BlockSpec((1, 1, tile), lambda i: (jnp.clip(i - begin, 0, tiles - 1), 0, 0))
    ffn_arrays = [a for pair in zip(ffn_kept, ffn_got) for a in pair]
    operands = ffn_arrays + [
        dhb_two, cross_ctx, y_one, dq_cross, grad, part.reshape(tiles, tile, width), part, params,
        normed, spread, qkv, qkv_w, out_w, ids_col, ids_row, text, context,
    ]
    ins = [anywhere] * 6 + [
        whole(dhb_two.shape), whole(cross_ctx.shape), whole(y_one.shape), whole(dq_cross.shape),
        rows(width), anywhere, rows(width), whole(params.shape), rows(width), rows(1),
        rows(3 * here), whole(qkv_w.shape), whole(out_w.shape), rows(1), ids_spec,
        whole(text.shape), whole(context.shape),
    ]
    outs = [
        ((tokens, here), F32, rows(here)),
        ((tokens, here), BF, rows(here)),
        small_out((8, width)),
        small_out((size, 3 * ffn_cols)),
    ]
    outs += [small_out(self_streams[0].shape(0), BF)] * 6
    outs += [small_out(cross[0].shape(1), BF)] * 6
    scratch = [
        pltpu.VMEM((width, tokens), BF),
        pltpu.VMEM((width, here), F32),
        pltpu.VMEM((3 * here, width), BF),
        pltpu.VMEM((width, here), BF),
        pltpu.VMEM((tiles, tile, width), BF),
        pltpu.VMEM((tokens, 3 * here), BF),
        pltpu.VMEM((tokens, width), BF),
        pltpu.VMEM((width, 4 * here), BF),
        pltpu.SemaphoreType.DMA((2,)),
    ]
    scratch += [pltpu.VMEM(ffn[0].shape(0), BF)] * 6 + [pltpu.SemaphoreType.DMA((6,))]
    for stream in ffn:
        stream.first = 1
        scratch += stream.scratch(1)
    for stream in cross:
        scratch += stream.scratch(0)
    made = call(
        body, "rows_backward", steps, ins, outs, scratch,
        2 * tokens * width * 10 * here, tokens * width * 30, collective=1,
    )(*operands)
    return made[:4], [made[4 + 2 * i : 6 + 2 * i] for i in range(3)], [
        made[10 + 2 * i : 12 + 2 * i] for i in range(3)]


def patch_backward(patches, pair, cross_kv, cross_pairs, self_pairs, sums, padded):
    images, count, visual = patches.shape
    width = cross_kv.shape[2]
    half = visual // 2
    wide = 2 * width
    size = visual // 16
    group = 5
    steps = images // group
    small = cross_pairs[0][0].shape[1]
    third = wide // 3
    self_cols = self_pairs[0][0].shape[2]
    cross = [Stream(small, third, order, 1) for order in ORDERS]
    selves = [Stream(small, self_cols, order) for order in ORDERS]
    kvs = [Stream(size, third, order) for order in ORDERS]
    given = list(cross_pairs) + list(self_pairs)

    def body(p_ref, g_ref, w_ref, s1_ref, s2_ref, s3_ref, *refs):
        firsts = [refs[2 * i : 2 * i + 2] for i in range(6)]
        out_ref, cross_ref, self_ref, kv_ref, sum_ref = refs[12:17]
        rows, acc, wt, send, got, send_sem, got_sem, sum_now, sum_got, sum_sems = refs[17:27]
        rest = refs[27:]
        for which, stream in enumerate(cross):
            rest = stream.bind(rest, 2, firsts[which])
        for which, stream in enumerate(selves):
            rest = stream.bind(rest, 1, firsts[3 + which])
        for stream in kvs:
            rest = stream.bind(rest, 0)
        side = lax.axis_index("mp")
        at = pl.program_id(0)

        def patch_copy(tile):
            return remote(send.at[tile], got.at[tile], send_sem.at[tile], got_sem.at[tile], None)

        def sum_copy(bit):
            return remote(sum_now.at[bit], sum_got.at[bit], sum_sems.at[bit],
                          sum_sems.at[4 + bit], bit)

        @pl.when(at == 0)
        def _():
            greet()
            rows[...] = jnp.zeros_like(rows)
            sum_now[0, :8] = s3_ref[...]
            sum_now[0, 8:12] = s1_ref[0:4]
            sum_now[0, 12:16] = s2_ref[0:4]
            met()
            for stream in selves:
                stream.start(0)
            sum_copy(0).start()
            for stream in cross:
                stream.start(1)
            wt[:width, :] = w_ref[0].T
            wt[width:, :] = w_ref[1].T

        for bit in range(4):
            @pl.when(at == bit + 1)
            def _(bit=bit):
                sum_copy(bit).wait()
                total = sum_now[bit] + sum_got[bit]
                if bit == 3:
                    sum_ref[...] = total
                else:
                    sum_now[bit + 1] = total
                    sum_copy(bit + 1).start()

        def plan(step, streams, t):
            @pl.when(at == step)
            def _():
                for stream in streams:
                    stream.advance(t)

        plan(3, cross, 1)
        plan(5, cross, 2)
        plan(5, selves, 0)
        plan(9, selves, 1)
        plan(11, selves, 2)
        plan(12, kvs, 0)
        plan(13, kvs, 1)
        plan(14, kvs, 2)

        @pl.when(at < steps)
        def _():
            for i in range(group):
                rows[padded * i : padded * i + count, :] = p_ref[i]
            new = tn(rows[...], g_ref[...])

            @pl.when(at == 0)
            def _():
                acc[...] = new

            @pl.when(at > 0)
            def _():
                acc[...] += new

            @pl.when(at == steps - 1)
            def _():
                for which, stream in enumerate(kvs):
                    split_shards(acc, slice(which * third, (which + 1) * third), stream.pairs[0],
                                 stream.order[0], size)
                    stream.start(0)

        def product(half_at):
            lanes = pl.ds(pl.multiple_of(half_at * half, 128), half)
            return nn(g_ref[...], wt[:, lanes])

        @pl.when((at >= steps) & (at < 2 * steps))
        def _():
            tile = at - steps
            out = product(1 - side)
            for i in range(group):
                send[tile, i] = out[padded * i : padded * i + count].astype(BF)
            patch_copy(tile).start()

        @pl.when(at >= 2 * steps)
        def _():
            tile = at - 2 * steps
            out = product(side)
            patch_copy(tile).wait()
            for i in range(group):
                mine = out[padded * i : padded * i + count]
                out_ref[i] = (mine + got[tile, i].astype(F32)).astype(BF)

        @pl.when(at == 3 * steps - 1)
        def _():
            for target, streams in ((cross_ref, cross), (self_ref, selves), (kv_ref, kvs)):
                for which, stream in enumerate(streams):
                    lo = which * stream.columns
                    target[:, lo : lo + stream.columns] = stream.finish()

    anywhere = pl.BlockSpec(memory_space=pl.ANY)
    ins = [
        pl.BlockSpec((group, count, visual), lambda i: (jnp.minimum(i, steps - 1), 0, 0)),
        pl.BlockSpec((group * padded, wide), lambda i: (i % steps, 0)),
        whole(cross_kv.shape),
    ] + [whole(s.shape) for s in sums]
    operands = [patches, pair, cross_kv, *sums]
    for sent, kept in given:
        ins += [anywhere, whole(kept.shape)]
        operands += [sent, kept]
    scratch = [
        pltpu.VMEM((group * padded, visual), BF),
        pltpu.VMEM((visual, wide), F32),
        pltpu.VMEM((wide, visual), BF),
        pltpu.VMEM((steps, group, count, half), BF),
        pltpu.VMEM((steps, group, count, half), BF),
        pltpu.SemaphoreType.DMA((steps,)),
        pltpu.SemaphoreType.DMA((steps,)),
        pltpu.VMEM((4, 16, wide), F32),
        pltpu.VMEM((4, 16, wide), F32),
        pltpu.SemaphoreType.DMA((8,)),
    ]
    for stream in cross:
        scratch += stream.scratch(2)
    for stream in selves:
        scratch += stream.scratch(1)
    for stream in kvs:
        scratch += stream.scratch(0)
    return call(
        body,
        "patch_backward",
        3 * steps,
        ins,
        [
            ((images, count, half), BF,
             pl.BlockSpec((group, count, half), lambda i: (jnp.maximum(i - 2 * steps, 0), 0, 0))),
            small_out((small, wide)),
            small_out((small, 3 * self_cols)),
            small_out((size, wide)),
            small_out((16, wide)),
        ],
        scratch,
        2 * images * padded * visual * wide * 2,
        patches.size * 2 + pair.size * 6 + images * count * half * 4,
        collective=2,
    )(*operands)


def finish(side, patch, text_keep, text_other, ffn, cross, self_sum, kv, sums):
    images, count, half = patch.shape
    tokens, here = text_keep.shape
    block = ffn.shape[0]
    hidden = ffn.shape[1] // 2
    steps = 5
    tile = tokens // steps
    group = images // steps

    def body(side_ref, p_ref, k_ref, t_ref, f_ref, c_ref, s_ref, v_ref, m_ref,
             patch_out, text_out, qkv_out, so_out, cq_out, kv_out, co_out, fi_out, fo_out,
             sb_out, cb_out, fb_out, br_out, ga_out, sh_out):
        patch_out[...] = p_ref[...].astype(F32)
        text_out[...] = k_ref[...] + t_ref[...].astype(F32)

        @pl.when(pl.program_id(0) == 0)
        def _():
            for i in range(3):
                qkv_out[i] = s_ref[:, i * here : (i + 1) * here]
            so_out[...] = s_ref[:, 3 * here :]
            cq_out[...] = c_ref[:, here:]
            co_out[...] = c_ref[:, :here]
            fi_out[...] = f_ref[:, hidden:]
            fo_out[...] = f_ref[:, :hidden]
            for i in range(2):
                kv_out[i] = v_ref[:, i * here : (i + 1) * here]
                sb_out[i : i + 1, :] = m_ref[11:12, i * here : (i + 1) * here]
                cb_out[i : i + 1, :] = m_ref[15:16, i * here : (i + 1) * here]
                fb_out[:, 2 * i * here : 2 * (i + 1) * here] = m_ref[4 + i : 5 + i, :]
            first = side_ref[0] == 0
            for out, at in ((ga_out, 0), (sh_out, 1), (br_out, 2)):
                for i, row in enumerate((8 + at, 12 + at, at)):
                    out[i : i + 1, :] = jnp.where(
                        first, m_ref[row : row + 1, :here], m_ref[row : row + 1, here:]
                    )

    rows = tiled((tile, here))
    blocks = tiled((group, count, half))
    return call(
        body,
        "finish",
        steps,
        [blocks, rows, rows] + [whole(a.shape) for a in (ffn, cross, self_sum, kv, sums)],
        [
            (patch.shape, F32, blocks),
            (text_keep.shape, F32, rows),
            small_out((3, block, here)),
            small_out((block, here)),
            small_out((block, here)),
            small_out((2, kv.shape[0], here)),
            small_out((block, here)),
            small_out((block, hidden)),
            small_out((block, hidden)),
            small_out((2, here)),
            small_out((2, here)),
            small_out((1, hidden)),
            small_out((3, here)),
            small_out((3, here)),
            small_out((3, here)),
        ],
        [],
        images * count * half,
        images * count * half * 6,
        scalars=1,
    )(side, patch, text_keep, text_other, ffn, cross, self_sum, kv, sums)


def swap_dp(value, bit, shards):
    return lax.ppermute(value, "dp", [(i, i ^ (1 << bit)) for i in range(shards)])


def add_pair(keep, arrived):
    return keep.astype(F32) + arrived.astype(F32)


def split_next(total, position, mine):
    lead = total.shape[0]
    inner = 1 << position
    view = total.reshape((lead // (2 * inner), 2, inner) + total.shape[1:])
    send = lax.dynamic_index_in_dim(view, 1 - mine, 1, keepdims=False)
    keep = lax.dynamic_index_in_dim(view, mine, 1, keepdims=False)
    shape = (lead // 2,) + total.shape[1:]
    return send.reshape(shape).astype(BF), keep.reshape(shape).astype(BF)


class Sum:
    def __init__(self, first, second, join, bits, shards):
        self.bits, self.shards, self.join = bits, shards, join
        self.keep = [first[1], second[1]]
        self.sent = [swap_dp(first[0], 0, shards), swap_dp(second[0], 1, shards)]
        self.bit = 1

    def step(self, *behind):
        arrived = after(self.sent, behind)
        totals = [add_pair(k, a) for k, a in zip(self.keep, arrived)]
        bit, bits, shards = self.bit, self.bits, self.shards
        if bit == 1:
            pairs = [split_next(t, 0, bits[b]) for t, b in zip(totals, (1, 0))]
            self.keep = [keep for _, keep in pairs]
            self.sent = [swap_dp(send, b, shards) for (send, _), b in zip(pairs, (1, 0))]
        else:
            total = totals[0]
            if bit == 2:
                total = jnp.concatenate(totals, axis=self.join)
            if total.shape[0] == 1:
                return total[0]
            send, keep = split_next(total, 0, bits[bit])
            self.keep, self.sent = [keep], [swap_dp(send, bit, shards)]
        self.bit += 1
        return None

    def finish(self):
        done = None
        while done is None:
            done = self.step()
        return done


def after(values, behind):
    if not behind:
        return values
    return lax.optimization_barrier((values, behind))[0]


def sum_dp(value, shards):
    bit = 0
    while (1 << bit) < shards:
        value = value + swap_dp(value, bit, shards)
        bit += 1
    return value


def swap_mp(value):
    return lax.ppermute(value, "mp", [(0, 1), (1, 0)])


def local(
    shards,
    text,
    patches,
    segment_ids,
    row_image,
    self_qkv,
    self_bias,
    self_out,
    cross_query,
    cross_bias,
    cross_kv,
    cross_out,
    ffn_in,
    ffn_in_bias,
    ffn_out,
    branch_bias,
    norm_gain,
    norm_bias,
    cotangent,
):
    rows, length = segment_ids.shape
    images, count, visual = patches.shape
    tokens, here = text.shape
    padded = -(-count // 32) * 32
    tile = 5 * length
    hidden = ffn_in.shape[1]
    dp_at = lax.axis_index("dp")
    mp_at = lax.axis_index("mp")
    side = mp_at.reshape(1).astype(jnp.int32)
    bit_count = max(2, shards.bit_length() - 1)
    bits = (dp_at >> jnp.arange(bit_count, dtype=jnp.int32)) & 1
    bits = bits.astype(jnp.int32)
    bit_at = [(dp_at >> b) & 1 for b in range(bit_count)]

    def both(own):
        other = swap_mp(own)
        return jnp.where(
            mp_at == 0,
            jnp.concatenate((own, other), axis=1),
            jnp.concatenate((other, own), axis=1),
        )

    text_full = both(text)
    params = both(jnp.concatenate((branch_bias, norm_gain, norm_bias), axis=0)).astype(F32)
    cot_full = both(cotangent)

    picks = (row_image - dp_at * images).astype(jnp.int32)
    ids = segment_ids + 32 * (jnp.arange(rows, dtype=jnp.int32) % (tile // length))[:, None]
    ids_col = ids.reshape(tokens, 1)
    ids_row = ids.reshape(tokens // tile, 1, tile)
    zero = jnp.zeros((here,), F32)
    qkv_b = jnp.concatenate((self_bias[0].astype(F32), zero, self_bias[1].astype(F32)))[None]

    keys, values = project_patches(patches, cross_kv, cross_bias, padded)
    qkv, context, part_one = self_forward(
        text_full, self_qkv, qkv_b, self_out, ids_col, ids_row, tile
    )
    n_one, r_one, y_one, query, cross_ctx, part_two = cross_forward(
        picks, text_full, part_one, swap_mp(part_one), params, cross_query, cross_bias,
        keys, values, cross_out, tile, length, count, padded,
    )
    n_two, r_two, y_two, act, slope, part_three = ffn_forward(
        n_one, part_two, swap_mp(part_two), params, ffn_in, ffn_in_bias[None], ffn_out, tile
    )
    joined, dh_three, dhb_three, du, part_four, sums_three = ffn_backward(
        side, n_two, part_three, swap_mp(part_three), params, cot_full, slope, ffn_in, ffn_out,
        tile,
    )
    other_four = swap_mp(part_four)
    quick = shards == 16
    if quick:
        most, few = 2 * hidden // 3, hidden // 3
        ffn_groups = grad_weight(
            bits,
            [
                (0, [(dhb_three, act, 0, most)]),
                (1, [(dhb_three, act, most, few), (y_two, du, 0, few)]),
                (2, [(y_two, du, few, most)]),
            ],
            shards, "grad_ffn", few,
        )
        ffn_got = [swap_dp(g[0], b, shards) for b, g in enumerate(ffn_groups)]
        part_four, _ = after([part_four, other_four], tuple(g[0] for g in ffn_groups))
        dh_two, dhb_two, dq_cross, part_five, pair, sums_two = cross_backward(
            picks, dh_three, part_four, other_four, params, n_two, r_two, query, keys, values,
            cross_query, cross_out, tile, length, count, padded,
        )
        ffn_got = after(ffn_got, (part_five,))
        (text_keep, text_send, sums_one, ffn_shard), self_pairs, cross_pairs = rows_backward(
            [g[1] for g in ffn_groups], ffn_got, (dhb_two, cross_ctx, y_one, dq_cross), dh_two,
            part_five, params, n_one, r_one, qkv, self_qkv, self_out, ids_col, ids_row,
            text_full, context, tile,
        )
        text_other = swap_mp(text_send)
        patch, cross_shard, self_shard, kv_shard, sums = patch_backward(
            patches, pair, cross_kv, cross_pairs, self_pairs, (sums_one, sums_two, sums_three),
            padded,
        )
        (patch_grad, text_grad, g_qkv, g_so, g_cq, g_kv, g_co, g_fi, g_fo, g_sb, g_cb, g_fb, g_br,
         g_ga, g_sh) = finish(
            side, patch, text_keep, text_other, ffn_shard, cross_shard, self_shard, kv_shard, sums
        )
        return (joined, text_grad, patch_grad, g_qkv, g_sb, g_so.T, g_cq, g_cb, g_kv, g_co.T, g_fi,
                g_fb.reshape(-1), g_fo.T, g_br, g_ga, g_sh)
    ffn_groups = grad_weight(
        bits,
        [(0, [(dhb_three, act, 0, hidden)]), (1, [(y_two, du, 0, hidden)])],
        shards, "grad_ffn", 512,
    )
    ffn_sum = Sum(*ffn_groups, 2, bit_at, shards)

    part_four, _ = after([part_four, other_four], tuple(g[0] for g in ffn_groups))
    dh_two, dhb_two, dq_cross, part_five, pair, sums_two = cross_backward(
        picks, dh_three, part_four, other_four, params, n_two, r_two, query, keys, values,
        cross_query, cross_out, tile, length, count, padded,
    )
    other_five = swap_mp(part_five)
    ffn_sum.step(part_five)
    (out_pair,) = grad_weight(
        bits,
        [(0, [(dhb_two, cross_ctx, 0, here), (y_one, dq_cross, 0, here)])],
        shards, "grad_cross", here,
    )
    kv_pair = grad_weight_patches(bits, patches, pair, padded, shards, 1)
    cross_sum = Sum(out_pair, kv_pair, 1, bit_at, shards)
    ffn_sum.step(kv_pair[0])

    part_five, _ = after([part_five, other_five], (kv_pair[0],))
    dhb_one, dqkv, text_keep, text_send, sums_one = self_backward(
        side, dh_two, part_five, other_five, params, n_one, r_one, qkv, self_qkv, self_out,
        ids_col, ids_row, tile,
    )
    text_other = swap_mp(text_send)
    cross_sum.step(dhb_one)
    ffn_sum.step(dhb_one)
    self_groups = grad_weight(
        bits,
        [
            (0, [(text_full, dqkv, 0, 2 * here)]),
            (1, [(text_full, dqkv, 2 * here, here), (dhb_one, context, 0, here)]),
        ],
        shards, "grad_self", here,
    )
    self_sum = Sum(*self_groups, 2, bit_at, shards)
    cross_sum.step(self_groups[0][0])
    sent = patch_send(side, after([pair], (self_groups[0][0],))[0], cross_kv, images, count, padded)
    ffn_shard = ffn_sum.finish()
    arrived = swap_mp(sent)
    self_sum.step(sent)
    patch_grad = patch_keep(side, pair, cross_kv, arrived, padded)
    cross_shard = cross_sum.finish()
    self_shard = self_sum.finish()
    text_grad = text_keep + text_other.astype(F32)

    def mine(block):
        return jnp.where(mp_at == 0, block[:, :here], block[:, here:])

    smalls = jnp.concatenate(
        (
            mine(sums_one[:3]),
            mine(sums_two[:3]),
            mine(sums_three[:3]),
            sums_one[3].reshape(2, here),
            sums_two[3].reshape(2, here),
            sums_three[4:6].reshape(-1, here),
        ),
        axis=0,
    )
    smalls = sum_dp(smalls, shards)
    block = self_shard.shape[0]
    self_grad = jnp.stack([self_shard[:, i * here : (i + 1) * here] for i in range(3)])
    return (
        joined,
        text_grad,
        patch_grad,
        self_grad,
        smalls[9:11],
        self_shard[:, 3 * here :].T,
        cross_shard[:block, here:],
        smalls[11:13],
        jnp.stack((cross_shard[block:, :here], cross_shard[block:, here:])),
        cross_shard[:block, :here].T,
        ffn_shard[:, hidden:],
        smalls[13:].reshape(-1),
        ffn_shard[:, :hidden].T,
        jnp.stack((smalls[2], smalls[5], smalls[8])),
        jnp.stack((smalls[0], smalls[3], smalls[6])),
        jnp.stack((smalls[1], smalls[4], smalls[7])),
    )


def solution(mesh):
    return jax.shard_map(
        partial(local, mesh.shape["dp"]),
        mesh=mesh,
        in_specs=(
            P("dp", "mp"),
            P("dp", None, None),
            P("dp", None),
            P("dp"),
            P(None, None, "mp"),
            P(None, "mp"),
            P("mp", None),
            P(None, "mp"),
            P(None, "mp"),
            P(None, None, "mp"),
            P("mp", None),
            P(None, "mp"),
            P("mp"),
            P("mp", None),
            P(None, "mp"),
            P(None, "mp"),
            P(None, "mp"),
            P("dp", "mp"),
        ),
        out_specs=(
            P("dp", "mp"),
            P("dp", "mp"),
            P("dp", None, "mp"),
            P(None, "dp", "mp"),
            P(None, "mp"),
            P("mp", "dp"),
            P("dp", "mp"),
            P(None, "mp"),
            P(None, "dp", "mp"),
            P("mp", "dp"),
            P("dp", "mp"),
            P("mp"),
            P("mp", "dp"),
            P(None, "mp"),
            P(None, "mp"),
            P(None, "mp"),
        ),
        check_vma=False,
    )
```

```python
import math
from functools import partial

import jax
import jax.numpy as jnp
from jax import lax
from jax.experimental import pallas as pl
from jax.experimental.pallas import tpu as pltpu
from jax.sharding import PartitionSpec as P

HD = 64
EPS = 1e-06
BIG_NEG = -1000000000.0
SCALE = 0.125
BF = jnp.bfloat16
F32 = jnp.float32
MIB = 1 << 20


def nn(a, b):
    return lax.dot_general(a, b, (((1,), (0,)), ((), ())), preferred_element_type=F32)


def nt(a, b):
    return lax.dot_general(a, b, (((1,), (1,)), ((), ())), preferred_element_type=F32)


def tn(a, b):
    return lax.dot_general(a, b, (((0,), (0,)), ((), ())), preferred_element_type=F32)


def head_mask(width, head, dtype):
    lane = lax.broadcasted_iota(jnp.int32, (1, width), 1)
    return ((lane >= head * HD) & (lane < (head + 1) * HD)).astype(F32).astype(dtype)


def whole(shape):
    zeros = (0,) * len(shape)
    return pl.BlockSpec(shape, lambda i, *_: zeros, pipeline_mode=pl.Buffered(1))


def tiled(shape):
    zeros = (0,) * (len(shape) - 1)
    return pl.BlockSpec(shape, lambda i, *_: (i,) + zeros)


def call(body, name, grid, ins, outs, scratch, flops, nbytes, scalars=0, vmem=60,
         collective=None):
    return pl.pallas_call(
        body,
        name=name,
        out_shape=[jax.ShapeDtypeStruct(s, d) for s, d, _ in outs],
        grid_spec=pltpu.PrefetchScalarGridSpec(
            num_scalar_prefetch=scalars,
            grid=(grid,),
            in_specs=ins,
            out_specs=[spec for _, _, spec in outs],
            scratch_shapes=scratch,
        ),
        compiler_params=pltpu.CompilerParams(
            dimension_semantics=("arbitrary",), vmem_limit_bytes=vmem * MIB,
            collective_id=collective, has_side_effects=collective is not None,
        ),
        cost_estimate=pl.CostEstimate(flops=flops, bytes_accessed=nbytes, transcendentals=0),
    )


def norm(z):
    mu = jnp.mean(z, axis=1, keepdims=True)
    sq = jnp.mean(z * z, axis=1, keepdims=True)
    r = lax.rsqrt(sq - mu * mu + EPS)
    return (z - mu) * r, r


def norm_back(e, n, r, gain):
    a = e * gain
    ma = jnp.mean(a, axis=1, keepdims=True)
    mn = jnp.mean(a * n, axis=1, keepdims=True)
    return r * (a - ma - n * mn)


def colsum(v):
    return jnp.sum(v, axis=0, keepdims=True)


def softmax_cols(s):
    e = jnp.exp(s - jnp.max(s, axis=0, keepdims=True))
    return e * (1.0 / jnp.sum(e, axis=0, keepdims=True))


def softmax_rows(s):
    e = jnp.exp(s - jnp.max(s, axis=1, keepdims=True))
    return e * (1.0 / jnp.sum(e, axis=1, keepdims=True))


MESH = pl.DeviceIdType.MESH


def digit(bit):
    return (lax.axis_index("dp") // (1 << bit)) % 2


def partner(bit):
    dp_at, mp_at = lax.axis_index("dp"), lax.axis_index("mp")
    if bit is None:
        return {"dp": dp_at, "mp": 1 - mp_at}
    return {"dp": dp_at + (1 << bit) - 2 * (1 << bit) * digit(bit), "mp": mp_at}


def remote(source, target, send_sem, got_sem, bit):
    return pltpu.make_async_remote_copy(
        src_ref=source, dst_ref=target, send_sem=send_sem, recv_sem=got_sem,
        device_id=partner(bit), device_id_type=MESH,
    )


def greet(links):
    barrier = pltpu.get_barrier_semaphore()
    for bit in links:
        pl.semaphore_signal(barrier, inc=1, device_id=partner(bit), device_id_type=MESH)


def met(links):
    pl.semaphore_wait(pltpu.get_barrier_semaphore(), len(links))


class Swap:
    def __init__(self, tiles, tile, width):
        self.tiles = tiles
        self.shape = (tiles, tile, width)
        self.scratch = [pltpu.VMEM(self.shape, BF)] + [pltpu.SemaphoreType.DMA((tiles,))] * 2

    def bind(self, target, refs):
        self.target = target
        self.buffer, self.send, self.got = refs

    def copy(self, tile):
        return remote(self.buffer.at[tile], self.target.at[tile], self.send.at[tile],
                      self.got.at[tile], None)

    def put(self, tile, value):
        @pl.when(tile == 0)
        def _():
            met((None,))

        self.buffer[tile] = value
        self.copy(tile).start()

        @pl.when(tile == self.tiles - 1)
        def _():
            for i in range(self.tiles):
                self.copy(i).wait()


def project_patches(patches, cross_kv, bias, padded):
    images, count, visual = patches.shape
    width = cross_kv.shape[2]
    group = 5

    def body(p_ref, w_ref, b_ref, k_ref, v_ref, rows, wcat):
        @pl.when(pl.program_id(0) == 0)
        def _():
            wcat[:, :width] = w_ref[0]
            wcat[:, width:] = w_ref[1]
            rows[...] = jnp.zeros_like(rows)

        for i in range(group):
            rows[padded * i : padded * i + count, :] = p_ref[i]
        out = nn(rows[...], wcat[...])
        k_ref[...] = out[:, :width].astype(BF)
        v_ref[...] = (out[:, width:] + b_ref[1:2, :].astype(F32)).astype(BF)

    tall = (images * padded, width)
    return call(
        body,
        "project_patches",
        images // group,
        [tiled((group, count, visual)), whole(cross_kv.shape), whole(bias.shape)],
        [(tall, BF, tiled((group * padded, width)))] * 2,
        [pltpu.VMEM((group * padded, visual), BF), pltpu.VMEM((visual, 2 * width), BF)],
        2 * images * padded * visual * 2 * width,
        patches.size * 2 + cross_kv.size * 2 + 4 * images * padded * width,
    )(patches, cross_kv, bias)


def self_forward(side, own, other, qkv_w, qkv_b, out_w, ids_col, ids_row, tile):
    tokens, here = own.shape
    width = 2 * here

    def body(side_ref, a_ref, z_ref, w_ref, b_ref, o_ref, ic_ref, ir_ref,
             qkv_ref, c_ref, part_ref, x_ref, wcat):
        @pl.when(pl.program_id(0) == 0)
        def _():
            for s in range(3):
                wcat[:, s * here : (s + 1) * here] = w_ref[s]

        mine, theirs = a_ref[...], z_ref[...]
        first = side_ref[0] == 0
        x_ref[:, :here] = jnp.where(first, mine, theirs)
        x_ref[:, here:] = jnp.where(first, theirs, mine)
        qkv = (nn(x_ref[...], wcat[...]) + b_ref[...]).astype(BF)
        qkv_ref[...] = qkv
        same = ic_ref[...] == ir_ref[0]
        parts = []
        for p in range(here // 128):
            q = qkv[:, 128 * p : 128 * p + 128]
            k = qkv[:, here + 128 * p : here + 128 * p + 128]
            v = qkv[:, 2 * here + 128 * p : 2 * here + 128 * p + 128]
            total = None
            for a in range(2):
                mask = head_mask(128, a, BF)
                s = jnp.where(same, nt(q * mask, k) * SCALE, BIG_NEG)
                o = nn(softmax_rows(s).astype(BF), v * mask)
                total = o if total is None else total + o
            parts.append(total)
        c = jnp.concatenate(parts, axis=1).astype(BF)
        c_ref[...] = c
        part_ref[...] = nn(c, o_ref[...]).astype(BF)

    return call(
        body,
        "self_forward",
        tokens // tile,
        [
            tiled((tile, here)),
            tiled((tile, here)),
            whole(qkv_w.shape),
            whole(qkv_b.shape),
            whole(out_w.shape),
            tiled((tile, 1)),
            tiled((1, 1, tile)),
        ],
        [
            ((tokens, 3 * here), BF, tiled((tile, 3 * here))),
            ((tokens, here), BF, tiled((tile, here))),
            ((tokens, width), BF, tiled((tile, width))),
            ((tokens, width), BF, tiled((tile, width))),
        ],
        [pltpu.VMEM((width, 3 * here), BF)],
        2 * tokens * width * 4 * here,
        tokens * (width + 4 * here + width) * 2 + 4 * width * here * 2,
        scalars=1,
    )(side, own, other, qkv_w, qkv_b, out_w, ids_col, ids_row)


def quads(here):
    return [(at, min(256, here - at)) for at in range(0, here, 256)]


def stacked(rows, span):
    return jnp.concatenate(
        [rows * head_mask(span, h, F32) for h in range(span // HD)], axis=0
    ).astype(BF)


def unstacked(tall, span, length):
    total = None
    for h in range(span // HD):
        piece = tall[h * length : (h + 1) * length] * head_mask(span, h, F32)
        total = piece if total is None else total + piece
    return total


def cross_forward(picks, text, mine, other, params, query_w, query_b, keys, values, out_w,
                  tile, length, count, padded):
    tokens, width = text.shape
    here = out_w.shape[0]
    rows = tile // length
    swap = Swap(tokens // tile, tile, width)
    keys = keys.reshape(-1, padded, here)
    values = values.reshape(-1, padded, here)

    def body(pick, x_ref, m_ref, t_ref, pr_ref, w_ref, b_ref, k_ref, v_ref, o_ref,
             n_ref, r_ref, y_ref, q_ref, c_ref, part_ref, got_ref, q32, c32, *swap_refs):
        swap.bind(got_ref, swap_refs)

        @pl.when(pl.program_id(0) == 0)
        def _():
            greet((None,))

        h = x_ref[...].astype(F32) + (m_ref[...].astype(F32) + t_ref[...].astype(F32)) + pr_ref[0:1, :]
        n, r = norm(h)
        n_ref[...] = n
        r_ref[...] = r
        y = (n * pr_ref[3:4, :] + pr_ref[6:7, :]).astype(BF)
        y_ref[...] = y
        q = nn(y, w_ref[...]) + b_ref[0:1, :].astype(F32)
        q32[...] = q
        q_ref[...] = q.astype(BF)
        base = pl.program_id(0) * rows
        for j in range(rows):
            k_row = k_ref[pick[base + j]]
            v_row = v_ref[pick[base + j]]
            for lo, span in quads(here):
                qs = stacked(q32[j * length : (j + 1) * length, lo : lo + span], span)
                s = nt(qs, k_row[:, lo : lo + span]) * SCALE
                live = lax.broadcasted_iota(jnp.int32, s.shape, 1) < count
                p = softmax_rows(jnp.where(live, s, -1e30))
                o = nn(p.astype(BF), v_row[:, lo : lo + span])
                c32[j * length : (j + 1) * length, lo : lo + span] = unstacked(o, span, length)
        c = c32[...].astype(BF)
        c_ref[...] = c
        part = nn(c, o_ref[...]).astype(BF)
        part_ref[...] = part
        swap.put(pl.program_id(0), part)

    full = tiled((tile, width))
    half = tiled((tile, here))
    return call(
        body,
        "cross_forward",
        tokens // tile,
        [full, full, full, whole(params.shape), whole(query_w.shape), whole(query_b.shape),
         whole(keys.shape), whole(values.shape), whole(out_w.shape)],
        [
            ((tokens, width), F32, full),
            ((tokens, 1), F32, tiled((tile, 1))),
            ((tokens, width), BF, full),
            ((tokens, here), BF, half),
            ((tokens, here), BF, half),
            ((tokens, width), BF, full),
            (swap.shape, BF, pl.BlockSpec(memory_space=pl.ANY)),
        ],
        [pltpu.VMEM((tile, here), F32)] * 2 + swap.scratch,
        2 * tokens * width * 2 * here + 4 * tokens * padded * here * 4,
        tokens * width * 14 + keys.size * 4,
        scalars=1,
        collective=3,
    )(picks, text, mine, other, params, query_w, query_b, keys, values, out_w)


def ffn_forward(normed, mine, other, params, in_w, in_b, out_w, tile):
    tokens, width = normed.shape
    hidden = in_w.shape[1]
    swap = Swap(tokens // tile, tile, width)

    def body(n1_ref, m_ref, t_ref, pr_ref, w_ref, b_ref, o_ref,
             n_ref, r_ref, y_ref, g_ref, d_ref, part_ref, got_ref, *swap_refs):
        swap.bind(got_ref, swap_refs)

        @pl.when(pl.program_id(0) == 0)
        def _():
            greet((None,))

        h = (n1_ref[...] * pr_ref[3:4, :] + pr_ref[6:7, :]) + (
            m_ref[...].astype(F32) + t_ref[...].astype(F32)
        ) + pr_ref[1:2, :]
        n, r = norm(h)
        n_ref[...] = n
        r_ref[...] = r
        y = (n * pr_ref[4:5, :] + pr_ref[7:8, :]).astype(BF)
        y_ref[...] = y
        u = nn(y, w_ref[...]) + b_ref[...].astype(F32)
        phi = 0.5 * (1.0 + lax.erf(u * math.sqrt(0.5)))
        g = (u * phi).astype(BF)
        g_ref[...] = g
        density = jnp.exp(u * u * -0.5) * (1.0 / math.sqrt(2.0 * math.pi))
        d_ref[...] = (phi + u * density).astype(BF)
        part = nn(g, o_ref[...]).astype(BF)
        part_ref[...] = part
        swap.put(pl.program_id(0), part)

    full = tiled((tile, width))
    wide = tiled((tile, hidden))
    return call(
        body,
        "ffn_forward",
        tokens // tile,
        [full, full, full, whole(params.shape), whole(in_w.shape), whole(in_b.shape),
         whole(out_w.shape)],
        [
            ((tokens, width), F32, full),
            ((tokens, 1), F32, tiled((tile, 1))),
            ((tokens, width), BF, full),
            ((tokens, hidden), BF, wide),
            ((tokens, hidden), BF, wide),
            ((tokens, width), BF, full),
            (swap.shape, BF, pl.BlockSpec(memory_space=pl.ANY)),
        ],
        swap.scratch,
        2 * tokens * width * 2 * hidden,
        tokens * width * 16 + tokens * hidden * 4 + width * hidden * 4,
        collective=4,
    )(normed, mine, other, params, in_w, in_b, out_w)


def ffn_backward(side, normed, mine, other, params, cot, slope, in_w, out_w, tile):
    tokens, width = normed.shape
    hidden = in_w.shape[1]
    here = width // 2

    def body(side_ref, n2_ref, m_ref, t_ref, pr_ref, e_ref, d_ref, w_ref, o_ref,
             j_ref, dh_ref, dhb_ref, du_ref, part_ref, sum_ref, wt, ot):
        @pl.when(pl.program_id(0) == 0)
        def _():
            wt[...] = w_ref[...].T
            ot[...] = o_ref[...].T
            sum_ref[...] = jnp.zeros_like(sum_ref)

        h = (n2_ref[...] * pr_ref[4:5, :] + pr_ref[7:8, :]) + (
            m_ref[...].astype(F32) + t_ref[...].astype(F32)
        ) + pr_ref[2:3, :]
        n, r = norm(h)
        joined = n * pr_ref[5:6, :] + pr_ref[8:9, :]
        j_ref[...] = jnp.where(side_ref[0] == 0, joined[:, :here], joined[:, here:])
        e = e_ref[...].astype(F32)
        dh = norm_back(e, n, r, pr_ref[5:6, :])
        dh_ref[...] = dh
        dhb = dh.astype(BF)
        dhb_ref[...] = dhb
        sum_ref[0:1, :] += colsum(e * n)
        sum_ref[1:2, :] += colsum(e)
        sum_ref[2:3, :] += colsum(dh)
        dg = nn(dhb, ot[...]).astype(BF)
        du = dg.astype(F32) * d_ref[...].astype(F32)
        total = colsum(du)
        sum_ref[4:5, :] += total[:, :width]
        sum_ref[5:6, :] += total[:, width:]
        dub = du.astype(BF)
        du_ref[...] = dub
        part_ref[...] = nn(dub, wt[...]).astype(BF)

    full = tiled((tile, width))
    wide = tiled((tile, hidden))
    return call(
        body,
        "ffn_backward",
        tokens // tile,
        [full, full, full, whole(params.shape), full, wide, whole(in_w.shape), whole(out_w.shape)],
        [
            ((tokens, here), F32, tiled((tile, here))),
            ((tokens, width), F32, full),
            ((tokens, width), BF, full),
            ((tokens, hidden), BF, wide),
            ((tokens, width), BF, full),
            ((8, width), F32, whole((8, width))),
        ],
        [pltpu.VMEM((hidden, width), BF), pltpu.VMEM((width, hidden), BF)],
        2 * tokens * width * 2 * hidden,
        tokens * width * 22 + tokens * hidden * 4 + width * hidden * 4,
        scalars=1,
    )(side, normed, mine, other, params, cot, slope, in_w, out_w)


def cross_backward(picks, grad, mine, other, params, normed, spread, query, keys, values,
                   query_w, out_w, tile, length, count, padded):
    tokens, width = grad.shape
    here = out_w.shape[0]
    rows = tile // length
    steps = tokens // tile
    tall = keys.shape[0]

    def body(pick, g_ref, m_ref, t_ref, pr_ref, n_ref, r_ref, q_ref, k_ref, v_ref, w_ref, o_ref,
             dh_ref, dhb_ref, dq_ref, part_ref, kv_ref, sum_ref,
             wt, ot, q32, c32, dq32, dk_acc, dv_acc):
        @pl.when(pl.program_id(0) == 0)
        def _():
            wt[...] = w_ref[...].T
            ot[...] = o_ref[...].T
            sum_ref[...] = jnp.zeros_like(sum_ref)
            dk_acc[...] = jnp.zeros_like(dk_acc)
            dv_acc[...] = jnp.zeros_like(dv_acc)

        e = g_ref[...] + (m_ref[...].astype(F32) + t_ref[...].astype(F32))
        n = n_ref[...]
        dh = norm_back(e, n, r_ref[...], pr_ref[4:5, :])
        dh_ref[...] = dh
        dhb = dh.astype(BF)
        dhb_ref[...] = dhb
        sum_ref[0:1, :] += colsum(e * n)
        sum_ref[1:2, :] += colsum(e)
        sum_ref[2:3, :] += colsum(dh)
        c32[...] = nn(dhb, ot[...])
        q32[...] = q_ref[...].astype(F32)
        base = pl.program_id(0) * rows
        for j in range(rows):
            at = pl.multiple_of(pick[base + j] * padded, padded)
            for lo, span in quads(here):
                here_rows = slice(j * length, (j + 1) * length)
                cols = slice(lo, lo + span)
                qs = stacked(q32[here_rows, cols], span)
                cs = stacked(c32[here_rows, cols], span)
                k = k_ref[pl.ds(at, padded), cols]
                s = nt(k, qs) * SCALE
                live = lax.broadcasted_iota(jnp.int32, s.shape, 0) < count
                p = softmax_cols(jnp.where(live, s, -1e30))
                dp = nt(v_ref[pl.ds(at, padded), cols], cs)
                ds = (p * (dp - jnp.sum(dp * p, axis=0, keepdims=True))).astype(BF)
                dv_acc[pl.ds(at, padded), cols] += nn(p.astype(BF), cs)
                dk_acc[pl.ds(at, padded), cols] += nn(ds, qs) * SCALE
                dq32[here_rows, cols] = unstacked(tn(ds, k), span, length) * SCALE
        dq = dq32[...]
        sum_ref[3:4, :here] += colsum(dq)
        dqb = dq.astype(BF)
        dq_ref[...] = dqb
        part_ref[...] = nn(dqb, wt[...]).astype(BF)

        @pl.when(pl.program_id(0) == steps - 1)
        def _():
            def step(i, total):
                at = pl.ds(pl.multiple_of(i * padded, padded), padded)
                kv_ref[at, :here] = dk_acc[at, :].astype(BF)
                dv = dv_acc[at, :]
                kv_ref[at, here:] = dv.astype(BF)
                return total + colsum(dv)

            total = lax.fori_loop(0, tall // padded, step, jnp.zeros((1, here), F32))
            sum_ref[3:4, here:] = total

    full = tiled((tile, width))
    half = tiled((tile, here))
    return call(
        body,
        "cross_backward",
        steps,
        [full, full, full, whole(params.shape), full, tiled((tile, 1)), half, whole(keys.shape),
         whole(values.shape), whole(query_w.shape), whole(out_w.shape)],
        [
            ((tokens, width), F32, full),
            ((tokens, width), BF, full),
            ((tokens, here), BF, half),
            ((tokens, width), BF, full),
            ((tall, 2 * here), BF, whole((tall, 2 * here))),
            ((8, width), F32, whole((8, width))),
        ],
        [pltpu.VMEM((here, width), BF), pltpu.VMEM((width, here), BF)]
        + [pltpu.VMEM((tile, here), F32)] * 3
        + [pltpu.VMEM((tall, here), F32)] * 2,
        2 * tokens * width * 2 * here + 10 * tokens * padded * here * 4,
        tokens * width * 20 + keys.size * 8,
        scalars=1,
    )(picks, grad, mine, other, params, normed, spread, query, keys, values, query_w, out_w)


def self_tile(grad, mine, other, pr_ref, n, r, q_ref, wt, ot, same, sum_ref, keep_ref, send_ref,
              first, here, between=None):
    e = grad + (mine.astype(F32) + other.astype(F32))
    dh = norm_back(e, n, r, pr_ref[3:4, :])
    dhb = dh.astype(BF)
    sum_ref[0:1, :] += colsum(e * n)
    sum_ref[1:2, :] += colsum(e)
    sum_ref[2:3, :] += colsum(dh)
    dc = nn(dhb, ot[...]).astype(BF)
    grads = [[], [], []]
    for p in range(here // 128):
        if between is not None:
            between(p)
        q = q_ref[:, 128 * p : 128 * p + 128]
        k = q_ref[:, here + 128 * p : here + 128 * p + 128]
        v = q_ref[:, 2 * here + 128 * p : 2 * here + 128 * p + 128]
        c = dc[:, 128 * p : 128 * p + 128]
        sums = [None, None, None]
        for a in range(2):
            mask = head_mask(128, a, BF)
            qm = q * mask
            cm = c * mask
            pt = softmax_cols(jnp.where(same, nt(k, qm) * SCALE, BIG_NEG))
            dp = nt(v, cm)
            ds = (pt * (dp - jnp.sum(dp * pt, axis=0, keepdims=True))).astype(BF)
            new = (tn(ds, k * mask), nn(ds, qm), nn(pt.astype(BF), cm))
            sums = [b if a_ is None else a_ + b for a_, b in zip(sums, new)]
        grads[0].append(sums[0] * SCALE)
        grads[1].append(sums[1] * SCALE)
        grads[2].append(sums[2])
    dq, dk, dv = (jnp.concatenate(g, axis=1) for g in grads)
    sum_ref[3:4, :here] += colsum(dq)
    sum_ref[3:4, here:] += colsum(dv)
    dqkv = jnp.concatenate((dq, dk, dv), axis=1).astype(BF)
    part = nn(dqkv, wt[...])
    keep_ref[...] = jnp.where(first, dh[:, :here] + part[:, :here], dh[:, here:] + part[:, here:])
    send_ref[...] = jnp.where(first, part[:, here:], part[:, :here]).astype(BF)
    return dhb, dqkv


def self_backward(side, grad, mine, other, params, normed, spread, qkv, qkv_w, out_w,
                  ids_col, ids_row, tile):
    tokens, width = grad.shape
    here = out_w.shape[0]

    def body(side_ref, g_ref, m_ref, t_ref, pr_ref, n_ref, r_ref, q_ref, w_ref, o_ref,
             ic_ref, ir_ref, dhb_ref, dq_ref, keep_ref, send_ref, sum_ref, wt, ot):
        @pl.when(pl.program_id(0) == 0)
        def _():
            for s in range(3):
                wt[s * here : (s + 1) * here, :] = w_ref[s].T
            ot[...] = o_ref[...].T
            sum_ref[...] = jnp.zeros_like(sum_ref)

        dhb, dqkv = self_tile(
            g_ref[...], m_ref[...], t_ref[...], pr_ref, n_ref[...], r_ref[...], q_ref, wt, ot,
            ic_ref[...] == ir_ref[0], sum_ref, keep_ref, send_ref, side_ref[0] == 0, here,
        )
        dhb_ref[...] = dhb
        dq_ref[...] = dqkv

    full = tiled((tile, width))
    half = tiled((tile, here))
    return call(
        body,
        "self_backward",
        tokens // tile,
        [full, full, full, whole(params.shape), full, tiled((tile, 1)), tiled((tile, 3 * here)),
         whole(qkv_w.shape), whole(out_w.shape), tiled((tile, 1)), tiled((1, 1, tile))],
        [
            ((tokens, width), BF, full),
            ((tokens, 3 * here), BF, tiled((tile, 3 * here))),
            ((tokens, here), F32, half),
            ((tokens, here), BF, half),
            ((8, width), F32, whole((8, width))),
        ],
        [pltpu.VMEM((3 * here, width), BF), pltpu.VMEM((width, here), BF)],
        2 * tokens * width * 4 * here + 10 * tokens * tile * here,
        tokens * width * 16 + 8 * width * here,
        scalars=1,
    )(side, grad, mine, other, params, normed, spread, qkv, qkv_w, out_w, ids_col, ids_row)


def patch_send(side, pair, cross_kv, images, count, padded):
    width = cross_kv.shape[2]
    visual = cross_kv.shape[1]
    half = visual // 2
    group = 5

    def body(side_ref, p_ref, w_ref, s_ref, wt):
        @pl.when(pl.program_id(0) == 0)
        def _():
            wt[:width, :] = w_ref[0].T
            wt[width:, :] = w_ref[1].T

        out = nn(p_ref[...], wt[...])
        for i in range(group):
            s_ref[i] = out[padded * i : padded * i + count].astype(BF)

    return call(
        body,
        "patch_send",
        images // group,
        [
            tiled((group * padded, 2 * width)),
            pl.BlockSpec((2, half, width), lambda i, s: (0, 1 - s[0], 0), pipeline_mode=pl.Buffered(1)),
        ],
        [((images, count, half), BF, tiled((group, count, half)))],
        [pltpu.VMEM((2 * width, half), BF)],
        2 * images * padded * half * 2 * width,
        images * padded * (2 * width + half) * 2,
        scalars=1,
    )(side, pair, cross_kv)[0]


def patch_keep(side, pair, cross_kv, arrived, padded):
    images, count, half = arrived.shape
    width = cross_kv.shape[2]
    group = 5

    def body(side_ref, p_ref, w_ref, a_ref, o_ref, wt):
        @pl.when(pl.program_id(0) == 0)
        def _():
            wt[:width, :] = w_ref[0].T
            wt[width:, :] = w_ref[1].T

        out = nn(p_ref[...], wt[...])
        for i in range(group):
            o_ref[i] = out[padded * i : padded * i + count] + a_ref[i].astype(F32)

    return call(
        body,
        "patch_keep",
        images // group,
        [
            tiled((group * padded, 2 * width)),
            pl.BlockSpec((2, half, width), lambda i, s: (0, s[0], 0), pipeline_mode=pl.Buffered(1)),
            tiled((group, count, half)),
        ],
        [((images, count, half), F32, tiled((group, count, half)))],
        [pltpu.VMEM((2 * width, half), BF)],
        2 * images * padded * half * 2 * width,
        images * padded * (2 * width + half * 3) * 2,
        scalars=1,
    )(side, pair, cross_kv, arrived)[0]


def shards_of(bit, count):
    return [i for i in range(count) if not (i >> bit) & 1]


def split_rows(acc, send_ref, keep_ref, bits_ref, bit, shards, size):
    mine = bits_ref[bit]
    for slot, shard in enumerate(shards_of(bit, shards)):
        kept = pl.multiple_of((shard + (mine << bit)) * size, size)
        sent = pl.multiple_of((shard + ((1 - mine) << bit)) * size, size)
        keep_ref[slot] = acc[pl.ds(kept, size), :].astype(BF)
        send_ref[slot] = acc[pl.ds(sent, size), :].astype(BF)


def split_outside(full, bit, shards, bits):
    size = full.shape[0] // shards
    inner = 1 << bit
    view = full.reshape(shards // (2 * inner), 2, inner, size, full.shape[1])
    return [
        lax.dynamic_index_in_dim(view, at, 1, keepdims=False).reshape(
            shards // 2, size, full.shape[1]
        )
        for at in (1 - bits[bit], bits[bit])
    ]


def grad_weight(bits, groups, shards, name, tile):
    tokens, width = groups[0][1][0][0].shape
    size = width // shards
    inside = size % 16 == 0
    terms, specs, outs, operands = [], [], [], []
    at = 0
    for number, (bit, members) in enumerate(groups):
        first = at
        for left, right, column, columns in members:
            terms.append((at, columns // tile, number, bit))
            operands += [left, right]
            specs += [
                whole(left.shape),
                pl.BlockSpec(
                    (tokens, tile),
                    lambda i, *_, a=at, n=columns // tile, c=column // tile: (
                        0, c + jnp.clip(i - a, 0, n - 1)),
                ),
            ]
            at += columns // tile
        span = at - first
        if inside:
            for _ in range(2):
                outs.append((
                    (shards // 2, size, span * tile), BF,
                    pl.BlockSpec(
                        (shards // 2, size, tile),
                        lambda i, *_, a=first, n=span: (0, 0, jnp.clip(i - a, 0, n - 1)),
                    ),
                ))
        else:
            outs.append((
                (width, span * tile), BF,
                pl.BlockSpec(
                    (width, tile),
                    lambda i, *_, a=first, n=span: (0, jnp.clip(i - a, 0, n - 1)),
                ),
            ))
    total = at

    def body(bits_ref, *refs):
        ins = refs[: len(operands)]
        results = refs[len(operands) : -2]
        lt, acc = refs[-2:]
        step = pl.program_id(0)
        for which, (start, count, number, bit) in enumerate(terms):
            l_ref, r_ref = ins[2 * which : 2 * which + 2]

            if which == 0 or operands[2 * which] is not operands[2 * which - 2]:
                @pl.when(step == start)
                def _(l_ref=l_ref):
                    lt[...] = l_ref[...].T

            @pl.when((step >= start) & (step < start + count))
            def _(r_ref=r_ref, number=number, bit=bit):
                acc[...] = nn(lt[...], r_ref[...])
                if inside:
                    split_rows(acc, results[2 * number], results[2 * number + 1], bits_ref, bit,
                               shards, size)
                else:
                    results[number][...] = acc[...].astype(BF)

    made = call(
        body,
        name,
        total,
        specs,
        outs,
        [pltpu.VMEM((width, tokens), BF), pltpu.VMEM((width, tile), F32)],
        2 * tokens * width * total * tile,
        tokens * (width + total * tile) * 2 + width * total * tile * 2,
        scalars=1,
    )(bits, *operands)
    if inside:
        return [made[2 * i : 2 * i + 2] for i in range(len(groups))]
    return [split_outside(m, g[0], shards, bits) for m, g in zip(made, groups)]


def grad_weight_patches(bits, patches, pair, padded, shards, bit):
    images, count, visual = patches.shape
    size = visual // shards
    wide = pair.shape[1]
    group = 5
    steps = images // group
    inside = size % 16 == 0

    def body(bits_ref, p_ref, g_ref, *refs):
        rows, acc = refs[-2:]
        at = pl.program_id(0)

        @pl.when(at == 0)
        def _():
            rows[...] = jnp.zeros_like(rows)

        for i in range(group):
            rows[padded * i : padded * i + count, :] = p_ref[i]
        new = tn(rows[...], g_ref[...])

        @pl.when(at == 0)
        def _():
            acc[...] = new

        @pl.when(at > 0)
        def _():
            acc[...] += new

        @pl.when(at == steps - 1)
        def _():
            if inside:
                split_rows(acc, refs[0], refs[1], bits_ref, bit, shards, size)
            else:
                refs[0][...] = acc[...].astype(BF)

    half = (shards // 2, size, wide)
    full = (visual, wide)
    made = call(
        body,
        "grad_weight_patches",
        steps,
        [tiled((group, count, visual)), tiled((group * padded, wide))],
        [(half, BF, whole(half))] * 2 if inside else [(full, BF, whole(full))],
        [pltpu.VMEM((group * padded, visual), BF), pltpu.VMEM((visual, wide), F32)],
        2 * images * padded * visual * wide,
        patches.size * 2 + pair.size * 2 + visual * wide * 2,
        scalars=1,
    )(bits, patches, pair)
    return made if inside else split_outside(made[0], bit, shards, bits)


ORDERS = ((0, 1, 2, 3), (1, 2, 0, 3), (2, 0, 1, 3))
LINKS = (None, 0, 1, 2, 3)
FFN_STEPS = ((2, 0), (3, 2))


class Stream:
    def __init__(self, rows, columns, order, first=0, last=3):
        self.rows, self.columns, self.order = rows, columns, order
        self.first, self.last = first, last

    def shape(self, t):
        return (8 >> t, self.rows, self.columns)

    def position(self, t):
        return sorted(set(self.order) - set(self.order[:t])).index(self.order[t])

    def scratch(self, made):
        steps = range(self.first, self.last + 1)
        shapes = [pltpu.VMEM(self.shape(t), BF) for t in steps]
        for t in range(made, self.last + 1):
            shapes += [pltpu.VMEM(self.shape(t), BF)] * 2
        return shapes + [pltpu.SemaphoreType.DMA((4,))] * 2

    def bind(self, refs, made, given=None):
        size = len(self.scratch(made))
        mine, rest = refs[:size], refs[size:]
        steps = self.last + 1 - self.first
        self.got = {self.first + i: mine[i] for i in range(steps)}
        self.pairs = {}
        for i, t in enumerate(range(made, self.last + 1)):
            self.pairs[t] = mine[steps + 2 * i : steps + 2 * i + 2]
        if given is not None:
            self.pairs[made - 1] = given
        self.sems = mine[-2:]
        return rest

    def copy(self, t):
        return remote(self.pairs[t][0], self.got[t], self.sems[0].at[t], self.sems[1].at[t],
                      self.order[t])

    def start(self, t):
        self.copy(t).start()

    def total(self, t, shard):
        return self.pairs[t][1][shard].astype(F32) + self.got[t][shard].astype(F32)

    def fold(self, t, target):
        mine = digit(self.order[t + 1])
        low = 1 << self.position(t + 1)
        send, keep = target
        for j in range(8 >> (t + 1)):
            base = (j // low) * 2 * low + j % low
            send[j] = self.total(t, base + (1 - mine) * low).astype(BF)
            keep[j] = self.total(t, base + mine * low).astype(BF)

    def advance(self, t):
        self.copy(t).wait()
        self.fold(t, self.pairs[t + 1])
        self.start(t + 1)

    def finish(self):
        self.copy(3).wait()
        return self.total(3, 0)


def split_shards(full, columns, pair, bit, size):
    mine = digit(bit)
    for slot, shard in enumerate(shards_of(bit, 16)):
        kept = pl.multiple_of((shard + mine * (1 << bit)) * size, 16)
        sent = pl.multiple_of((shard + (1 - mine) * (1 << bit)) * size, 16)
        pair[1][slot] = full[pl.ds(kept, size), columns].astype(BF)
        pair[0][slot] = full[pl.ds(sent, size), columns].astype(BF)


def small_out(shape, dtype=F32):
    return (shape, dtype, whole(shape))


def rows_backward(ffn_kept, ffn_got, cross_terms, grad, part, params, normed, spread, qkv,
                  qkv_w, out_w, ids_col, ids_row, text, context, tile):
    tokens, width = grad.shape
    here = out_w.shape[0]
    tiles = tokens // tile
    size = width // 16
    third = 2 * here // 3
    ffn_cols = ffn_kept[0].shape[2]
    self_cols = 4 * here // 3
    dhb_two, cross_ctx, y_one, dq_cross = cross_terms
    begin = 2
    after_self = begin + tiles
    steps = after_self + 4
    ffn = [Stream(size, ffn_cols, order) for order in ORDERS]
    cross = [Stream(size, third, order, 0, 0) for order in ORDERS]
    self_streams = [Stream(size, self_cols, order) for order in ORDERS]

    def body(*refs):
        ffn_refs, refs = refs[:6], refs[6:]
        (l0_ref, r0_ref, l1_ref, r1_ref, g_ref, part_ref, mine_ref, pr_ref, n_ref, r_ref, q_ref,
         w_ref, o_ref, ic_ref, ir_ref, x_ref, c_ref) = refs[:17]
        keep_ref, send_ref, sum_ref, ffn_ref = refs[17:21]
        self_out, cross_out, rest = refs[21:27], refs[27:33], refs[33:]
        (lt, acc, wt, ot, other, dq_all, dhb_all, full, part_sems) = rest[:9]
        ffn_local, ffn_sems, rest = rest[9:15], rest[15], rest[16:]
        for which, stream in enumerate(ffn):
            rest = stream.bind(rest, 1)
            stream.pairs[0] = (None, ffn_local[2 * which])
            stream.got[0] = ffn_local[2 * which + 1]
        for stream in cross:
            rest = stream.bind(rest, 0)
        at = pl.program_id(0)
        side = lax.axis_index("mp")
        loads = [
            pltpu.make_async_copy(ffn_refs[i], ffn_local[i], ffn_sems.at[i]) for i in range(6)
        ]
        part_copy = remote(part_ref, other, part_sems.at[0], part_sems.at[1], None)

        @pl.when(at == 0)
        def _():
            greet(LINKS)
            for load in loads:
                load.start()
            lt[...] = l0_ref[...].T
            sum_ref[...] = jnp.zeros_like(sum_ref)
            met(LINKS)
            part_copy.start()
            for which, stream in enumerate(ffn):
                loads[2 * which].wait()
                loads[2 * which + 1].wait()
                stream.fold(0, stream.pairs[1])
                stream.start(1)
            acc[...] = nn(lt[...], r0_ref[...])
            full[:, :here] = acc[...].astype(BF)

        @pl.when(at == 1)
        def _():
            lt[...] = l1_ref[...].T
            acc[...] = nn(lt[...], r1_ref[...])
            full[:, here : 2 * here] = acc[...].astype(BF)
            for which, stream in enumerate(cross):
                split_shards(full, slice(which * third, (which + 1) * third), stream.pairs[0],
                             stream.order[0], size)
            for s in range(3):
                wt[s * here : (s + 1) * here, :] = w_ref[s].T
            ot[...] = o_ref[...].T
            part_copy.wait()

        def between(pair):
            for t, (step, place) in enumerate(FFN_STEPS):
                if pair != place:
                    continue

                @pl.when(at == begin + step)
                def _(t=t):
                    for stream in ffn:
                        stream.advance(t + 1)
                    if t == 1:
                        for stream in cross:
                            stream.start(0)

        @pl.when((at >= begin) & (at < after_self))
        def _():
            i = at - begin
            dhb, dqkv = self_tile(
                g_ref[...], mine_ref[...], other[i], pr_ref, n_ref[...], r_ref[...], q_ref,
                wt, ot, ic_ref[...] == ir_ref[0], sum_ref, keep_ref, send_ref, side == 0, here,
                between,
            )
            for j in range(tiles):
                @pl.when(i == j)
                def _(j=j):
                    dq_all[j * tile : (j + 1) * tile, :] = dqkv
                    dhb_all[j * tile : (j + 1) * tile, :] = dhb

        for j in range(4):
            @pl.when(at == after_self + j)
            def _(j=j):
                if j == 0:
                    lt[...] = x_ref[...].T
                if j == 3:
                    lt[...] = dhb_all[...].T
                right = c_ref[...] if j == 3 else dq_all[:, j * here : (j + 1) * here]
                acc[...] = nn(lt[...], right)
                full[:, j * here : (j + 1) * here] = acc[...].astype(BF)
                if j == 3:
                    for which, stream in enumerate(self_streams):
                        split_shards(
                            full, slice(which * self_cols, (which + 1) * self_cols),
                            self_out[2 * which : 2 * which + 2], stream.order[0], size,
                        )
                    for which, stream in enumerate(cross):
                        stream.copy(0).wait()
                        stream.fold(0, cross_out[2 * which : 2 * which + 2])
                    for which, stream in enumerate(ffn):
                        ffn_ref[:, which * ffn_cols : (which + 1) * ffn_cols] = stream.finish()

    anywhere = pl.BlockSpec(memory_space=pl.ANY)

    def rows(columns):
        return pl.BlockSpec((tile, columns), lambda i: (jnp.clip(i - begin, 0, tiles - 1), 0))

    ids_spec = pl.BlockSpec((1, 1, tile), lambda i: (jnp.clip(i - begin, 0, tiles - 1), 0, 0))
    ffn_arrays = [a for pair in zip(ffn_kept, ffn_got) for a in pair]
    operands = ffn_arrays + [
        dhb_two, cross_ctx, y_one, dq_cross, grad, part.reshape(tiles, tile, width), part, params,
        normed, spread, qkv, qkv_w, out_w, ids_col, ids_row, text, context,
    ]
    ins = [anywhere] * 6 + [
        whole(dhb_two.shape), whole(cross_ctx.shape), whole(y_one.shape), whole(dq_cross.shape),
        rows(width), anywhere, rows(width), whole(params.shape), rows(width), rows(1),
        rows(3 * here), whole(qkv_w.shape), whole(out_w.shape), rows(1), ids_spec,
        whole(text.shape), whole(context.shape),
    ]
    outs = [
        ((tokens, here), F32, rows(here)),
        ((tokens, here), BF, rows(here)),
        small_out((8, width)),
        small_out((size, 3 * ffn_cols)),
    ]
    outs += [small_out(self_streams[0].shape(0), BF)] * 6
    outs += [small_out(cross[0].shape(1), BF)] * 6
    scratch = [
        pltpu.VMEM((width, tokens), BF),
        pltpu.VMEM((width, here), F32),
        pltpu.VMEM((3 * here, width), BF),
        pltpu.VMEM((width, here), BF),
        pltpu.VMEM((tiles, tile, width), BF),
        pltpu.VMEM((tokens, 3 * here), BF),
        pltpu.VMEM((tokens, width), BF),
        pltpu.VMEM((width, 4 * here), BF),
        pltpu.SemaphoreType.DMA((2,)),
    ]
    scratch += [pltpu.VMEM(ffn[0].shape(0), BF)] * 6 + [pltpu.SemaphoreType.DMA((6,))]
    for stream in ffn:
        stream.first = 1
        scratch += stream.scratch(1)
    for stream in cross:
        scratch += stream.scratch(0)
    made = call(
        body, "rows_backward", steps, ins, outs, scratch,
        2 * tokens * width * 10 * here, tokens * width * 30, collective=1,
    )(*operands)
    return made[:4], [made[4 + 2 * i : 6 + 2 * i] for i in range(3)], [
        made[10 + 2 * i : 12 + 2 * i] for i in range(3)]


def patch_backward(patches, pair, cross_kv, cross_pairs, self_pairs, sums, padded):
    images, count, visual = patches.shape
    width = cross_kv.shape[2]
    half = visual // 2
    wide = 2 * width
    size = visual // 16
    group = 5
    steps = images // group
    small = cross_pairs[0][0].shape[1]
    third = wide // 3
    self_cols = self_pairs[0][0].shape[2]
    cross = [Stream(small, third, order, 1) for order in ORDERS]
    selves = [Stream(small, self_cols, order) for order in ORDERS]
    kvs = [Stream(size, third, order) for order in ORDERS]
    given = list(cross_pairs) + list(self_pairs)

    def body(p_ref, g_ref, w_ref, s1_ref, s2_ref, s3_ref, *refs):
        firsts = [refs[2 * i : 2 * i + 2] for i in range(6)]
        out_ref, cross_ref, self_ref, kv_ref, sum_ref = refs[12:17]
        rows, acc, wt, send, got, send_sem, got_sem, sum_now, sum_got, sum_sems = refs[17:27]
        p_all, g_all, load_sems, out_sems = refs[27:31]
        rest = refs[31:]
        for which, stream in enumerate(cross):
            rest = stream.bind(rest, 2, firsts[which])
        for which, stream in enumerate(selves):
            rest = stream.bind(rest, 1, firsts[3 + which])
        for stream in kvs:
            rest = stream.bind(rest, 0)
        side = lax.axis_index("mp")
        at = pl.program_id(0)

        def patch_copy(tile):
            return remote(send.at[tile], got.at[tile], send_sem.at[tile], got_sem.at[tile], None)

        def loads(tile):
            images_at = pl.ds(tile * group, group)
            rows_at = pl.ds(pl.multiple_of(tile * group * padded, 16), group * padded)
            return (
                pltpu.make_async_copy(p_ref.at[images_at], p_all.at[tile], load_sems.at[2 * tile]),
                pltpu.make_async_copy(g_ref.at[rows_at], g_all.at[tile], load_sems.at[2 * tile + 1]),
            )

        def store(tile):
            images_at = pl.ds(tile * group, group)
            return pltpu.make_async_copy(send.at[tile], out_ref.at[images_at], out_sems.at[tile])

        def sum_copy(bit):
            return remote(sum_now.at[bit], sum_got.at[bit], sum_sems.at[bit],
                          sum_sems.at[4 + bit], bit)

        @pl.when(at == 0)
        def _():
            greet(LINKS)
            for tile in range(steps):
                for load in loads(tile):
                    load.start(priority=1)
            rows[...] = jnp.zeros_like(rows)
            sum_now[0, :8] = s3_ref[...]
            sum_now[0, 8:12] = s1_ref[0:4]
            sum_now[0, 12:16] = s2_ref[0:4]
            met(LINKS)
            sum_copy(0).start()
            for stream in selves:
                stream.start(0)
            for stream in cross:
                stream.start(1)
            wt[:width, :] = w_ref[0].T
            wt[width:, :] = w_ref[1].T

        def sum_next(bit):
            sum_copy(bit).wait()
            sum_now[bit + 1] = sum_now[bit] + sum_got[bit]
            sum_copy(bit + 1).start()

        def advance(streams, t):
            for stream in streams:
                stream.advance(t)

        @pl.when(at == steps - 1)
        def _():
            sum_next(0)
            advance(selves, 0)
            advance(cross, 1)

        @pl.when(at == steps + 1)
        def _():
            sum_next(1)
            advance(selves, 1)
            for stream in kvs:
                stream.start(0)
            advance(cross, 2)

        @pl.when(at == steps + 3)
        def _():
            sum_next(2)
            advance(selves, 2)

        for step in range(3):
            @pl.when(at == 2 * steps + (1, 3, 4)[step])
            def _(step=step):
                advance(kvs, step)

        @pl.when(at < steps)
        def _():
            for load in loads(at):
                load.wait()
            for i in range(group):
                rows[padded * i : padded * i + count, :] = p_all[at, i]
            new = tn(rows[...], g_all[at])

            @pl.when(at == 0)
            def _():
                acc[...] = new

            @pl.when(at > 0)
            def _():
                acc[...] += new

            @pl.when(at == steps - 1)
            def _():
                for which, stream in enumerate(kvs):
                    split_shards(acc, slice(which * third, (which + 1) * third), stream.pairs[0],
                                 stream.order[0], size)

        def product(tile, half_at):
            lanes = pl.ds(pl.multiple_of(half_at * half, 128), half)
            return nn(g_all[tile], wt[:, lanes])

        @pl.when((at >= steps) & (at < 2 * steps))
        def _():
            tile = at - steps
            out = product(tile, 1 - side)
            for i in range(group):
                send[tile, i] = out[padded * i : padded * i + count].astype(BF)
            patch_copy(tile).start()

        @pl.when(at >= 2 * steps)
        def _():
            tile = at - 2 * steps
            out = product(tile, side)
            patch_copy(tile).wait()
            for i in range(group):
                mine = out[padded * i : padded * i + count]
                send[tile, i] = (mine + got[tile, i].astype(F32)).astype(BF)
            store(tile).start(priority=1)

        @pl.when(at == 3 * steps - 1)
        def _():
            sum_copy(3).wait()
            sum_ref[...] = sum_now[3] + sum_got[3]
            for target, streams in ((cross_ref, cross), (self_ref, selves), (kv_ref, kvs)):
                for which, stream in enumerate(streams):
                    lo = which * stream.columns
                    target[:, lo : lo + stream.columns] = stream.finish()
            for tile in range(steps):
                store(tile).wait()

    anywhere = pl.BlockSpec(memory_space=pl.ANY)
    ins = [
        anywhere,
        anywhere,
        whole(cross_kv.shape),
    ] + [whole(s.shape) for s in sums]
    operands = [patches, pair, cross_kv, *sums]
    for sent, kept in given:
        ins += [anywhere, whole(kept.shape)]
        operands += [sent, kept]
    scratch = [
        pltpu.VMEM((group * padded, visual), BF),
        pltpu.VMEM((visual, wide), F32),
        pltpu.VMEM((wide, visual), BF),
        pltpu.VMEM((steps, group, count, half), BF),
        pltpu.VMEM((steps, group, count, half), BF),
        pltpu.SemaphoreType.DMA((steps,)),
        pltpu.SemaphoreType.DMA((steps,)),
        pltpu.VMEM((4, 16, wide), F32),
        pltpu.VMEM((4, 16, wide), F32),
        pltpu.SemaphoreType.DMA((8,)),
        pltpu.VMEM((steps, group, count, visual), BF),
        pltpu.VMEM((steps, group * padded, wide), BF),
        pltpu.SemaphoreType.DMA((2 * steps,)),
        pltpu.SemaphoreType.DMA((steps,)),
    ]
    for stream in cross:
        scratch += stream.scratch(2)
    for stream in selves:
        scratch += stream.scratch(1)
    for stream in kvs:
        scratch += stream.scratch(0)
    return call(
        body,
        "patch_backward",
        3 * steps,
        ins,
        [
            ((images, count, half), BF, anywhere),
            small_out((small, wide)),
            small_out((small, 3 * self_cols)),
            small_out((size, wide)),
            small_out((16, wide)),
        ],
        scratch,
        2 * images * padded * visual * wide * 2,
        patches.size * 2 + pair.size * 6 + images * count * half * 4,
        collective=2,
    )(*operands)


def finish(side, patch, text_keep, text_other, ffn, cross, self_sum, kv, sums):
    images, count, half = patch.shape
    tokens, here = text_keep.shape
    block = ffn.shape[0]
    hidden = ffn.shape[1] // 2
    steps = 5
    tile = tokens // steps
    group = images // steps

    def body(side_ref, p_ref, k_ref, t_ref, f_ref, c_ref, s_ref, v_ref, m_ref,
             patch_out, text_out, qkv_out, so_out, cq_out, kv_out, co_out, fi_out, fo_out,
             sb_out, cb_out, fb_out, br_out, ga_out, sh_out):
        patch_out[...] = p_ref[...].astype(F32)
        text_out[...] = k_ref[...] + t_ref[...].astype(F32)

        @pl.when(pl.program_id(0) == 0)
        def _():
            for i in range(3):
                qkv_out[i] = s_ref[:, i * here : (i + 1) * here]
            so_out[...] = s_ref[:, 3 * here :]
            cq_out[...] = c_ref[:, here:]
            co_out[...] = c_ref[:, :here]
            fi_out[...] = f_ref[:, hidden:]
            fo_out[...] = f_ref[:, :hidden]
            for i in range(2):
                kv_out[i] = v_ref[:, i * here : (i + 1) * here]
                sb_out[i : i + 1, :] = m_ref[11:12, i * here : (i + 1) * here]
                cb_out[i : i + 1, :] = m_ref[15:16, i * here : (i + 1) * here]
                fb_out[:, 2 * i * here : 2 * (i + 1) * here] = m_ref[4 + i : 5 + i, :]
            first = side_ref[0] == 0
            for out, at in ((ga_out, 0), (sh_out, 1), (br_out, 2)):
                for i, row in enumerate((8 + at, 12 + at, at)):
                    out[i : i + 1, :] = jnp.where(
                        first, m_ref[row : row + 1, :here], m_ref[row : row + 1, here:]
                    )

    rows = tiled((tile, here))
    blocks = tiled((group, count, half))
    return call(
        body,
        "finish",
        steps,
        [blocks, rows, rows] + [whole(a.shape) for a in (ffn, cross, self_sum, kv, sums)],
        [
            (patch.shape, F32, blocks),
            (text_keep.shape, F32, rows),
            small_out((3, block, here)),
            small_out((block, here)),
            small_out((block, here)),
            small_out((2, kv.shape[0], here)),
            small_out((block, here)),
            small_out((block, hidden)),
            small_out((block, hidden)),
            small_out((2, here)),
            small_out((2, here)),
            small_out((1, hidden)),
            small_out((3, here)),
            small_out((3, here)),
            small_out((3, here)),
        ],
        [],
        images * count * half,
        images * count * half * 6,
        scalars=1,
    )(side, patch, text_keep, text_other, ffn, cross, self_sum, kv, sums)


def swap_dp(value, bit, shards):
    return lax.ppermute(value, "dp", [(i, i ^ (1 << bit)) for i in range(shards)])


def add_pair(keep, arrived):
    return keep.astype(F32) + arrived.astype(F32)


def split_next(total, position, mine):
    lead = total.shape[0]
    inner = 1 << position
    view = total.reshape((lead // (2 * inner), 2, inner) + total.shape[1:])
    send = lax.dynamic_index_in_dim(view, 1 - mine, 1, keepdims=False)
    keep = lax.dynamic_index_in_dim(view, mine, 1, keepdims=False)
    shape = (lead // 2,) + total.shape[1:]
    return send.reshape(shape).astype(BF), keep.reshape(shape).astype(BF)


class Sum:
    def __init__(self, first, second, join, bits, shards):
        self.bits, self.shards, self.join = bits, shards, join
        self.keep = [first[1], second[1]]
        self.sent = [swap_dp(first[0], 0, shards), swap_dp(second[0], 1, shards)]
        self.bit = 1

    def step(self, *behind):
        arrived = after(self.sent, behind)
        totals = [add_pair(k, a) for k, a in zip(self.keep, arrived)]
        bit, bits, shards = self.bit, self.bits, self.shards
        if bit == 1:
            pairs = [split_next(t, 0, bits[b]) for t, b in zip(totals, (1, 0))]
            self.keep = [keep for _, keep in pairs]
            self.sent = [swap_dp(send, b, shards) for (send, _), b in zip(pairs, (1, 0))]
        else:
            total = totals[0]
            if bit == 2:
                total = jnp.concatenate(totals, axis=self.join)
            if total.shape[0] == 1:
                return total[0]
            send, keep = split_next(total, 0, bits[bit])
            self.keep, self.sent = [keep], [swap_dp(send, bit, shards)]
        self.bit += 1
        return None

    def finish(self):
        done = None
        while done is None:
            done = self.step()
        return done


def after(values, behind):
    if not behind:
        return values
    return lax.optimization_barrier((values, behind))[0]


def sum_dp(value, shards):
    bit = 0
    while (1 << bit) < shards:
        value = value + swap_dp(value, bit, shards)
        bit += 1
    return value


def swap_mp(value):
    return lax.ppermute(value, "mp", [(0, 1), (1, 0)])


def local(
    shards,
    text,
    patches,
    segment_ids,
    row_image,
    self_qkv,
    self_bias,
    self_out,
    cross_query,
    cross_bias,
    cross_kv,
    cross_out,
    ffn_in,
    ffn_in_bias,
    ffn_out,
    branch_bias,
    norm_gain,
    norm_bias,
    cotangent,
):
    rows, length = segment_ids.shape
    images, count, visual = patches.shape
    tokens, here = text.shape
    padded = -(-count // 32) * 32
    tile = 5 * length
    hidden = ffn_in.shape[1]
    dp_at = lax.axis_index("dp")
    mp_at = lax.axis_index("mp")
    side = mp_at.reshape(1).astype(jnp.int32)
    bit_count = max(2, shards.bit_length() - 1)
    bits = (dp_at >> jnp.arange(bit_count, dtype=jnp.int32)) & 1
    bits = bits.astype(jnp.int32)
    bit_at = [(dp_at >> b) & 1 for b in range(bit_count)]

    def both(own):
        other = swap_mp(own)
        return jnp.where(
            mp_at == 0,
            jnp.concatenate((own, other), axis=1),
            jnp.concatenate((other, own), axis=1),
        )

    params = both(jnp.concatenate((branch_bias, norm_gain, norm_bias), axis=0)).astype(F32)
    cot_full = both(cotangent)

    picks = (row_image - dp_at * images).astype(jnp.int32)
    ids = segment_ids + 32 * (jnp.arange(rows, dtype=jnp.int32) % (tile // length))[:, None]
    ids_col = ids.reshape(tokens, 1)
    ids_row = ids.reshape(tokens // tile, 1, tile)
    zero = jnp.zeros((here,), F32)
    qkv_b = jnp.concatenate((self_bias[0].astype(F32), zero, self_bias[1].astype(F32)))[None]

    keys, values = project_patches(patches, cross_kv, cross_bias, padded)
    keys, cot_full = lax.optimization_barrier((keys, cot_full))
    qkv, context, part_one, text_full = self_forward(
        side, text, swap_mp(text), self_qkv, qkv_b, self_out, ids_col, ids_row, tile
    )
    n_one, r_one, y_one, query, cross_ctx, part_two, other_two = cross_forward(
        picks, text_full, part_one, swap_mp(part_one), params, cross_query, cross_bias,
        keys, values, cross_out, tile, length, count, padded,
    )
    n_two, r_two, y_two, act, slope, part_three, other_three = ffn_forward(
        n_one, part_two, other_two.reshape(tokens, -1), params, ffn_in, ffn_in_bias[None], ffn_out, tile
    )
    joined, dh_three, dhb_three, du, part_four, sums_three = ffn_backward(
        side, n_two, part_three, other_three.reshape(tokens, -1), params, cot_full, slope, ffn_in, ffn_out,
        tile,
    )
    other_four = swap_mp(part_four)
    quick = shards == 16
    if quick:
        most, few = 2 * hidden // 3, hidden // 3
        ffn_groups = grad_weight(
            bits,
            [
                (0, [(dhb_three, act, 0, most)]),
                (1, [(dhb_three, act, most, few), (y_two, du, 0, few)]),
                (2, [(y_two, du, few, most)]),
            ],
            shards, "grad_ffn", few,
        )
        ffn_got = [swap_dp(g[0], b, shards) for b, g in enumerate(ffn_groups)]
        part_four, _ = after([part_four, other_four], tuple(g[0] for g in ffn_groups))
        dh_two, dhb_two, dq_cross, part_five, pair, sums_two = cross_backward(
            picks, dh_three, part_four, other_four, params, n_two, r_two, query, keys, values,
            cross_query, cross_out, tile, length, count, padded,
        )
        ffn_got = after(ffn_got, (part_five,))
        (text_keep, text_send, sums_one, ffn_shard), self_pairs, cross_pairs = rows_backward(
            [g[1] for g in ffn_groups], ffn_got, (dhb_two, cross_ctx, y_one, dq_cross), dh_two,
            part_five, params, n_one, r_one, qkv, self_qkv, self_out, ids_col, ids_row,
            text_full, context, tile,
        )
        text_other = swap_mp(text_send)
        patch, cross_shard, self_shard, kv_shard, sums = patch_backward(
            patches, pair, cross_kv, cross_pairs, self_pairs, (sums_one, sums_two, sums_three),
            padded,
        )
        (patch_grad, text_grad, g_qkv, g_so, g_cq, g_kv, g_co, g_fi, g_fo, g_sb, g_cb, g_fb, g_br,
         g_ga, g_sh) = finish(
            side, patch, text_keep, text_other, ffn_shard, cross_shard, self_shard, kv_shard, sums
        )
        return (joined, text_grad, patch_grad, g_qkv, g_sb, g_so.T, g_cq, g_cb, g_kv, g_co.T, g_fi,
                g_fb.reshape(-1), g_fo.T, g_br, g_ga, g_sh)
    ffn_groups = grad_weight(
        bits,
        [(0, [(dhb_three, act, 0, hidden)]), (1, [(y_two, du, 0, hidden)])],
        shards, "grad_ffn", 512,
    )
    ffn_sum = Sum(*ffn_groups, 2, bit_at, shards)

    part_four, _ = after([part_four, other_four], tuple(g[0] for g in ffn_groups))
    dh_two, dhb_two, dq_cross, part_five, pair, sums_two = cross_backward(
        picks, dh_three, part_four, other_four, params, n_two, r_two, query, keys, values,
        cross_query, cross_out, tile, length, count, padded,
    )
    other_five = swap_mp(part_five)
    ffn_sum.step(part_five)
    (out_pair,) = grad_weight(
        bits,
        [(0, [(dhb_two, cross_ctx, 0, here), (y_one, dq_cross, 0, here)])],
        shards, "grad_cross", here,
    )
    kv_pair = grad_weight_patches(bits, patches, pair, padded, shards, 1)
    cross_sum = Sum(out_pair, kv_pair, 1, bit_at, shards)
    ffn_sum.step(kv_pair[0])

    part_five, _ = after([part_five, other_five], (kv_pair[0],))
    dhb_one, dqkv, text_keep, text_send, sums_one = self_backward(
        side, dh_two, part_five, other_five, params, n_one, r_one, qkv, self_qkv, self_out,
        ids_col, ids_row, tile,
    )
    text_other = swap_mp(text_send)
    cross_sum.step(dhb_one)
    ffn_sum.step(dhb_one)
    self_groups = grad_weight(
        bits,
        [
            (0, [(text_full, dqkv, 0, 2 * here)]),
            (1, [(text_full, dqkv, 2 * here, here), (dhb_one, context, 0, here)]),
        ],
        shards, "grad_self", here,
    )
    self_sum = Sum(*self_groups, 2, bit_at, shards)
    cross_sum.step(self_groups[0][0])
    sent = patch_send(side, after([pair], (self_groups[0][0],))[0], cross_kv, images, count, padded)
    ffn_shard = ffn_sum.finish()
    arrived = swap_mp(sent)
    self_sum.step(sent)
    patch_grad = patch_keep(side, pair, cross_kv, arrived, padded)
    cross_shard = cross_sum.finish()
    self_shard = self_sum.finish()
    text_grad = text_keep + text_other.astype(F32)

    def mine(block):
        return jnp.where(mp_at == 0, block[:, :here], block[:, here:])

    smalls = jnp.concatenate(
        (
            mine(sums_one[:3]),
            mine(sums_two[:3]),
            mine(sums_three[:3]),
            sums_one[3].reshape(2, here),
            sums_two[3].reshape(2, here),
            sums_three[4:6].reshape(-1, here),
        ),
        axis=0,
    )
    smalls = sum_dp(smalls, shards)
    block = self_shard.shape[0]
    self_grad = jnp.stack([self_shard[:, i * here : (i + 1) * here] for i in range(3)])
    return (
        joined,
        text_grad,
        patch_grad,
        self_grad,
        smalls[9:11],
        self_shard[:, 3 * here :].T,
        cross_shard[:block, here:],
        smalls[11:13],
        jnp.stack((cross_shard[block:, :here], cross_shard[block:, here:])),
        cross_shard[:block, :here].T,
        ffn_shard[:, hidden:],
        smalls[13:].reshape(-1),
        ffn_shard[:, :hidden].T,
        jnp.stack((smalls[2], smalls[5], smalls[8])),
        jnp.stack((smalls[0], smalls[3], smalls[6])),
        jnp.stack((smalls[1], smalls[4], smalls[7])),
    )


def solution(mesh):
    return jax.shard_map(
        partial(local, mesh.shape["dp"]),
        mesh=mesh,
        in_specs=(
            P("dp", "mp"),
            P("dp", None, None),
            P("dp", None),
            P("dp"),
            P(None, None, "mp"),
            P(None, "mp"),
            P("mp", None),
            P(None, "mp"),
            P(None, "mp"),
            P(None, None, "mp"),
            P("mp", None),
            P(None, "mp"),
            P("mp"),
            P("mp", None),
            P(None, "mp"),
            P(None, "mp"),
            P(None, "mp"),
            P("dp", "mp"),
        ),
        out_specs=(
            P("dp", "mp"),
            P("dp", "mp"),
            P("dp", None, "mp"),
            P(None, "dp", "mp"),
            P(None, "mp"),
            P("mp", "dp"),
            P("dp", "mp"),
            P(None, "mp"),
            P(None, "dp", "mp"),
            P("mp", "dp"),
            P("dp", "mp"),
            P("mp"),
            P("mp", "dp"),
            P(None, "mp"),
            P(None, "mp"),
            P(None, "mp"),
        ),
        check_vma=False,
    )
```

```python
import math
from functools import partial

import jax
import jax.numpy as jnp
from jax import lax
from jax.experimental import pallas as pl
from jax.experimental.pallas import tpu as pltpu
from jax.sharding import PartitionSpec as P

HD = 64
EPS = 1e-06
BIG_NEG = -1000000000.0
SCALE = 0.125
BF = jnp.bfloat16
F32 = jnp.float32
MIB = 1 << 20


def nn(a, b):
    return lax.dot_general(a, b, (((1,), (0,)), ((), ())), preferred_element_type=F32)


def nt(a, b):
    return lax.dot_general(a, b, (((1,), (1,)), ((), ())), preferred_element_type=F32)


def tn(a, b):
    return lax.dot_general(a, b, (((0,), (0,)), ((), ())), preferred_element_type=F32)


def head_mask(width, head, dtype):
    lane = lax.broadcasted_iota(jnp.int32, (1, width), 1)
    return ((lane >= head * HD) & (lane < (head + 1) * HD)).astype(F32).astype(dtype)


def whole(shape):
    zeros = (0,) * len(shape)
    return pl.BlockSpec(shape, lambda i, *_: zeros, pipeline_mode=pl.Buffered(1))


def tiled(shape):
    zeros = (0,) * (len(shape) - 1)
    return pl.BlockSpec(shape, lambda i, *_: (i,) + zeros)


def call(body, name, grid, ins, outs, scratch, flops, nbytes, scalars=0, vmem=63,
         collective=None):
    return pl.pallas_call(
        body,
        name=name,
        out_shape=[jax.ShapeDtypeStruct(s, d) for s, d, _ in outs],
        grid_spec=pltpu.PrefetchScalarGridSpec(
            num_scalar_prefetch=scalars,
            grid=(grid,),
            in_specs=ins,
            out_specs=[spec for _, _, spec in outs],
            scratch_shapes=scratch,
        ),
        compiler_params=pltpu.CompilerParams(
            dimension_semantics=("arbitrary",), vmem_limit_bytes=vmem * MIB,
            collective_id=collective, has_side_effects=collective is not None,
        ),
        cost_estimate=pl.CostEstimate(flops=flops, bytes_accessed=nbytes, transcendentals=0),
    )


def norm(z):
    mu = jnp.mean(z, axis=1, keepdims=True)
    sq = jnp.mean(z * z, axis=1, keepdims=True)
    r = lax.rsqrt(sq - mu * mu + EPS)
    return (z - mu) * r, r


def norm_back(e, n, r, gain):
    a = e * gain
    ma = jnp.mean(a, axis=1, keepdims=True)
    mn = jnp.mean(a * n, axis=1, keepdims=True)
    return r * (a - ma - n * mn)


def colsum(v):
    return jnp.sum(v, axis=0, keepdims=True)


def softmax_cols(s):
    e = jnp.exp(s - jnp.max(s, axis=0, keepdims=True))
    return e * (1.0 / jnp.sum(e, axis=0, keepdims=True))


def softmax_rows(s):
    e = jnp.exp(s - jnp.max(s, axis=1, keepdims=True))
    return e * (1.0 / jnp.sum(e, axis=1, keepdims=True))


MESH = pl.DeviceIdType.MESH


def digit(bit):
    return (lax.axis_index("dp") // (1 << bit)) % 2


def partner(bit):
    dp_at, mp_at = lax.axis_index("dp"), lax.axis_index("mp")
    if bit is None:
        return {"dp": dp_at, "mp": 1 - mp_at}
    return {"dp": dp_at + (1 << bit) - 2 * (1 << bit) * digit(bit), "mp": mp_at}


def remote(source, target, send_sem, got_sem, bit):
    return pltpu.make_async_remote_copy(
        src_ref=source, dst_ref=target, send_sem=send_sem, recv_sem=got_sem,
        device_id=partner(bit), device_id_type=MESH,
    )


def greet(links):
    barrier = pltpu.get_barrier_semaphore()
    for bit in links:
        pl.semaphore_signal(barrier, inc=1, device_id=partner(bit), device_id_type=MESH)


def met(links):
    pl.semaphore_wait(pltpu.get_barrier_semaphore(), len(links))


class Swap:
    def __init__(self, tiles, tile, width):
        self.tiles = tiles
        self.shape = (tiles, tile, width)
        self.scratch = [pltpu.VMEM(self.shape, BF)] + [pltpu.SemaphoreType.DMA((tiles,))] * 2

    def bind(self, target, refs):
        self.target = target
        self.buffer, self.send, self.got = refs

    def copy(self, tile):
        return remote(self.buffer.at[tile], self.target.at[tile], self.send.at[tile],
                      self.got.at[tile], None)

    def put(self, tile, value):
        @pl.when(tile == 0)
        def _():
            met((None,))

        self.buffer[tile] = value
        self.copy(tile).start()

        @pl.when(tile == self.tiles - 1)
        def _():
            for i in range(self.tiles):
                self.copy(i).wait()


def project_patches(patches, cross_kv, bias, padded):
    images, count, visual = patches.shape
    width = cross_kv.shape[2]
    group = 5

    def body(p_ref, w_ref, b_ref, k_ref, v_ref, rows, wcat):
        @pl.when(pl.program_id(0) == 0)
        def _():
            wcat[:, :width] = w_ref[0]
            wcat[:, width:] = w_ref[1]
            rows[...] = jnp.zeros_like(rows)

        for i in range(group):
            rows[padded * i : padded * i + count, :] = p_ref[i]
        out = nn(rows[...], wcat[...])
        k_ref[...] = out[:, :width].astype(BF)
        v_ref[...] = (out[:, width:] + b_ref[1:2, :].astype(F32)).astype(BF)

    tall = (images * padded, width)
    return call(
        body,
        "project_patches",
        images // group,
        [tiled((group, count, visual)), whole(cross_kv.shape), whole(bias.shape)],
        [(tall, BF, tiled((group * padded, width)))] * 2,
        [pltpu.VMEM((group * padded, visual), BF), pltpu.VMEM((visual, 2 * width), BF)],
        2 * images * padded * visual * 2 * width,
        patches.size * 2 + cross_kv.size * 2 + 4 * images * padded * width,
    )(patches, cross_kv, bias)


def self_forward(side, own, other, qkv_w, qkv_b, out_w, ids_col, ids_row, tile):
    tokens, here = own.shape
    width = 2 * here

    def body(side_ref, a_ref, z_ref, w_ref, b_ref, o_ref, ic_ref, ir_ref,
             qkv_ref, c_ref, part_ref, x_ref, wcat):
        @pl.when(pl.program_id(0) == 0)
        def _():
            for s in range(3):
                wcat[:, s * here : (s + 1) * here] = w_ref[s]

        mine, theirs = a_ref[...], z_ref[...]
        first = side_ref[0] == 0
        x_ref[:, :here] = jnp.where(first, mine, theirs)
        x_ref[:, here:] = jnp.where(first, theirs, mine)
        qkv = (nn(x_ref[...], wcat[...]) + b_ref[...]).astype(BF)
        qkv_ref[...] = qkv
        same = ic_ref[...] == ir_ref[0]
        parts = []
        for p in range(here // 128):
            q = qkv[:, 128 * p : 128 * p + 128]
            k = qkv[:, here + 128 * p : here + 128 * p + 128]
            v = qkv[:, 2 * here + 128 * p : 2 * here + 128 * p + 128]
            total = None
            for a in range(2):
                mask = head_mask(128, a, BF)
                s = jnp.where(same, nt(q * mask, k) * SCALE, BIG_NEG)
                o = nn(softmax_rows(s).astype(BF), v * mask)
                total = o if total is None else total + o
            parts.append(total)
        c = jnp.concatenate(parts, axis=1).astype(BF)
        c_ref[...] = c
        part_ref[...] = nn(c, o_ref[...]).astype(BF)

    return call(
        body,
        "self_forward",
        tokens // tile,
        [
            tiled((tile, here)),
            tiled((tile, here)),
            whole(qkv_w.shape),
            whole(qkv_b.shape),
            whole(out_w.shape),
            tiled((tile, 1)),
            tiled((1, 1, tile)),
        ],
        [
            ((tokens, 3 * here), BF, tiled((tile, 3 * here))),
            ((tokens, here), BF, tiled((tile, here))),
            ((tokens, width), BF, tiled((tile, width))),
            ((tokens, width), BF, tiled((tile, width))),
        ],
        [pltpu.VMEM((width, 3 * here), BF)],
        2 * tokens * width * 4 * here,
        tokens * (width + 4 * here + width) * 2 + 4 * width * here * 2,
        scalars=1,
    )(side, own, other, qkv_w, qkv_b, out_w, ids_col, ids_row)


def quads(here):
    return [(at, min(256, here - at)) for at in range(0, here, 256)]


def stacked(rows, span):
    return jnp.concatenate(
        [rows * head_mask(span, h, F32) for h in range(span // HD)], axis=0
    ).astype(BF)


def unstacked(tall, span, length):
    total = None
    for h in range(span // HD):
        piece = tall[h * length : (h + 1) * length] * head_mask(span, h, F32)
        total = piece if total is None else total + piece
    return total


def cross_forward(picks, text, mine, other, params, query_w, query_b, keys, values, out_w,
                  tile, length, count, padded):
    tokens, width = text.shape
    here = out_w.shape[0]
    rows = tile // length
    swap = Swap(tokens // tile, tile, width)
    keys = keys.reshape(-1, padded, here)
    values = values.reshape(-1, padded, here)

    def body(pick, x_ref, m_ref, t_ref, pr_ref, w_ref, b_ref, k_ref, v_ref, o_ref,
             n_ref, r_ref, y_ref, q_ref, c_ref, part_ref, got_ref, q32, c32, *swap_refs):
        swap.bind(got_ref, swap_refs)

        @pl.when(pl.program_id(0) == 0)
        def _():
            greet((None,))

        h = x_ref[...].astype(F32) + (m_ref[...].astype(F32) + t_ref[...].astype(F32)) + pr_ref[0:1, :]
        n, r = norm(h)
        n_ref[...] = n
        r_ref[...] = r
        y = (n * pr_ref[3:4, :] + pr_ref[6:7, :]).astype(BF)
        y_ref[...] = y
        q = nn(y, w_ref[...]) + b_ref[0:1, :].astype(F32)
        q32[...] = q
        q_ref[...] = q.astype(BF)
        base = pl.program_id(0) * rows
        for j in range(rows):
            k_row = k_ref[pick[base + j]]
            v_row = v_ref[pick[base + j]]
            for lo, span in quads(here):
                qs = stacked(q32[j * length : (j + 1) * length, lo : lo + span], span)
                s = nt(qs, k_row[:, lo : lo + span]) * SCALE
                live = lax.broadcasted_iota(jnp.int32, s.shape, 1) < count
                p = softmax_rows(jnp.where(live, s, -1e30))
                o = nn(p.astype(BF), v_row[:, lo : lo + span])
                c32[j * length : (j + 1) * length, lo : lo + span] = unstacked(o, span, length)
        c = c32[...].astype(BF)
        c_ref[...] = c
        part = nn(c, o_ref[...]).astype(BF)
        part_ref[...] = part
        swap.put(pl.program_id(0), part)

    full = tiled((tile, width))
    half = tiled((tile, here))
    return call(
        body,
        "cross_forward",
        tokens // tile,
        [full, full, full, whole(params.shape), whole(query_w.shape), whole(query_b.shape),
         whole(keys.shape), whole(values.shape), whole(out_w.shape)],
        [
            ((tokens, width), F32, full),
            ((tokens, 1), F32, tiled((tile, 1))),
            ((tokens, width), BF, full),
            ((tokens, here), BF, half),
            ((tokens, here), BF, half),
            ((tokens, width), BF, full),
            (swap.shape, BF, pl.BlockSpec(memory_space=pl.ANY)),
        ],
        [pltpu.VMEM((tile, here), F32)] * 2 + swap.scratch,
        2 * tokens * width * 2 * here + 4 * tokens * padded * here * 4,
        tokens * width * 14 + keys.size * 4,
        scalars=1,
        collective=3,
    )(picks, text, mine, other, params, query_w, query_b, keys, values, out_w)


def ffn_forward(normed, mine, other, params, in_w, in_b, out_w, tile):
    tokens, width = normed.shape
    hidden = in_w.shape[1]
    swap = Swap(tokens // tile, tile, width)

    def body(n1_ref, m_ref, t_ref, pr_ref, w_ref, b_ref, o_ref,
             n_ref, r_ref, y_ref, g_ref, d_ref, part_ref, got_ref, *swap_refs):
        swap.bind(got_ref, swap_refs)

        @pl.when(pl.program_id(0) == 0)
        def _():
            greet((None,))

        h = (n1_ref[...] * pr_ref[3:4, :] + pr_ref[6:7, :]) + (
            m_ref[...].astype(F32) + t_ref[...].astype(F32)
        ) + pr_ref[1:2, :]
        n, r = norm(h)
        n_ref[...] = n
        r_ref[...] = r
        y = (n * pr_ref[4:5, :] + pr_ref[7:8, :]).astype(BF)
        y_ref[...] = y
        u = nn(y, w_ref[...]) + b_ref[...].astype(F32)
        phi = 0.5 * (1.0 + lax.erf(u * math.sqrt(0.5)))
        g = (u * phi).astype(BF)
        g_ref[...] = g
        density = jnp.exp(u * u * -0.5) * (1.0 / math.sqrt(2.0 * math.pi))
        d_ref[...] = (phi + u * density).astype(BF)
        part = nn(g, o_ref[...]).astype(BF)
        part_ref[...] = part
        swap.put(pl.program_id(0), part)

    full = tiled((tile, width))
    wide = tiled((tile, hidden))
    return call(
        body,
        "ffn_forward",
        tokens // tile,
        [full, full, full, whole(params.shape), whole(in_w.shape), whole(in_b.shape),
         whole(out_w.shape)],
        [
            ((tokens, width), F32, full),
            ((tokens, 1), F32, tiled((tile, 1))),
            ((tokens, width), BF, full),
            ((tokens, hidden), BF, wide),
            ((tokens, hidden), BF, wide),
            ((tokens, width), BF, full),
            (swap.shape, BF, pl.BlockSpec(memory_space=pl.ANY)),
        ],
        swap.scratch,
        2 * tokens * width * 2 * hidden,
        tokens * width * 16 + tokens * hidden * 4 + width * hidden * 4,
        collective=4,
    )(normed, mine, other, params, in_w, in_b, out_w)


def ffn_backward(side, normed, mine, other, params, cot, slope, in_w, out_w, tile):
    tokens, width = normed.shape
    hidden = in_w.shape[1]
    here = width // 2

    def body(side_ref, n2_ref, m_ref, t_ref, pr_ref, e_ref, d_ref, w_ref, o_ref,
             j_ref, dh_ref, dhb_ref, du_ref, part_ref, sum_ref, wt, ot):
        @pl.when(pl.program_id(0) == 0)
        def _():
            wt[...] = w_ref[...].T
            ot[...] = o_ref[...].T
            sum_ref[...] = jnp.zeros_like(sum_ref)

        h = (n2_ref[...] * pr_ref[4:5, :] + pr_ref[7:8, :]) + (
            m_ref[...].astype(F32) + t_ref[...].astype(F32)
        ) + pr_ref[2:3, :]
        n, r = norm(h)
        joined = n * pr_ref[5:6, :] + pr_ref[8:9, :]
        j_ref[...] = jnp.where(side_ref[0] == 0, joined[:, :here], joined[:, here:])
        e = e_ref[...].astype(F32)
        dh = norm_back(e, n, r, pr_ref[5:6, :])
        dh_ref[...] = dh
        dhb = dh.astype(BF)
        dhb_ref[...] = dhb
        sum_ref[0:1, :] += colsum(e * n)
        sum_ref[1:2, :] += colsum(e)
        sum_ref[2:3, :] += colsum(dh)
        dg = nn(dhb, ot[...]).astype(BF)
        du = dg.astype(F32) * d_ref[...].astype(F32)
        total = colsum(du)
        sum_ref[4:5, :] += total[:, :width]
        sum_ref[5:6, :] += total[:, width:]
        dub = du.astype(BF)
        du_ref[...] = dub
        part_ref[...] = nn(dub, wt[...]).astype(BF)

    full = tiled((tile, width))
    wide = tiled((tile, hidden))
    return call(
        body,
        "ffn_backward",
        tokens // tile,
        [full, full, full, whole(params.shape), full, wide, whole(in_w.shape), whole(out_w.shape)],
        [
            ((tokens, here), F32, tiled((tile, here))),
            ((tokens, width), F32, full),
            ((tokens, width), BF, full),
            ((tokens, hidden), BF, wide),
            ((tokens, width), BF, full),
            ((8, width), F32, whole((8, width))),
        ],
        [pltpu.VMEM((hidden, width), BF), pltpu.VMEM((width, hidden), BF)],
        2 * tokens * width * 2 * hidden,
        tokens * width * 22 + tokens * hidden * 4 + width * hidden * 4,
        scalars=1,
    )(side, normed, mine, other, params, cot, slope, in_w, out_w)


def cross_backward(picks, grad, mine, other, params, normed, spread, query, keys, values,
                   query_w, out_w, tile, length, count, padded):
    tokens, width = grad.shape
    here = out_w.shape[0]
    rows = tile // length
    steps = tokens // tile
    tall = keys.shape[0]

    def body(pick, g_ref, m_ref, t_ref, pr_ref, n_ref, r_ref, q_ref, k_ref, v_ref, w_ref, o_ref,
             dh_ref, dhb_ref, dq_ref, part_ref, kv_ref, sum_ref,
             wt, ot, q32, c32, dq32, dk_acc, dv_acc):
        @pl.when(pl.program_id(0) == 0)
        def _():
            wt[...] = w_ref[...].T
            ot[...] = o_ref[...].T
            sum_ref[...] = jnp.zeros_like(sum_ref)
            dk_acc[...] = jnp.zeros_like(dk_acc)
            dv_acc[...] = jnp.zeros_like(dv_acc)

        e = g_ref[...] + (m_ref[...].astype(F32) + t_ref[...].astype(F32))
        n = n_ref[...]
        dh = norm_back(e, n, r_ref[...], pr_ref[4:5, :])
        dh_ref[...] = dh
        dhb = dh.astype(BF)
        dhb_ref[...] = dhb
        sum_ref[0:1, :] += colsum(e * n)
        sum_ref[1:2, :] += colsum(e)
        sum_ref[2:3, :] += colsum(dh)
        c32[...] = nn(dhb, ot[...])
        q32[...] = q_ref[...].astype(F32)
        base = pl.program_id(0) * rows
        for j in range(rows):
            at = pl.multiple_of(pick[base + j] * padded, padded)
            for lo, span in quads(here):
                here_rows = slice(j * length, (j + 1) * length)
                cols = slice(lo, lo + span)
                qs = stacked(q32[here_rows, cols], span)
                cs = stacked(c32[here_rows, cols], span)
                k = k_ref[pl.ds(at, padded), cols]
                s = nt(k, qs) * SCALE
                live = lax.broadcasted_iota(jnp.int32, s.shape, 0) < count
                p = softmax_cols(jnp.where(live, s, -1e30))
                dp = nt(v_ref[pl.ds(at, padded), cols], cs)
                ds = (p * (dp - jnp.sum(dp * p, axis=0, keepdims=True))).astype(BF)
                dv_acc[pl.ds(at, padded), cols] += nn(p.astype(BF), cs)
                dk_acc[pl.ds(at, padded), cols] += nn(ds, qs) * SCALE
                dq32[here_rows, cols] = unstacked(tn(ds, k), span, length) * SCALE
        dq = dq32[...]
        sum_ref[3:4, :here] += colsum(dq)
        dqb = dq.astype(BF)
        dq_ref[...] = dqb
        part_ref[...] = nn(dqb, wt[...]).astype(BF)

        @pl.when(pl.program_id(0) == steps - 1)
        def _():
            def step(i, total):
                at = pl.ds(pl.multiple_of(i * padded, padded), padded)
                kv_ref[at, :here] = dk_acc[at, :].astype(BF)
                dv = dv_acc[at, :]
                kv_ref[at, here:] = dv.astype(BF)
                return total + colsum(dv)

            total = lax.fori_loop(0, tall // padded, step, jnp.zeros((1, here), F32))
            sum_ref[3:4, here:] = total

    full = tiled((tile, width))
    half = tiled((tile, here))
    return call(
        body,
        "cross_backward",
        steps,
        [full, full, full, whole(params.shape), full, tiled((tile, 1)), half, whole(keys.shape),
         whole(values.shape), whole(query_w.shape), whole(out_w.shape)],
        [
            ((tokens, width), F32, full),
            ((tokens, width), BF, full),
            ((tokens, here), BF, half),
            ((tokens, width), BF, full),
            ((tall, 2 * here), BF, whole((tall, 2 * here))),
            ((8, width), F32, whole((8, width))),
        ],
        [pltpu.VMEM((here, width), BF), pltpu.VMEM((width, here), BF)]
        + [pltpu.VMEM((tile, here), F32)] * 3
        + [pltpu.VMEM((tall, here), F32)] * 2,
        2 * tokens * width * 2 * here + 10 * tokens * padded * here * 4,
        tokens * width * 20 + keys.size * 8,
        scalars=1,
    )(picks, grad, mine, other, params, normed, spread, query, keys, values, query_w, out_w)


def self_tile(grad, mine, other, pr_ref, n, r, q_ref, wt, ot, same, sum_ref, keep_ref, send_ref,
              first, here, between=None):
    e = grad + (mine.astype(F32) + other.astype(F32))
    dh = norm_back(e, n, r, pr_ref[3:4, :])
    dhb = dh.astype(BF)
    sum_ref[0:1, :] += colsum(e * n)
    sum_ref[1:2, :] += colsum(e)
    sum_ref[2:3, :] += colsum(dh)
    dc = nn(dhb, ot[...]).astype(BF)
    grads = [[], [], []]
    for p in range(here // 128):
        if between is not None:
            between(p)
        q = q_ref[:, 128 * p : 128 * p + 128]
        k = q_ref[:, here + 128 * p : here + 128 * p + 128]
        v = q_ref[:, 2 * here + 128 * p : 2 * here + 128 * p + 128]
        c = dc[:, 128 * p : 128 * p + 128]
        sums = [None, None, None]
        for a in range(2):
            mask = head_mask(128, a, BF)
            qm = q * mask
            cm = c * mask
            pt = softmax_cols(jnp.where(same, nt(k, qm) * SCALE, BIG_NEG))
            dp = nt(v, cm)
            ds = (pt * (dp - jnp.sum(dp * pt, axis=0, keepdims=True))).astype(BF)
            new = (tn(ds, k * mask), nn(ds, qm), nn(pt.astype(BF), cm))
            sums = [b if a_ is None else a_ + b for a_, b in zip(sums, new)]
        grads[0].append(sums[0] * SCALE)
        grads[1].append(sums[1] * SCALE)
        grads[2].append(sums[2])
    dq, dk, dv = (jnp.concatenate(g, axis=1) for g in grads)
    sum_ref[3:4, :here] += colsum(dq)
    sum_ref[3:4, here:] += colsum(dv)
    dqkv = jnp.concatenate((dq, dk, dv), axis=1).astype(BF)
    part = nn(dqkv, wt[...])
    keep_ref[...] = jnp.where(first, dh[:, :here] + part[:, :here], dh[:, here:] + part[:, here:])
    send_ref[...] = jnp.where(first, part[:, here:], part[:, :here]).astype(BF)
    return dhb, dqkv


def self_backward(side, grad, mine, other, params, normed, spread, qkv, qkv_w, out_w,
                  ids_col, ids_row, tile):
    tokens, width = grad.shape
    here = out_w.shape[0]

    def body(side_ref, g_ref, m_ref, t_ref, pr_ref, n_ref, r_ref, q_ref, w_ref, o_ref,
             ic_ref, ir_ref, dhb_ref, dq_ref, keep_ref, send_ref, sum_ref, wt, ot):
        @pl.when(pl.program_id(0) == 0)
        def _():
            for s in range(3):
                wt[s * here : (s + 1) * here, :] = w_ref[s].T
            ot[...] = o_ref[...].T
            sum_ref[...] = jnp.zeros_like(sum_ref)

        dhb, dqkv = self_tile(
            g_ref[...], m_ref[...], t_ref[...], pr_ref, n_ref[...], r_ref[...], q_ref, wt, ot,
            ic_ref[...] == ir_ref[0], sum_ref, keep_ref, send_ref, side_ref[0] == 0, here,
        )
        dhb_ref[...] = dhb
        dq_ref[...] = dqkv

    full = tiled((tile, width))
    half = tiled((tile, here))
    return call(
        body,
        "self_backward",
        tokens // tile,
        [full, full, full, whole(params.shape), full, tiled((tile, 1)), tiled((tile, 3 * here)),
         whole(qkv_w.shape), whole(out_w.shape), tiled((tile, 1)), tiled((1, 1, tile))],
        [
            ((tokens, width), BF, full),
            ((tokens, 3 * here), BF, tiled((tile, 3 * here))),
            ((tokens, here), F32, half),
            ((tokens, here), BF, half),
            ((8, width), F32, whole((8, width))),
        ],
        [pltpu.VMEM((3 * here, width), BF), pltpu.VMEM((width, here), BF)],
        2 * tokens * width * 4 * here + 10 * tokens * tile * here,
        tokens * width * 16 + 8 * width * here,
        scalars=1,
    )(side, grad, mine, other, params, normed, spread, qkv, qkv_w, out_w, ids_col, ids_row)


def patch_send(side, pair, cross_kv, images, count, padded):
    width = cross_kv.shape[2]
    visual = cross_kv.shape[1]
    half = visual // 2
    group = 5

    def body(side_ref, p_ref, w_ref, s_ref, wt):
        @pl.when(pl.program_id(0) == 0)
        def _():
            wt[:width, :] = w_ref[0].T
            wt[width:, :] = w_ref[1].T

        out = nn(p_ref[...], wt[...])
        for i in range(group):
            s_ref[i] = out[padded * i : padded * i + count].astype(BF)

    return call(
        body,
        "patch_send",
        images // group,
        [
            tiled((group * padded, 2 * width)),
            pl.BlockSpec((2, half, width), lambda i, s: (0, 1 - s[0], 0), pipeline_mode=pl.Buffered(1)),
        ],
        [((images, count, half), BF, tiled((group, count, half)))],
        [pltpu.VMEM((2 * width, half), BF)],
        2 * images * padded * half * 2 * width,
        images * padded * (2 * width + half) * 2,
        scalars=1,
    )(side, pair, cross_kv)[0]


def patch_keep(side, pair, cross_kv, arrived, padded):
    images, count, half = arrived.shape
    width = cross_kv.shape[2]
    group = 5

    def body(side_ref, p_ref, w_ref, a_ref, o_ref, wt):
        @pl.when(pl.program_id(0) == 0)
        def _():
            wt[:width, :] = w_ref[0].T
            wt[width:, :] = w_ref[1].T

        out = nn(p_ref[...], wt[...])
        for i in range(group):
            o_ref[i] = out[padded * i : padded * i + count] + a_ref[i].astype(F32)

    return call(
        body,
        "patch_keep",
        images // group,
        [
            tiled((group * padded, 2 * width)),
            pl.BlockSpec((2, half, width), lambda i, s: (0, s[0], 0), pipeline_mode=pl.Buffered(1)),
            tiled((group, count, half)),
        ],
        [((images, count, half), F32, tiled((group, count, half)))],
        [pltpu.VMEM((2 * width, half), BF)],
        2 * images * padded * half * 2 * width,
        images * padded * (2 * width + half * 3) * 2,
        scalars=1,
    )(side, pair, cross_kv, arrived)[0]


def shards_of(bit, count):
    return [i for i in range(count) if not (i >> bit) & 1]


def split_rows(acc, send_ref, keep_ref, bits_ref, bit, shards, size):
    mine = bits_ref[bit]
    for slot, shard in enumerate(shards_of(bit, shards)):
        kept = pl.multiple_of((shard + (mine << bit)) * size, size)
        sent = pl.multiple_of((shard + ((1 - mine) << bit)) * size, size)
        keep_ref[slot] = acc[pl.ds(kept, size), :].astype(BF)
        send_ref[slot] = acc[pl.ds(sent, size), :].astype(BF)


def split_outside(full, bit, shards, bits):
    size = full.shape[0] // shards
    inner = 1 << bit
    view = full.reshape(shards // (2 * inner), 2, inner, size, full.shape[1])
    return [
        lax.dynamic_index_in_dim(view, at, 1, keepdims=False).reshape(
            shards // 2, size, full.shape[1]
        )
        for at in (1 - bits[bit], bits[bit])
    ]


def grad_weight(bits, groups, shards, name, tile):
    tokens, width = groups[0][1][0][0].shape
    size = width // shards
    inside = size % 16 == 0
    terms, specs, outs, operands = [], [], [], []
    at = 0
    for number, (bit, members) in enumerate(groups):
        first = at
        for left, right, column, columns in members:
            terms.append((at, columns // tile, number, bit))
            operands += [left, right]
            specs += [
                whole(left.shape),
                pl.BlockSpec(
                    (tokens, tile),
                    lambda i, *_, a=at, n=columns // tile, c=column // tile: (
                        0, c + jnp.clip(i - a, 0, n - 1)),
                ),
            ]
            at += columns // tile
        span = at - first
        if inside:
            for _ in range(2):
                outs.append((
                    (shards // 2, size, span * tile), BF,
                    pl.BlockSpec(
                        (shards // 2, size, tile),
                        lambda i, *_, a=first, n=span: (0, 0, jnp.clip(i - a, 0, n - 1)),
                    ),
                ))
        else:
            outs.append((
                (width, span * tile), BF,
                pl.BlockSpec(
                    (width, tile),
                    lambda i, *_, a=first, n=span: (0, jnp.clip(i - a, 0, n - 1)),
                ),
            ))
    total = at

    def body(bits_ref, *refs):
        ins = refs[: len(operands)]
        results = refs[len(operands) : -2]
        lt, acc = refs[-2:]
        step = pl.program_id(0)
        for which, (start, count, number, bit) in enumerate(terms):
            l_ref, r_ref = ins[2 * which : 2 * which + 2]

            if which == 0 or operands[2 * which] is not operands[2 * which - 2]:
                @pl.when(step == start)
                def _(l_ref=l_ref):
                    lt[...] = l_ref[...].T

            @pl.when((step >= start) & (step < start + count))
            def _(r_ref=r_ref, number=number, bit=bit):
                acc[...] = nn(lt[...], r_ref[...])
                if inside:
                    split_rows(acc, results[2 * number], results[2 * number + 1], bits_ref, bit,
                               shards, size)
                else:
                    results[number][...] = acc[...].astype(BF)

    made = call(
        body,
        name,
        total,
        specs,
        outs,
        [pltpu.VMEM((width, tokens), BF), pltpu.VMEM((width, tile), F32)],
        2 * tokens * width * total * tile,
        tokens * (width + total * tile) * 2 + width * total * tile * 2,
        scalars=1,
    )(bits, *operands)
    if inside:
        return [made[2 * i : 2 * i + 2] for i in range(len(groups))]
    return [split_outside(m, g[0], shards, bits) for m, g in zip(made, groups)]


def grad_weight_patches(bits, patches, pair, padded, shards, bit):
    images, count, visual = patches.shape
    size = visual // shards
    wide = pair.shape[1]
    group = 5
    steps = images // group
    inside = size % 16 == 0

    def body(bits_ref, p_ref, g_ref, *refs):
        rows, acc = refs[-2:]
        at = pl.program_id(0)

        @pl.when(at == 0)
        def _():
            rows[...] = jnp.zeros_like(rows)

        for i in range(group):
            rows[padded * i : padded * i + count, :] = p_ref[i]
        new = tn(rows[...], g_ref[...])

        @pl.when(at == 0)
        def _():
            acc[...] = new

        @pl.when(at > 0)
        def _():
            acc[...] += new

        @pl.when(at == steps - 1)
        def _():
            if inside:
                split_rows(acc, refs[0], refs[1], bits_ref, bit, shards, size)
            else:
                refs[0][...] = acc[...].astype(BF)

    half = (shards // 2, size, wide)
    full = (visual, wide)
    made = call(
        body,
        "grad_weight_patches",
        steps,
        [tiled((group, count, visual)), tiled((group * padded, wide))],
        [(half, BF, whole(half))] * 2 if inside else [(full, BF, whole(full))],
        [pltpu.VMEM((group * padded, visual), BF), pltpu.VMEM((visual, wide), F32)],
        2 * images * padded * visual * wide,
        patches.size * 2 + pair.size * 2 + visual * wide * 2,
        scalars=1,
    )(bits, patches, pair)
    return made if inside else split_outside(made[0], bit, shards, bits)


ORDERS = ((0, 1, 2, 3), (1, 2, 0, 3), (2, 0, 1, 3))
LINKS = (None, 0, 1, 2, 3)
FFN_STEPS = ((2, 0), (3, 2))


class Stream:
    def __init__(self, rows, columns, order, first=0, last=3):
        self.rows, self.columns, self.order = rows, columns, order
        self.first, self.last = first, last

    def shape(self, t):
        return (8 >> t, self.rows, self.columns)

    def position(self, t):
        return sorted(set(self.order) - set(self.order[:t])).index(self.order[t])

    def scratch(self, made):
        steps = range(self.first, self.last + 1)
        shapes = [pltpu.VMEM(self.shape(t), BF) for t in steps]
        for t in range(made, self.last + 1):
            shapes += [pltpu.VMEM(self.shape(t), BF)] * 2
        return shapes + [pltpu.SemaphoreType.DMA((4,))] * 2

    def bind(self, refs, made, given=None):
        size = len(self.scratch(made))
        mine, rest = refs[:size], refs[size:]
        steps = self.last + 1 - self.first
        self.got = {self.first + i: mine[i] for i in range(steps)}
        self.pairs = {}
        for i, t in enumerate(range(made, self.last + 1)):
            self.pairs[t] = mine[steps + 2 * i : steps + 2 * i + 2]
        if given is not None:
            self.pairs[made - 1] = given
        self.sems = mine[-2:]
        return rest

    def copy(self, t):
        return remote(self.pairs[t][0], self.got[t], self.sems[0].at[t], self.sems[1].at[t],
                      self.order[t])

    def start(self, t):
        self.copy(t).start()

    def total(self, t, shard):
        return self.pairs[t][1][shard].astype(F32) + self.got[t][shard].astype(F32)

    def fold(self, t, target):
        mine = digit(self.order[t + 1])
        low = 1 << self.position(t + 1)
        send, keep = target
        for j in range(8 >> (t + 1)):
            base = (j // low) * 2 * low + j % low
            send[j] = self.total(t, base + (1 - mine) * low).astype(BF)
            keep[j] = self.total(t, base + mine * low).astype(BF)

    def advance(self, t):
        self.copy(t).wait()
        self.fold(t, self.pairs[t + 1])
        self.start(t + 1)

    def finish(self):
        self.copy(3).wait()
        return self.total(3, 0)


def split_shards(full, columns, pair, bit, size):
    mine = digit(bit)
    for slot, shard in enumerate(shards_of(bit, 16)):
        kept = pl.multiple_of((shard + mine * (1 << bit)) * size, 16)
        sent = pl.multiple_of((shard + (1 - mine) * (1 << bit)) * size, 16)
        pair[1][slot] = full[pl.ds(kept, size), columns].astype(BF)
        pair[0][slot] = full[pl.ds(sent, size), columns].astype(BF)


def small_out(shape, dtype=F32):
    return (shape, dtype, whole(shape))


def rows_backward(ffn_kept, ffn_got, cross_terms, grad, part, params, normed, spread, qkv,
                  qkv_w, out_w, ids_col, ids_row, text, context, tile):
    tokens, width = grad.shape
    here = out_w.shape[0]
    tiles = tokens // tile
    size = width // 16
    third = 2 * here // 3
    ffn_cols = ffn_kept[0].shape[2]
    self_cols = 4 * here // 3
    dhb_two, cross_ctx, y_one, dq_cross = cross_terms
    begin = 2
    after_self = begin + tiles
    steps = after_self + 4
    ffn = [Stream(size, ffn_cols, order) for order in ORDERS]
    cross = [Stream(size, third, order, 0, 0) for order in ORDERS]
    self_streams = [Stream(size, self_cols, order) for order in ORDERS]

    def body(*refs):
        ffn_refs, refs = refs[:6], refs[6:]
        (l0_ref, r0_ref, l1_ref, r1_ref, g_ref, part_ref, mine_ref, pr_ref, n_ref, r_ref, q_ref,
         w_ref, o_ref, ic_ref, ir_ref, x_ref, c_ref) = refs[:17]
        keep_ref, send_ref, sum_ref, ffn_ref = refs[17:21]
        self_out, cross_out, rest = refs[21:27], refs[27:33], refs[33:]
        (lt, acc, wt, ot, other, dq_all, dhb_all, full, part_sems) = rest[:9]
        ffn_local, ffn_sems, rest = rest[9:15], rest[15], rest[16:]
        for which, stream in enumerate(ffn):
            rest = stream.bind(rest, 1)
            stream.pairs[0] = (None, ffn_local[2 * which])
            stream.got[0] = ffn_local[2 * which + 1]
        for stream in cross:
            rest = stream.bind(rest, 0)
        at = pl.program_id(0)
        side = lax.axis_index("mp")
        loads = [
            pltpu.make_async_copy(ffn_refs[i], ffn_local[i], ffn_sems.at[i]) for i in range(6)
        ]
        part_copy = remote(part_ref, other, part_sems.at[0], part_sems.at[1], None)

        @pl.when(at == 0)
        def _():
            greet(LINKS)
            for load in loads:
                load.start()
            lt[...] = l0_ref[...].T
            sum_ref[...] = jnp.zeros_like(sum_ref)
            met(LINKS)
            part_copy.start()
            for which, stream in enumerate(ffn):
                loads[2 * which].wait()
                loads[2 * which + 1].wait()
                stream.fold(0, stream.pairs[1])
                stream.start(1)
            acc[...] = nn(lt[...], r0_ref[...])
            full[:, :here] = acc[...].astype(BF)

        @pl.when(at == 1)
        def _():
            lt[...] = l1_ref[...].T
            acc[...] = nn(lt[...], r1_ref[...])
            full[:, here : 2 * here] = acc[...].astype(BF)
            for which, stream in enumerate(cross):
                split_shards(full, slice(which * third, (which + 1) * third), stream.pairs[0],
                             stream.order[0], size)
            for s in range(3):
                wt[s * here : (s + 1) * here, :] = w_ref[s].T
            ot[...] = o_ref[...].T
            part_copy.wait()

        def between(pair):
            for t, (step, place) in enumerate(FFN_STEPS):
                if pair != place:
                    continue

                @pl.when(at == begin + step)
                def _(t=t):
                    for stream in ffn:
                        stream.advance(t + 1)
                    if t == 1:
                        for stream in cross:
                            stream.start(0)

        @pl.when((at >= begin) & (at < after_self))
        def _():
            i = at - begin
            dhb, dqkv = self_tile(
                g_ref[...], mine_ref[...], other[i], pr_ref, n_ref[...], r_ref[...], q_ref,
                wt, ot, ic_ref[...] == ir_ref[0], sum_ref, keep_ref, send_ref, side == 0, here,
                between,
            )
            for j in range(tiles):
                @pl.when(i == j)
                def _(j=j):
                    dq_all[j * tile : (j + 1) * tile, :] = dqkv
                    dhb_all[j * tile : (j + 1) * tile, :] = dhb

        for j in range(4):
            @pl.when(at == after_self + j)
            def _(j=j):
                if j == 0:
                    lt[...] = x_ref[...].T
                if j == 3:
                    lt[...] = dhb_all[...].T
                right = c_ref[...] if j == 3 else dq_all[:, j * here : (j + 1) * here]
                acc[...] = nn(lt[...], right)
                full[:, j * here : (j + 1) * here] = acc[...].astype(BF)
                if j == 3:
                    for which, stream in enumerate(self_streams):
                        split_shards(
                            full, slice(which * self_cols, (which + 1) * self_cols),
                            self_out[2 * which : 2 * which + 2], stream.order[0], size,
                        )
                    for which, stream in enumerate(cross):
                        stream.copy(0).wait()
                        stream.fold(0, cross_out[2 * which : 2 * which + 2])
                    for which, stream in enumerate(ffn):
                        ffn_ref[:, which * ffn_cols : (which + 1) * ffn_cols] = stream.finish()

    anywhere = pl.BlockSpec(memory_space=pl.ANY)

    def rows(columns):
        return pl.BlockSpec((tile, columns), lambda i: (jnp.clip(i - begin, 0, tiles - 1), 0))

    ids_spec = pl.BlockSpec((1, 1, tile), lambda i: (jnp.clip(i - begin, 0, tiles - 1), 0, 0))
    ffn_arrays = [a for pair in zip(ffn_kept, ffn_got) for a in pair]
    operands = ffn_arrays + [
        dhb_two, cross_ctx, y_one, dq_cross, grad, part.reshape(tiles, tile, width), part, params,
        normed, spread, qkv, qkv_w, out_w, ids_col, ids_row, text, context,
    ]
    ins = [anywhere] * 6 + [
        whole(dhb_two.shape), whole(cross_ctx.shape), whole(y_one.shape), whole(dq_cross.shape),
        rows(width), anywhere, rows(width), whole(params.shape), rows(width), rows(1),
        rows(3 * here), whole(qkv_w.shape), whole(out_w.shape), rows(1), ids_spec,
        whole(text.shape), whole(context.shape),
    ]
    outs = [
        ((tokens, here), F32, rows(here)),
        ((tokens, here), BF, rows(here)),
        small_out((8, width)),
        small_out((size, 3 * ffn_cols)),
    ]
    outs += [small_out(self_streams[0].shape(0), BF)] * 6
    outs += [small_out(cross[0].shape(1), BF)] * 6
    scratch = [
        pltpu.VMEM((width, tokens), BF),
        pltpu.VMEM((width, here), F32),
        pltpu.VMEM((3 * here, width), BF),
        pltpu.VMEM((width, here), BF),
        pltpu.VMEM((tiles, tile, width), BF),
        pltpu.VMEM((tokens, 3 * here), BF),
        pltpu.VMEM((tokens, width), BF),
        pltpu.VMEM((width, 4 * here), BF),
        pltpu.SemaphoreType.DMA((2,)),
    ]
    scratch += [pltpu.VMEM(ffn[0].shape(0), BF)] * 6 + [pltpu.SemaphoreType.DMA((6,))]
    for stream in ffn:
        stream.first = 1
        scratch += stream.scratch(1)
    for stream in cross:
        scratch += stream.scratch(0)
    made = call(
        body, "rows_backward", steps, ins, outs, scratch,
        2 * tokens * width * 10 * here, tokens * width * 30, collective=1,
    )(*operands)
    return made[:4], [made[4 + 2 * i : 6 + 2 * i] for i in range(3)], [
        made[10 + 2 * i : 12 + 2 * i] for i in range(3)]


def patch_backward(patches, pair, cross_kv, cross_pairs, self_pairs, sums, padded):
    images, count, visual = patches.shape
    width = cross_kv.shape[2]
    half = visual // 2
    wide = 2 * width
    size = visual // 16
    group = 5
    steps = images // group
    small = cross_pairs[0][0].shape[1]
    third = wide // 3
    self_cols = self_pairs[0][0].shape[2]
    cross = [Stream(small, third, order, 1) for order in ORDERS]
    selves = [Stream(small, self_cols, order) for order in ORDERS]
    kvs = [Stream(size, third, order) for order in ORDERS]
    given = list(cross_pairs) + list(self_pairs)

    def body(p_ref, g_ref, w_ref, s1_ref, s2_ref, s3_ref, *refs):
        firsts = [refs[2 * i : 2 * i + 2] for i in range(6)]
        out_ref, cross_ref, self_ref, kv_ref, sum_ref = refs[12:17]
        rows, acc, wt, send, got, send_sem, got_sem, sum_now, sum_got, sum_sems = refs[17:27]
        p_all, g_all, load_sems, out_sems = refs[27:31]
        rest = refs[31:]
        for which, stream in enumerate(cross):
            rest = stream.bind(rest, 2, firsts[which])
        for which, stream in enumerate(selves):
            rest = stream.bind(rest, 1, firsts[3 + which])
        for stream in kvs:
            rest = stream.bind(rest, 0)
        side = lax.axis_index("mp")
        at = pl.program_id(0)

        def patch_copy(tile):
            return remote(send.at[tile], got.at[tile], send_sem.at[tile], got_sem.at[tile], None)

        def loads(tile):
            images_at = pl.ds(tile * group, group)
            rows_at = pl.ds(pl.multiple_of(tile * group * padded, 16), group * padded)
            return (
                pltpu.make_async_copy(p_ref.at[images_at], p_all.at[tile], load_sems.at[2 * tile]),
                pltpu.make_async_copy(g_ref.at[rows_at], g_all.at[tile], load_sems.at[2 * tile + 1]),
            )

        def store(tile):
            images_at = pl.ds(tile * group, group)
            return pltpu.make_async_copy(send.at[tile], out_ref.at[images_at], out_sems.at[tile])

        def sum_copy(bit):
            return remote(sum_now.at[bit], sum_got.at[bit], sum_sems.at[bit],
                          sum_sems.at[4 + bit], bit)

        @pl.when(at == 0)
        def _():
            greet(LINKS)
            for tile in range(steps):
                for load in loads(tile):
                    load.start(priority=1)
            rows[...] = jnp.zeros_like(rows)
            sum_now[0, :8] = s3_ref[...]
            sum_now[0, 8:12] = s1_ref[0:4]
            sum_now[0, 12:16] = s2_ref[0:4]
            met(LINKS)
            sum_copy(0).start()
            for stream in selves:
                stream.start(0)
            for stream in cross:
                stream.start(1)
            wt[:width, :] = w_ref[0].T
            wt[width:, :] = w_ref[1].T

        def sum_next(bit):
            sum_copy(bit).wait()
            sum_now[bit + 1] = sum_now[bit] + sum_got[bit]
            sum_copy(bit + 1).start()

        def advance(streams, t):
            for stream in streams:
                stream.advance(t)

        @pl.when(at == steps - 1)
        def _():
            sum_next(0)
            advance(selves, 0)
            advance(cross, 1)

        @pl.when(at == steps + 1)
        def _():
            sum_next(1)
            advance(selves, 1)
            for stream in kvs:
                stream.start(0)
            advance(cross, 2)

        @pl.when(at == steps + 3)
        def _():
            sum_next(2)
            advance(selves, 2)

        for step in range(3):
            @pl.when(at == 2 * steps + (1, 3, 4)[step])
            def _(step=step):
                advance(kvs, step)

        @pl.when(at < steps)
        def _():
            for load in loads(at):
                load.wait()
            for i in range(group):
                rows[padded * i : padded * i + count, :] = p_all[at, i]
            new = tn(rows[...], g_all[at])

            @pl.when(at == 0)
            def _():
                acc[...] = new

            @pl.when(at > 0)
            def _():
                acc[...] += new

            @pl.when(at == steps - 1)
            def _():
                for which, stream in enumerate(kvs):
                    split_shards(acc, slice(which * third, (which + 1) * third), stream.pairs[0],
                                 stream.order[0], size)

        def product(tile, half_at):
            lanes = pl.ds(pl.multiple_of(half_at * half, 128), half)
            return nn(g_all[tile], wt[:, lanes])

        @pl.when((at >= steps) & (at < 2 * steps))
        def _():
            tile = at - steps
            out = product(tile, 1 - side)
            for i in range(group):
                send[tile, i] = out[padded * i : padded * i + count].astype(BF)
            patch_copy(tile).start()

        @pl.when(at >= 2 * steps)
        def _():
            tile = at - 2 * steps
            out = product(tile, side)
            patch_copy(tile).wait()
            for i in range(group):
                mine = out[padded * i : padded * i + count]
                send[tile, i] = (mine + got[tile, i].astype(F32)).astype(BF)
            store(tile).start(priority=1)

        @pl.when(at == 3 * steps - 1)
        def _():
            sum_copy(3).wait()
            sum_ref[...] = sum_now[3] + sum_got[3]
            for target, streams in ((cross_ref, cross), (self_ref, selves), (kv_ref, kvs)):
                for which, stream in enumerate(streams):
                    lo = which * stream.columns
                    target[:, lo : lo + stream.columns] = stream.finish()
            for tile in range(steps):
                store(tile).wait()

    anywhere = pl.BlockSpec(memory_space=pl.ANY)
    ins = [
        anywhere,
        anywhere,
        whole(cross_kv.shape),
    ] + [whole(s.shape) for s in sums]
    operands = [patches, pair, cross_kv, *sums]
    for sent, kept in given:
        ins += [anywhere, whole(kept.shape)]
        operands += [sent, kept]
    scratch = [
        pltpu.VMEM((group * padded, visual), BF),
        pltpu.VMEM((visual, wide), F32),
        pltpu.VMEM((wide, visual), BF),
        pltpu.VMEM((steps, group, count, half), BF),
        pltpu.VMEM((steps, group, count, half), BF),
        pltpu.SemaphoreType.DMA((steps,)),
        pltpu.SemaphoreType.DMA((steps,)),
        pltpu.VMEM((4, 16, wide), F32),
        pltpu.VMEM((4, 16, wide), F32),
        pltpu.SemaphoreType.DMA((8,)),
        pltpu.VMEM((steps, group, count, visual), BF),
        pltpu.VMEM((steps, group * padded, wide), BF),
        pltpu.SemaphoreType.DMA((2 * steps,)),
        pltpu.SemaphoreType.DMA((steps,)),
    ]
    for stream in cross:
        scratch += stream.scratch(2)
    for stream in selves:
        scratch += stream.scratch(1)
    for stream in kvs:
        scratch += stream.scratch(0)
    return call(
        body,
        "patch_backward",
        3 * steps,
        ins,
        [
            ((images, count, half), BF, anywhere),
            small_out((small, wide)),
            small_out((small, 3 * self_cols)),
            small_out((size, wide)),
            small_out((16, wide)),
        ],
        scratch,
        2 * images * padded * visual * wide * 2,
        patches.size * 2 + pair.size * 6 + images * count * half * 4,
        collective=2,
    )(*operands)


def finish(side, patch, text_keep, text_other, ffn, cross, self_sum, kv, sums):
    images, count, half = patch.shape
    tokens, here = text_keep.shape
    block = ffn.shape[0]
    hidden = ffn.shape[1] // 2
    steps = 5
    tile = tokens // steps
    group = images // steps

    def body(side_ref, p_ref, k_ref, t_ref, f_ref, c_ref, s_ref, v_ref, m_ref,
             patch_out, text_out, qkv_out, so_out, cq_out, kv_out, co_out, fi_out, fo_out,
             sb_out, cb_out, fb_out, br_out, ga_out, sh_out):
        patch_out[...] = p_ref[...].astype(F32)
        text_out[...] = k_ref[...] + t_ref[...].astype(F32)

        @pl.when(pl.program_id(0) == 0)
        def _():
            for i in range(3):
                qkv_out[i] = s_ref[:, i * here : (i + 1) * here]
            so_out[...] = s_ref[:, 3 * here :]
            cq_out[...] = c_ref[:, here:]
            co_out[...] = c_ref[:, :here]
            fi_out[...] = f_ref[:, hidden:]
            fo_out[...] = f_ref[:, :hidden]
            for i in range(2):
                kv_out[i] = v_ref[:, i * here : (i + 1) * here]
                sb_out[i : i + 1, :] = m_ref[11:12, i * here : (i + 1) * here]
                cb_out[i : i + 1, :] = m_ref[15:16, i * here : (i + 1) * here]
                fb_out[:, 2 * i * here : 2 * (i + 1) * here] = m_ref[4 + i : 5 + i, :]
            first = side_ref[0] == 0
            for out, at in ((ga_out, 0), (sh_out, 1), (br_out, 2)):
                for i, row in enumerate((8 + at, 12 + at, at)):
                    out[i : i + 1, :] = jnp.where(
                        first, m_ref[row : row + 1, :here], m_ref[row : row + 1, here:]
                    )

    rows = tiled((tile, here))
    blocks = tiled((group, count, half))
    return call(
        body,
        "finish",
        steps,
        [blocks, rows, rows] + [whole(a.shape) for a in (ffn, cross, self_sum, kv, sums)],
        [
            (patch.shape, F32, blocks),
            (text_keep.shape, F32, rows),
            small_out((3, block, here)),
            small_out((block, here)),
            small_out((block, here)),
            small_out((2, kv.shape[0], here)),
            small_out((block, here)),
            small_out((block, hidden)),
            small_out((block, hidden)),
            small_out((2, here)),
            small_out((2, here)),
            small_out((1, hidden)),
            small_out((3, here)),
            small_out((3, here)),
            small_out((3, here)),
        ],
        [],
        images * count * half,
        images * count * half * 6,
        scalars=1,
    )(side, patch, text_keep, text_other, ffn, cross, self_sum, kv, sums)


def swap_dp(value, bit, shards):
    return lax.ppermute(value, "dp", [(i, i ^ (1 << bit)) for i in range(shards)])


def add_pair(keep, arrived):
    return keep.astype(F32) + arrived.astype(F32)


def split_next(total, position, mine):
    lead = total.shape[0]
    inner = 1 << position
    view = total.reshape((lead // (2 * inner), 2, inner) + total.shape[1:])
    send = lax.dynamic_index_in_dim(view, 1 - mine, 1, keepdims=False)
    keep = lax.dynamic_index_in_dim(view, mine, 1, keepdims=False)
    shape = (lead // 2,) + total.shape[1:]
    return send.reshape(shape).astype(BF), keep.reshape(shape).astype(BF)


class Sum:
    def __init__(self, first, second, join, bits, shards):
        self.bits, self.shards, self.join = bits, shards, join
        self.keep = [first[1], second[1]]
        self.sent = [swap_dp(first[0], 0, shards), swap_dp(second[0], 1, shards)]
        self.bit = 1

    def step(self, *behind):
        arrived = after(self.sent, behind)
        totals = [add_pair(k, a) for k, a in zip(self.keep, arrived)]
        bit, bits, shards = self.bit, self.bits, self.shards
        if bit == 1:
            pairs = [split_next(t, 0, bits[b]) for t, b in zip(totals, (1, 0))]
            self.keep = [keep for _, keep in pairs]
            self.sent = [swap_dp(send, b, shards) for (send, _), b in zip(pairs, (1, 0))]
        else:
            total = totals[0]
            if bit == 2:
                total = jnp.concatenate(totals, axis=self.join)
            if total.shape[0] == 1:
                return total[0]
            send, keep = split_next(total, 0, bits[bit])
            self.keep, self.sent = [keep], [swap_dp(send, bit, shards)]
        self.bit += 1
        return None

    def finish(self):
        done = None
        while done is None:
            done = self.step()
        return done


def after(values, behind):
    if not behind:
        return values
    return lax.optimization_barrier((values, behind))[0]


def sum_dp(value, shards):
    bit = 0
    while (1 << bit) < shards:
        value = value + swap_dp(value, bit, shards)
        bit += 1
    return value


def swap_mp(value):
    return lax.ppermute(value, "mp", [(0, 1), (1, 0)])


def local(
    shards,
    text,
    patches,
    segment_ids,
    row_image,
    self_qkv,
    self_bias,
    self_out,
    cross_query,
    cross_bias,
    cross_kv,
    cross_out,
    ffn_in,
    ffn_in_bias,
    ffn_out,
    branch_bias,
    norm_gain,
    norm_bias,
    cotangent,
):
    rows, length = segment_ids.shape
    images, count, visual = patches.shape
    tokens, here = text.shape
    padded = -(-count // 32) * 32
    tile = 5 * length
    hidden = ffn_in.shape[1]
    dp_at = lax.axis_index("dp")
    mp_at = lax.axis_index("mp")
    side = mp_at.reshape(1).astype(jnp.int32)
    bit_count = max(2, shards.bit_length() - 1)
    bits = (dp_at >> jnp.arange(bit_count, dtype=jnp.int32)) & 1
    bits = bits.astype(jnp.int32)
    bit_at = [(dp_at >> b) & 1 for b in range(bit_count)]

    def both(own):
        other = swap_mp(own)
        return jnp.where(
            mp_at == 0,
            jnp.concatenate((own, other), axis=1),
            jnp.concatenate((other, own), axis=1),
        )

    params = both(jnp.concatenate((branch_bias, norm_gain, norm_bias), axis=0)).astype(F32)
    cot_full = both(cotangent)

    picks = (row_image - dp_at * images).astype(jnp.int32)
    ids = segment_ids + 32 * (jnp.arange(rows, dtype=jnp.int32) % (tile // length))[:, None]
    ids_col = ids.reshape(tokens, 1)
    ids_row = ids.reshape(tokens // tile, 1, tile)
    zero = jnp.zeros((here,), F32)
    qkv_b = jnp.concatenate((self_bias[0].astype(F32), zero, self_bias[1].astype(F32)))[None]

    keys, values = project_patches(patches, cross_kv, cross_bias, padded)
    keys, cot_full = lax.optimization_barrier((keys, cot_full))
    qkv, context, part_one, text_full = self_forward(
        side, text, swap_mp(text), self_qkv, qkv_b, self_out, ids_col, ids_row, tile
    )
    n_one, r_one, y_one, query, cross_ctx, part_two, other_two = cross_forward(
        picks, text_full, part_one, swap_mp(part_one), params, cross_query, cross_bias,
        keys, values, cross_out, tile, length, count, padded,
    )
    n_two, r_two, y_two, act, slope, part_three, other_three = ffn_forward(
        n_one, part_two, other_two.reshape(tokens, -1), params, ffn_in, ffn_in_bias[None], ffn_out, tile
    )
    joined, dh_three, dhb_three, du, part_four, sums_three = ffn_backward(
        side, n_two, part_three, other_three.reshape(tokens, -1), params, cot_full, slope, ffn_in, ffn_out,
        tile,
    )
    other_four = swap_mp(part_four)
    quick = shards == 16
    if quick:
        most, few = 2 * hidden // 3, hidden // 3
        ffn_groups = grad_weight(
            bits,
            [
                (0, [(dhb_three, act, 0, most)]),
                (1, [(dhb_three, act, most, few), (y_two, du, 0, few)]),
                (2, [(y_two, du, few, most)]),
            ],
            shards, "grad_ffn", few,
        )
        ffn_got = [swap_dp(g[0], b, shards) for b, g in enumerate(ffn_groups)]
        part_four, _ = after([part_four, other_four], tuple(g[0] for g in ffn_groups))
        dh_two, dhb_two, dq_cross, part_five, pair, sums_two = cross_backward(
            picks, dh_three, part_four, other_four, params, n_two, r_two, query, keys, values,
            cross_query, cross_out, tile, length, count, padded,
        )
        ffn_got = after(ffn_got, (part_five,))
        (text_keep, text_send, sums_one, ffn_shard), self_pairs, cross_pairs = rows_backward(
            [g[1] for g in ffn_groups], ffn_got, (dhb_two, cross_ctx, y_one, dq_cross), dh_two,
            part_five, params, n_one, r_one, qkv, self_qkv, self_out, ids_col, ids_row,
            text_full, context, tile,
        )
        text_other = swap_mp(text_send)
        patch, cross_shard, self_shard, kv_shard, sums = patch_backward(
            patches, pair, cross_kv, cross_pairs, self_pairs, (sums_one, sums_two, sums_three),
            padded,
        )
        (patch_grad, text_grad, g_qkv, g_so, g_cq, g_kv, g_co, g_fi, g_fo, g_sb, g_cb, g_fb, g_br,
         g_ga, g_sh) = finish(
            side, patch, text_keep, text_other, ffn_shard, cross_shard, self_shard, kv_shard, sums
        )
        return (joined, text_grad, patch_grad, g_qkv, g_sb, g_so.T, g_cq, g_cb, g_kv, g_co.T, g_fi,
                g_fb.reshape(-1), g_fo.T, g_br, g_ga, g_sh)
    ffn_groups = grad_weight(
        bits,
        [(0, [(dhb_three, act, 0, hidden)]), (1, [(y_two, du, 0, hidden)])],
        shards, "grad_ffn", 512,
    )
    ffn_sum = Sum(*ffn_groups, 2, bit_at, shards)

    part_four, _ = after([part_four, other_four], tuple(g[0] for g in ffn_groups))
    dh_two, dhb_two, dq_cross, part_five, pair, sums_two = cross_backward(
        picks, dh_three, part_four, other_four, params, n_two, r_two, query, keys, values,
        cross_query, cross_out, tile, length, count, padded,
    )
    other_five = swap_mp(part_five)
    ffn_sum.step(part_five)
    (out_pair,) = grad_weight(
        bits,
        [(0, [(dhb_two, cross_ctx, 0, here), (y_one, dq_cross, 0, here)])],
        shards, "grad_cross", here,
    )
    kv_pair = grad_weight_patches(bits, patches, pair, padded, shards, 1)
    cross_sum = Sum(out_pair, kv_pair, 1, bit_at, shards)
    ffn_sum.step(kv_pair[0])

    part_five, _ = after([part_five, other_five], (kv_pair[0],))
    dhb_one, dqkv, text_keep, text_send, sums_one = self_backward(
        side, dh_two, part_five, other_five, params, n_one, r_one, qkv, self_qkv, self_out,
        ids_col, ids_row, tile,
    )
    text_other = swap_mp(text_send)
    cross_sum.step(dhb_one)
    ffn_sum.step(dhb_one)
    self_groups = grad_weight(
        bits,
        [
            (0, [(text_full, dqkv, 0, 2 * here)]),
            (1, [(text_full, dqkv, 2 * here, here), (dhb_one, context, 0, here)]),
        ],
        shards, "grad_self", here,
    )
    self_sum = Sum(*self_groups, 2, bit_at, shards)
    cross_sum.step(self_groups[0][0])
    sent = patch_send(side, after([pair], (self_groups[0][0],))[0], cross_kv, images, count, padded)
    ffn_shard = ffn_sum.finish()
    arrived = swap_mp(sent)
    self_sum.step(sent)
    patch_grad = patch_keep(side, pair, cross_kv, arrived, padded)
    cross_shard = cross_sum.finish()
    self_shard = self_sum.finish()
    text_grad = text_keep + text_other.astype(F32)

    def mine(block):
        return jnp.where(mp_at == 0, block[:, :here], block[:, here:])

    smalls = jnp.concatenate(
        (
            mine(sums_one[:3]),
            mine(sums_two[:3]),
            mine(sums_three[:3]),
            sums_one[3].reshape(2, here),
            sums_two[3].reshape(2, here),
            sums_three[4:6].reshape(-1, here),
        ),
        axis=0,
    )
    smalls = sum_dp(smalls, shards)
    block = self_shard.shape[0]
    self_grad = jnp.stack([self_shard[:, i * here : (i + 1) * here] for i in range(3)])
    return (
        joined,
        text_grad,
        patch_grad,
        self_grad,
        smalls[9:11],
        self_shard[:, 3 * here :].T,
        cross_shard[:block, here:],
        smalls[11:13],
        jnp.stack((cross_shard[block:, :here], cross_shard[block:, here:])),
        cross_shard[:block, :here].T,
        ffn_shard[:, hidden:],
        smalls[13:].reshape(-1),
        ffn_shard[:, :hidden].T,
        jnp.stack((smalls[2], smalls[5], smalls[8])),
        jnp.stack((smalls[0], smalls[3], smalls[6])),
        jnp.stack((smalls[1], smalls[4], smalls[7])),
    )


def solution(mesh):
    return jax.shard_map(
        partial(local, mesh.shape["dp"]),
        mesh=mesh,
        in_specs=(
            P("dp", "mp"),
            P("dp", None, None),
            P("dp", None),
            P("dp"),
            P(None, None, "mp"),
            P(None, "mp"),
            P("mp", None),
            P(None, "mp"),
            P(None, "mp"),
            P(None, None, "mp"),
            P("mp", None),
            P(None, "mp"),
            P("mp"),
            P("mp", None),
            P(None, "mp"),
            P(None, "mp"),
            P(None, "mp"),
            P("dp", "mp"),
        ),
        out_specs=(
            P("dp", "mp"),
            P("dp", "mp"),
            P("dp", None, "mp"),
            P(None, "dp", "mp"),
            P(None, "mp"),
            P("mp", "dp"),
            P("dp", "mp"),
            P(None, "mp"),
            P(None, "dp", "mp"),
            P("mp", "dp"),
            P("dp", "mp"),
            P("mp"),
            P("mp", "dp"),
            P(None, "mp"),
            P(None, "mp"),
            P(None, "mp"),
        ),
        check_vma=False,
    )
```

```python
import math
from functools import partial

import jax
import jax.numpy as jnp
from jax import lax
from jax.experimental import pallas as pl
from jax.experimental.pallas import tpu as pltpu
from jax.sharding import PartitionSpec as P

HD = 64
EPS = 1e-06
BIG_NEG = -1000000000.0
SCALE = 0.125
BF = jnp.bfloat16
F32 = jnp.float32
MIB = 1 << 20


def nn(a, b):
    return lax.dot_general(a, b, (((1,), (0,)), ((), ())), preferred_element_type=F32)


def nt(a, b):
    return lax.dot_general(a, b, (((1,), (1,)), ((), ())), preferred_element_type=F32)


def tn(a, b):
    return lax.dot_general(a, b, (((0,), (0,)), ((), ())), preferred_element_type=F32)


def head_mask(width, head, dtype):
    lane = lax.broadcasted_iota(jnp.int32, (1, width), 1)
    return ((lane >= head * HD) & (lane < (head + 1) * HD)).astype(F32).astype(dtype)


def whole(shape):
    zeros = (0,) * len(shape)
    return pl.BlockSpec(shape, lambda i, *_: zeros, pipeline_mode=pl.Buffered(1))


def tiled(shape):
    zeros = (0,) * (len(shape) - 1)
    return pl.BlockSpec(shape, lambda i, *_: (i,) + zeros)


def call(body, name, grid, ins, outs, scratch, flops, nbytes, scalars=0, vmem=63,
         collective=None):
    return pl.pallas_call(
        body,
        name=name,
        out_shape=[jax.ShapeDtypeStruct(s, d) for s, d, _ in outs],
        grid_spec=pltpu.PrefetchScalarGridSpec(
            num_scalar_prefetch=scalars,
            grid=(grid,),
            in_specs=ins,
            out_specs=[spec for _, _, spec in outs],
            scratch_shapes=scratch,
        ),
        compiler_params=pltpu.CompilerParams(
            dimension_semantics=("arbitrary",), vmem_limit_bytes=vmem * MIB,
            collective_id=collective, has_side_effects=collective is not None,
        ),
        cost_estimate=pl.CostEstimate(flops=flops, bytes_accessed=nbytes, transcendentals=0),
    )


def norm(z):
    mu = jnp.mean(z, axis=1, keepdims=True)
    sq = jnp.mean(z * z, axis=1, keepdims=True)
    r = lax.rsqrt(sq - mu * mu + EPS)
    return (z - mu) * r, r


def norm_back(e, n, r, gain):
    a = e * gain
    ma = jnp.mean(a, axis=1, keepdims=True)
    mn = jnp.mean(a * n, axis=1, keepdims=True)
    return r * (a - ma - n * mn)


def colsum(v):
    return jnp.sum(v, axis=0, keepdims=True)


def softmax_cols(s):
    e = jnp.exp(s - jnp.max(s, axis=0, keepdims=True))
    return e * (1.0 / jnp.sum(e, axis=0, keepdims=True))


def softmax_rows(s):
    e = jnp.exp(s - jnp.max(s, axis=1, keepdims=True))
    return e * (1.0 / jnp.sum(e, axis=1, keepdims=True))


MESH = pl.DeviceIdType.MESH


def digit(bit):
    return (lax.axis_index("dp") // (1 << bit)) % 2


def partner(bit):
    dp_at, mp_at = lax.axis_index("dp"), lax.axis_index("mp")
    if bit is None:
        return {"dp": dp_at, "mp": 1 - mp_at}
    return {"dp": dp_at + (1 << bit) - 2 * (1 << bit) * digit(bit), "mp": mp_at}


def remote(source, target, send_sem, got_sem, bit):
    return pltpu.make_async_remote_copy(
        src_ref=source, dst_ref=target, send_sem=send_sem, recv_sem=got_sem,
        device_id=partner(bit), device_id_type=MESH,
    )


def greet(links):
    barrier = pltpu.get_barrier_semaphore()
    for bit in links:
        pl.semaphore_signal(barrier, inc=1, device_id=partner(bit), device_id_type=MESH)


def met(links):
    pl.semaphore_wait(pltpu.get_barrier_semaphore(), len(links))


class Swap:
    def __init__(self, tiles, tile, width):
        self.tiles = tiles
        self.shape = (tiles, tile, width)
        self.scratch = [pltpu.VMEM(self.shape, BF)] + [pltpu.SemaphoreType.DMA((tiles,))] * 2

    def bind(self, target, refs):
        self.target = target
        self.buffer, self.send, self.got = refs

    def copy(self, tile):
        return remote(self.buffer.at[tile], self.target.at[tile], self.send.at[tile],
                      self.got.at[tile], None)

    def put(self, tile, value):
        @pl.when(tile == 0)
        def _():
            met((None,))

        self.buffer[tile] = value
        self.copy(tile).start()

        @pl.when(tile == self.tiles - 1)
        def _():
            for i in range(self.tiles):
                self.copy(i).wait()


def project_patches(patches, cross_kv, bias, padded):
    images, count, visual = patches.shape
    width = cross_kv.shape[2]
    group = 5

    def body(p_ref, w_ref, b_ref, k_ref, v_ref, rows, wcat):
        @pl.when(pl.program_id(0) == 0)
        def _():
            wcat[:, :width] = w_ref[0]
            wcat[:, width:] = w_ref[1]
            rows[...] = jnp.zeros_like(rows)

        for i in range(group):
            rows[padded * i : padded * i + count, :] = p_ref[i]
        out = nn(rows[...], wcat[...])
        k_ref[...] = out[:, :width].astype(BF)
        v_ref[...] = (out[:, width:] + b_ref[1:2, :].astype(F32)).astype(BF)

    tall = (images * padded, width)
    return call(
        body,
        "project_patches",
        images // group,
        [tiled((group, count, visual)), whole(cross_kv.shape), whole(bias.shape)],
        [(tall, BF, tiled((group * padded, width)))] * 2,
        [pltpu.VMEM((group * padded, visual), BF), pltpu.VMEM((visual, 2 * width), BF)],
        2 * images * padded * visual * 2 * width,
        patches.size * 2 + cross_kv.size * 2 + 4 * images * padded * width,
    )(patches, cross_kv, bias)


def self_forward(side, own, other, qkv_w, qkv_b, out_w, ids_col, ids_row, tile):
    tokens, here = own.shape
    width = 2 * here

    def body(side_ref, a_ref, z_ref, w_ref, b_ref, o_ref, ic_ref, ir_ref,
             qkv_ref, c_ref, part_ref, x_ref, wcat):
        @pl.when(pl.program_id(0) == 0)
        def _():
            for s in range(3):
                wcat[:, s * here : (s + 1) * here] = w_ref[s]

        mine, theirs = a_ref[...], z_ref[...]
        first = side_ref[0] == 0
        x_ref[:, :here] = jnp.where(first, mine, theirs)
        x_ref[:, here:] = jnp.where(first, theirs, mine)
        qkv = (nn(x_ref[...], wcat[...]) + b_ref[...]).astype(BF)
        qkv_ref[...] = qkv
        same = ic_ref[...] == ir_ref[0]
        parts = []
        for p in range(here // 128):
            q = qkv[:, 128 * p : 128 * p + 128]
            k = qkv[:, here + 128 * p : here + 128 * p + 128]
            v = qkv[:, 2 * here + 128 * p : 2 * here + 128 * p + 128]
            total = None
            for a in range(2):
                mask = head_mask(128, a, BF)
                s = jnp.where(same, nt(q * mask, k) * SCALE, BIG_NEG)
                o = nn(softmax_rows(s).astype(BF), v * mask)
                total = o if total is None else total + o
            parts.append(total)
        c = jnp.concatenate(parts, axis=1).astype(BF)
        c_ref[...] = c
        part_ref[...] = nn(c, o_ref[...]).astype(BF)

    return call(
        body,
        "self_forward",
        tokens // tile,
        [
            tiled((tile, here)),
            tiled((tile, here)),
            whole(qkv_w.shape),
            whole(qkv_b.shape),
            whole(out_w.shape),
            tiled((tile, 1)),
            tiled((1, 1, tile)),
        ],
        [
            ((tokens, 3 * here), BF, tiled((tile, 3 * here))),
            ((tokens, here), BF, tiled((tile, here))),
            ((tokens, width), BF, tiled((tile, width))),
            ((tokens, width), BF, tiled((tile, width))),
        ],
        [pltpu.VMEM((width, 3 * here), BF)],
        2 * tokens * width * 4 * here,
        tokens * (width + 4 * here + width) * 2 + 4 * width * here * 2,
        scalars=1,
    )(side, own, other, qkv_w, qkv_b, out_w, ids_col, ids_row)


def quads(here):
    return [(at, min(256, here - at)) for at in range(0, here, 256)]


def stacked(rows, span):
    return jnp.concatenate(
        [rows * head_mask(span, h, F32) for h in range(span // HD)], axis=0
    ).astype(BF)


def unstacked(tall, span, length):
    total = None
    for h in range(span // HD):
        piece = tall[h * length : (h + 1) * length] * head_mask(span, h, F32)
        total = piece if total is None else total + piece
    return total


def cross_forward(picks, text, mine, other, params, query_w, query_b, keys, values, out_w,
                  tile, length, count, padded):
    tokens, width = text.shape
    here = out_w.shape[0]
    rows = tile // length
    swap = Swap(tokens // tile, tile, width)
    keys = keys.reshape(-1, padded, here)
    values = values.reshape(-1, padded, here)

    def body(pick, x_ref, m_ref, t_ref, pr_ref, w_ref, b_ref, k_ref, v_ref, o_ref,
             n_ref, r_ref, y_ref, q_ref, c_ref, part_ref, got_ref, q32, c32, *swap_refs):
        swap.bind(got_ref, swap_refs)

        @pl.when(pl.program_id(0) == 0)
        def _():
            greet((None,))

        h = x_ref[...].astype(F32) + (m_ref[...].astype(F32) + t_ref[...].astype(F32)) + pr_ref[0:1, :]
        n, r = norm(h)
        n_ref[...] = n
        r_ref[...] = r
        y = (n * pr_ref[3:4, :] + pr_ref[6:7, :]).astype(BF)
        y_ref[...] = y
        q = nn(y, w_ref[...]) + b_ref[0:1, :].astype(F32)
        q32[...] = q
        q_ref[...] = q.astype(BF)
        base = pl.program_id(0) * rows
        for j in range(rows):
            k_row = k_ref[pick[base + j]]
            v_row = v_ref[pick[base + j]]
            for lo, span in quads(here):
                qs = stacked(q32[j * length : (j + 1) * length, lo : lo + span], span)
                s = nt(qs, k_row[:, lo : lo + span]) * SCALE
                live = lax.broadcasted_iota(jnp.int32, s.shape, 1) < count
                p = softmax_rows(jnp.where(live, s, -1e30))
                o = nn(p.astype(BF), v_row[:, lo : lo + span])
                c32[j * length : (j + 1) * length, lo : lo + span] = unstacked(o, span, length)
        c = c32[...].astype(BF)
        c_ref[...] = c
        part = nn(c, o_ref[...]).astype(BF)
        part_ref[...] = part
        swap.put(pl.program_id(0), part)

    full = tiled((tile, width))
    half = tiled((tile, here))
    return call(
        body,
        "cross_forward",
        tokens // tile,
        [full, full, full, whole(params.shape), whole(query_w.shape), whole(query_b.shape),
         whole(keys.shape), whole(values.shape), whole(out_w.shape)],
        [
            ((tokens, width), F32, full),
            ((tokens, 1), F32, tiled((tile, 1))),
            ((tokens, width), BF, full),
            ((tokens, here), BF, half),
            ((tokens, here), BF, half),
            ((tokens, width), BF, full),
            (swap.shape, BF, pl.BlockSpec(memory_space=pl.ANY)),
        ],
        [pltpu.VMEM((tile, here), F32)] * 2 + swap.scratch,
        2 * tokens * width * 2 * here + 4 * tokens * padded * here * 4,
        tokens * width * 14 + keys.size * 4,
        scalars=1,
        collective=3,
    )(picks, text, mine, other, params, query_w, query_b, keys, values, out_w)


def ffn_forward(normed, mine, other, params, in_w, in_b, out_w, tile):
    tokens, width = normed.shape
    hidden = in_w.shape[1]
    swap = Swap(tokens // tile, tile, width)

    def body(n1_ref, m_ref, t_ref, pr_ref, w_ref, b_ref, o_ref,
             n_ref, r_ref, y_ref, g_ref, d_ref, part_ref, got_ref, *swap_refs):
        swap.bind(got_ref, swap_refs)

        @pl.when(pl.program_id(0) == 0)
        def _():
            greet((None,))

        h = (n1_ref[...] * pr_ref[3:4, :] + pr_ref[6:7, :]) + (
            m_ref[...].astype(F32) + t_ref[...].astype(F32)
        ) + pr_ref[1:2, :]
        n, r = norm(h)
        n_ref[...] = n
        r_ref[...] = r
        y = (n * pr_ref[4:5, :] + pr_ref[7:8, :]).astype(BF)
        y_ref[...] = y
        u = nn(y, w_ref[...]) + b_ref[...].astype(F32)
        phi = 0.5 * (1.0 + lax.erf(u * math.sqrt(0.5)))
        g = (u * phi).astype(BF)
        g_ref[...] = g
        density = jnp.exp(u * u * -0.5) * (1.0 / math.sqrt(2.0 * math.pi))
        d_ref[...] = (phi + u * density).astype(BF)
        part = nn(g, o_ref[...]).astype(BF)
        part_ref[...] = part
        swap.put(pl.program_id(0), part)

    full = tiled((tile, width))
    wide = tiled((tile, hidden))
    return call(
        body,
        "ffn_forward",
        tokens // tile,
        [full, full, full, whole(params.shape), whole(in_w.shape), whole(in_b.shape),
         whole(out_w.shape)],
        [
            ((tokens, width), F32, full),
            ((tokens, 1), F32, tiled((tile, 1))),
            ((tokens, width), BF, full),
            ((tokens, hidden), BF, wide),
            ((tokens, hidden), BF, wide),
            ((tokens, width), BF, full),
            (swap.shape, BF, pl.BlockSpec(memory_space=pl.ANY)),
        ],
        swap.scratch,
        2 * tokens * width * 2 * hidden,
        tokens * width * 16 + tokens * hidden * 4 + width * hidden * 4,
        collective=4,
    )(normed, mine, other, params, in_w, in_b, out_w)


def ffn_backward(side, normed, mine, other, params, cot, slope, in_w, out_w, tile):
    tokens, width = normed.shape
    hidden = in_w.shape[1]
    here = width // 2

    def body(side_ref, n2_ref, m_ref, t_ref, pr_ref, e_ref, d_ref, w_ref, o_ref,
             j_ref, dh_ref, dhb_ref, du_ref, part_ref, sum_ref, wt, ot):
        @pl.when(pl.program_id(0) == 0)
        def _():
            wt[...] = w_ref[...].T
            ot[...] = o_ref[...].T
            sum_ref[...] = jnp.zeros_like(sum_ref)

        h = (n2_ref[...] * pr_ref[4:5, :] + pr_ref[7:8, :]) + (
            m_ref[...].astype(F32) + t_ref[...].astype(F32)
        ) + pr_ref[2:3, :]
        n, r = norm(h)
        joined = n * pr_ref[5:6, :] + pr_ref[8:9, :]
        j_ref[...] = jnp.where(side_ref[0] == 0, joined[:, :here], joined[:, here:])
        e = e_ref[...].astype(F32)
        dh = norm_back(e, n, r, pr_ref[5:6, :])
        dh_ref[...] = dh
        dhb = dh.astype(BF)
        dhb_ref[...] = dhb
        sum_ref[0:1, :] += colsum(e * n)
        sum_ref[1:2, :] += colsum(e)
        sum_ref[2:3, :] += colsum(dh)
        dg = nn(dhb, ot[...]).astype(BF)
        du = dg.astype(F32) * d_ref[...].astype(F32)
        total = colsum(du)
        sum_ref[4:5, :] += total[:, :width]
        sum_ref[5:6, :] += total[:, width:]
        dub = du.astype(BF)
        du_ref[...] = dub
        part_ref[...] = nn(dub, wt[...]).astype(BF)

    full = tiled((tile, width))
    wide = tiled((tile, hidden))
    return call(
        body,
        "ffn_backward",
        tokens // tile,
        [full, full, full, whole(params.shape), full, wide, whole(in_w.shape), whole(out_w.shape)],
        [
            ((tokens, here), F32, tiled((tile, here))),
            ((tokens, width), F32, full),
            ((tokens, width), BF, full),
            ((tokens, hidden), BF, wide),
            ((tokens, width), BF, full),
            ((8, width), F32, whole((8, width))),
        ],
        [pltpu.VMEM((hidden, width), BF), pltpu.VMEM((width, hidden), BF)],
        2 * tokens * width * 2 * hidden,
        tokens * width * 22 + tokens * hidden * 4 + width * hidden * 4,
        scalars=1,
    )(side, normed, mine, other, params, cot, slope, in_w, out_w)


def cross_backward(picks, grad, mine, other, params, normed, spread, query, keys, values,
                   query_w, out_w, tile, length, count, padded):
    tokens, width = grad.shape
    here = out_w.shape[0]
    rows = tile // length
    steps = tokens // tile
    tall = keys.shape[0]

    def body(pick, g_ref, m_ref, t_ref, pr_ref, n_ref, r_ref, q_ref, k_ref, v_ref, w_ref, o_ref,
             dh_ref, dhb_ref, dq_ref, part_ref, kv_ref, sum_ref,
             wt, ot, q32, c32, dq32, dk_acc, dv_acc):
        @pl.when(pl.program_id(0) == 0)
        def _():
            wt[...] = w_ref[...].T
            ot[...] = o_ref[...].T
            sum_ref[...] = jnp.zeros_like(sum_ref)
            dk_acc[...] = jnp.zeros_like(dk_acc)
            dv_acc[...] = jnp.zeros_like(dv_acc)

        e = g_ref[...] + (m_ref[...].astype(F32) + t_ref[...].astype(F32))
        n = n_ref[...]
        dh = norm_back(e, n, r_ref[...], pr_ref[4:5, :])
        dh_ref[...] = dh
        dhb = dh.astype(BF)
        dhb_ref[...] = dhb
        sum_ref[0:1, :] += colsum(e * n)
        sum_ref[1:2, :] += colsum(e)
        sum_ref[2:3, :] += colsum(dh)
        c32[...] = nn(dhb, ot[...])
        q32[...] = q_ref[...].astype(F32)
        base = pl.program_id(0) * rows
        for j in range(rows):
            at = pl.multiple_of(pick[base + j] * padded, padded)
            for lo, span in quads(here):
                here_rows = slice(j * length, (j + 1) * length)
                cols = slice(lo, lo + span)
                qs = stacked(q32[here_rows, cols], span)
                cs = stacked(c32[here_rows, cols], span)
                k = k_ref[pl.ds(at, padded), cols]
                s = nt(k, qs) * SCALE
                live = lax.broadcasted_iota(jnp.int32, s.shape, 0) < count
                p = softmax_cols(jnp.where(live, s, -1e30))
                dp = nt(v_ref[pl.ds(at, padded), cols], cs)
                ds = (p * (dp - jnp.sum(dp * p, axis=0, keepdims=True))).astype(BF)
                dv_acc[pl.ds(at, padded), cols] += nn(p.astype(BF), cs)
                dk_acc[pl.ds(at, padded), cols] += nn(ds, qs) * SCALE
                dq32[here_rows, cols] = unstacked(tn(ds, k), span, length) * SCALE
        dq = dq32[...]
        sum_ref[3:4, :here] += colsum(dq)
        dqb = dq.astype(BF)
        dq_ref[...] = dqb
        part_ref[...] = nn(dqb, wt[...]).astype(BF)

        @pl.when(pl.program_id(0) == steps - 1)
        def _():
            def step(i, total):
                at = pl.ds(pl.multiple_of(i * padded, padded), padded)
                kv_ref[at, :here] = dk_acc[at, :].astype(BF)
                dv = dv_acc[at, :]
                kv_ref[at, here:] = dv.astype(BF)
                return total + colsum(dv)

            total = lax.fori_loop(0, tall // padded, step, jnp.zeros((1, here), F32))
            sum_ref[3:4, here:] = total

    full = tiled((tile, width))
    half = tiled((tile, here))
    return call(
        body,
        "cross_backward",
        steps,
        [full, full, full, whole(params.shape), full, tiled((tile, 1)), half, whole(keys.shape),
         whole(values.shape), whole(query_w.shape), whole(out_w.shape)],
        [
            ((tokens, width), F32, full),
            ((tokens, width), BF, full),
            ((tokens, here), BF, half),
            ((tokens, width), BF, full),
            ((tall, 2 * here), BF, whole((tall, 2 * here))),
            ((8, width), F32, whole((8, width))),
        ],
        [pltpu.VMEM((here, width), BF), pltpu.VMEM((width, here), BF)]
        + [pltpu.VMEM((tile, here), F32)] * 3
        + [pltpu.VMEM((tall, here), F32)] * 2,
        2 * tokens * width * 2 * here + 10 * tokens * padded * here * 4,
        tokens * width * 20 + keys.size * 8,
        scalars=1,
    )(picks, grad, mine, other, params, normed, spread, query, keys, values, query_w, out_w)


def self_tile(grad, mine, other, pr_ref, n, r, q_ref, wt, ot, same, sum_ref, keep_ref, send_ref,
              first, here, between=None):
    e = grad + (mine.astype(F32) + other.astype(F32))
    dh = norm_back(e, n, r, pr_ref[3:4, :])
    dhb = dh.astype(BF)
    sum_ref[0:1, :] += colsum(e * n)
    sum_ref[1:2, :] += colsum(e)
    sum_ref[2:3, :] += colsum(dh)
    dc = nn(dhb, ot[...]).astype(BF)
    grads = [[], [], []]
    for p in range(here // 128):
        if between is not None:
            between(p)
        q = q_ref[:, 128 * p : 128 * p + 128]
        k = q_ref[:, here + 128 * p : here + 128 * p + 128]
        v = q_ref[:, 2 * here + 128 * p : 2 * here + 128 * p + 128]
        c = dc[:, 128 * p : 128 * p + 128]
        sums = [None, None, None]
        for a in range(2):
            mask = head_mask(128, a, BF)
            qm = q * mask
            cm = c * mask
            pt = softmax_cols(jnp.where(same, nt(k, qm) * SCALE, BIG_NEG))
            dp = nt(v, cm)
            ds = (pt * (dp - jnp.sum(dp * pt, axis=0, keepdims=True))).astype(BF)
            new = (tn(ds, k * mask), nn(ds, qm), nn(pt.astype(BF), cm))
            sums = [b if a_ is None else a_ + b for a_, b in zip(sums, new)]
        grads[0].append(sums[0] * SCALE)
        grads[1].append(sums[1] * SCALE)
        grads[2].append(sums[2])
    dq, dk, dv = (jnp.concatenate(g, axis=1) for g in grads)
    sum_ref[3:4, :here] += colsum(dq)
    sum_ref[3:4, here:] += colsum(dv)
    dqkv = jnp.concatenate((dq, dk, dv), axis=1).astype(BF)
    part = nn(dqkv, wt[...])
    keep_ref[...] = jnp.where(first, dh[:, :here] + part[:, :here], dh[:, here:] + part[:, here:])
    send_ref[...] = jnp.where(first, part[:, here:], part[:, :here]).astype(BF)
    return dhb, dqkv


def self_backward(side, grad, mine, other, params, normed, spread, qkv, qkv_w, out_w,
                  ids_col, ids_row, tile):
    tokens, width = grad.shape
    here = out_w.shape[0]

    def body(side_ref, g_ref, m_ref, t_ref, pr_ref, n_ref, r_ref, q_ref, w_ref, o_ref,
             ic_ref, ir_ref, dhb_ref, dq_ref, keep_ref, send_ref, sum_ref, wt, ot):
        @pl.when(pl.program_id(0) == 0)
        def _():
            for s in range(3):
                wt[s * here : (s + 1) * here, :] = w_ref[s].T
            ot[...] = o_ref[...].T
            sum_ref[...] = jnp.zeros_like(sum_ref)

        dhb, dqkv = self_tile(
            g_ref[...], m_ref[...], t_ref[...], pr_ref, n_ref[...], r_ref[...], q_ref, wt, ot,
            ic_ref[...] == ir_ref[0], sum_ref, keep_ref, send_ref, side_ref[0] == 0, here,
        )
        dhb_ref[...] = dhb
        dq_ref[...] = dqkv

    full = tiled((tile, width))
    half = tiled((tile, here))
    return call(
        body,
        "self_backward",
        tokens // tile,
        [full, full, full, whole(params.shape), full, tiled((tile, 1)), tiled((tile, 3 * here)),
         whole(qkv_w.shape), whole(out_w.shape), tiled((tile, 1)), tiled((1, 1, tile))],
        [
            ((tokens, width), BF, full),
            ((tokens, 3 * here), BF, tiled((tile, 3 * here))),
            ((tokens, here), F32, half),
            ((tokens, here), BF, half),
            ((8, width), F32, whole((8, width))),
        ],
        [pltpu.VMEM((3 * here, width), BF), pltpu.VMEM((width, here), BF)],
        2 * tokens * width * 4 * here + 10 * tokens * tile * here,
        tokens * width * 16 + 8 * width * here,
        scalars=1,
    )(side, grad, mine, other, params, normed, spread, qkv, qkv_w, out_w, ids_col, ids_row)


def patch_send(side, pair, cross_kv, images, count, padded):
    width = cross_kv.shape[2]
    visual = cross_kv.shape[1]
    half = visual // 2
    group = 5

    def body(side_ref, p_ref, w_ref, s_ref, wt):
        @pl.when(pl.program_id(0) == 0)
        def _():
            wt[:width, :] = w_ref[0].T
            wt[width:, :] = w_ref[1].T

        out = nn(p_ref[...], wt[...])
        for i in range(group):
            s_ref[i] = out[padded * i : padded * i + count].astype(BF)

    return call(
        body,
        "patch_send",
        images // group,
        [
            tiled((group * padded, 2 * width)),
            pl.BlockSpec((2, half, width), lambda i, s: (0, 1 - s[0], 0), pipeline_mode=pl.Buffered(1)),
        ],
        [((images, count, half), BF, tiled((group, count, half)))],
        [pltpu.VMEM((2 * width, half), BF)],
        2 * images * padded * half * 2 * width,
        images * padded * (2 * width + half) * 2,
        scalars=1,
    )(side, pair, cross_kv)[0]


def patch_keep(side, pair, cross_kv, arrived, padded):
    images, count, half = arrived.shape
    width = cross_kv.shape[2]
    group = 5

    def body(side_ref, p_ref, w_ref, a_ref, o_ref, wt):
        @pl.when(pl.program_id(0) == 0)
        def _():
            wt[:width, :] = w_ref[0].T
            wt[width:, :] = w_ref[1].T

        out = nn(p_ref[...], wt[...])
        for i in range(group):
            o_ref[i] = out[padded * i : padded * i + count] + a_ref[i].astype(F32)

    return call(
        body,
        "patch_keep",
        images // group,
        [
            tiled((group * padded, 2 * width)),
            pl.BlockSpec((2, half, width), lambda i, s: (0, s[0], 0), pipeline_mode=pl.Buffered(1)),
            tiled((group, count, half)),
        ],
        [((images, count, half), F32, tiled((group, count, half)))],
        [pltpu.VMEM((2 * width, half), BF)],
        2 * images * padded * half * 2 * width,
        images * padded * (2 * width + half * 3) * 2,
        scalars=1,
    )(side, pair, cross_kv, arrived)[0]


def shards_of(bit, count):
    return [i for i in range(count) if not (i >> bit) & 1]


def split_rows(acc, send_ref, keep_ref, bits_ref, bit, shards, size):
    mine = bits_ref[bit]
    for slot, shard in enumerate(shards_of(bit, shards)):
        kept = pl.multiple_of((shard + (mine << bit)) * size, size)
        sent = pl.multiple_of((shard + ((1 - mine) << bit)) * size, size)
        keep_ref[slot] = acc[pl.ds(kept, size), :].astype(BF)
        send_ref[slot] = acc[pl.ds(sent, size), :].astype(BF)


def split_outside(full, bit, shards, bits):
    size = full.shape[0] // shards
    inner = 1 << bit
    view = full.reshape(shards // (2 * inner), 2, inner, size, full.shape[1])
    return [
        lax.dynamic_index_in_dim(view, at, 1, keepdims=False).reshape(
            shards // 2, size, full.shape[1]
        )
        for at in (1 - bits[bit], bits[bit])
    ]


def grad_weight(bits, groups, shards, name, tile):
    tokens, width = groups[0][1][0][0].shape
    size = width // shards
    inside = size % 16 == 0
    terms, specs, outs, operands = [], [], [], []
    at = 0
    for number, (bit, members) in enumerate(groups):
        first = at
        for left, right, column, columns in members:
            terms.append((at, columns // tile, number, bit))
            operands += [left, right]
            specs += [
                whole(left.shape),
                pl.BlockSpec(
                    (tokens, tile),
                    lambda i, *_, a=at, n=columns // tile, c=column // tile: (
                        0, c + jnp.clip(i - a, 0, n - 1)),
                ),
            ]
            at += columns // tile
        span = at - first
        if inside:
            for _ in range(2):
                outs.append((
                    (shards // 2, size, span * tile), BF,
                    pl.BlockSpec(
                        (shards // 2, size, tile),
                        lambda i, *_, a=first, n=span: (0, 0, jnp.clip(i - a, 0, n - 1)),
                    ),
                ))
        else:
            outs.append((
                (width, span * tile), BF,
                pl.BlockSpec(
                    (width, tile),
                    lambda i, *_, a=first, n=span: (0, jnp.clip(i - a, 0, n - 1)),
                ),
            ))
    total = at

    def body(bits_ref, *refs):
        ins = refs[: len(operands)]
        results = refs[len(operands) : -2]
        lt, acc = refs[-2:]
        step = pl.program_id(0)
        for which, (start, count, number, bit) in enumerate(terms):
            l_ref, r_ref = ins[2 * which : 2 * which + 2]

            if which == 0 or operands[2 * which] is not operands[2 * which - 2]:
                @pl.when(step == start)
                def _(l_ref=l_ref):
                    lt[...] = l_ref[...].T

            @pl.when((step >= start) & (step < start + count))
            def _(r_ref=r_ref, number=number, bit=bit):
                acc[...] = nn(lt[...], r_ref[...])
                if inside:
                    split_rows(acc, results[2 * number], results[2 * number + 1], bits_ref, bit,
                               shards, size)
                else:
                    results[number][...] = acc[...].astype(BF)

    made = call(
        body,
        name,
        total,
        specs,
        outs,
        [pltpu.VMEM((width, tokens), BF), pltpu.VMEM((width, tile), F32)],
        2 * tokens * width * total * tile,
        tokens * (width + total * tile) * 2 + width * total * tile * 2,
        scalars=1,
    )(bits, *operands)
    if inside:
        return [made[2 * i : 2 * i + 2] for i in range(len(groups))]
    return [split_outside(m, g[0], shards, bits) for m, g in zip(made, groups)]


def grad_weight_patches(bits, patches, pair, padded, shards, bit):
    images, count, visual = patches.shape
    size = visual // shards
    wide = pair.shape[1]
    group = 5
    steps = images // group
    inside = size % 16 == 0

    def body(bits_ref, p_ref, g_ref, *refs):
        rows, acc = refs[-2:]
        at = pl.program_id(0)

        @pl.when(at == 0)
        def _():
            rows[...] = jnp.zeros_like(rows)

        for i in range(group):
            rows[padded * i : padded * i + count, :] = p_ref[i]
        new = tn(rows[...], g_ref[...])

        @pl.when(at == 0)
        def _():
            acc[...] = new

        @pl.when(at > 0)
        def _():
            acc[...] += new

        @pl.when(at == steps - 1)
        def _():
            if inside:
                split_rows(acc, refs[0], refs[1], bits_ref, bit, shards, size)
            else:
                refs[0][...] = acc[...].astype(BF)

    half = (shards // 2, size, wide)
    full = (visual, wide)
    made = call(
        body,
        "grad_weight_patches",
        steps,
        [tiled((group, count, visual)), tiled((group * padded, wide))],
        [(half, BF, whole(half))] * 2 if inside else [(full, BF, whole(full))],
        [pltpu.VMEM((group * padded, visual), BF), pltpu.VMEM((visual, wide), F32)],
        2 * images * padded * visual * wide,
        patches.size * 2 + pair.size * 2 + visual * wide * 2,
        scalars=1,
    )(bits, patches, pair)
    return made if inside else split_outside(made[0], bit, shards, bits)


ORDERS = ((0, 1, 2, 3), (1, 2, 0, 3), (2, 0, 1, 3))
LINKS = (None, 0, 1, 2, 3)
FFN_STEPS = ((2, 0), (3, 2))


class Stream:
    def __init__(self, rows, columns, order, first=0, last=3):
        self.rows, self.columns, self.order = rows, columns, order
        self.first, self.last = first, last

    def shape(self, t):
        return (8 >> t, self.rows, self.columns)

    def position(self, t):
        return sorted(set(self.order) - set(self.order[:t])).index(self.order[t])

    def scratch(self, made):
        steps = range(self.first, self.last + 1)
        shapes = [pltpu.VMEM(self.shape(t), BF) for t in steps]
        for t in range(made, self.last + 1):
            shapes += [pltpu.VMEM(self.shape(t), BF)] * 2
        return shapes + [pltpu.SemaphoreType.DMA((4,))] * 2

    def bind(self, refs, made, given=None):
        size = len(self.scratch(made))
        mine, rest = refs[:size], refs[size:]
        steps = self.last + 1 - self.first
        self.got = {self.first + i: mine[i] for i in range(steps)}
        self.pairs = {}
        for i, t in enumerate(range(made, self.last + 1)):
            self.pairs[t] = mine[steps + 2 * i : steps + 2 * i + 2]
        if given is not None:
            self.pairs[made - 1] = given
        self.sems = mine[-2:]
        return rest

    def copy(self, t):
        return remote(self.pairs[t][0], self.got[t], self.sems[0].at[t], self.sems[1].at[t],
                      self.order[t])

    def start(self, t):
        self.copy(t).start()

    def total(self, t, shard):
        return self.pairs[t][1][shard].astype(F32) + self.got[t][shard].astype(F32)

    def fold(self, t, target):
        mine = digit(self.order[t + 1])
        low = 1 << self.position(t + 1)
        send, keep = target
        for j in range(8 >> (t + 1)):
            base = (j // low) * 2 * low + j % low
            send[j] = self.total(t, base + (1 - mine) * low).astype(BF)
            keep[j] = self.total(t, base + mine * low).astype(BF)

    def advance(self, t):
        self.copy(t).wait()
        self.fold(t, self.pairs[t + 1])
        self.start(t + 1)

    def finish(self):
        self.copy(3).wait()
        return self.total(3, 0)


def split_shards(full, columns, pair, bit, size):
    mine = digit(bit)
    for slot, shard in enumerate(shards_of(bit, 16)):
        kept = pl.multiple_of((shard + mine * (1 << bit)) * size, 16)
        sent = pl.multiple_of((shard + (1 - mine) * (1 << bit)) * size, 16)
        pair[1][slot] = full[pl.ds(kept, size), columns].astype(BF)
        pair[0][slot] = full[pl.ds(sent, size), columns].astype(BF)


def small_out(shape, dtype=F32):
    return (shape, dtype, whole(shape))


def rows_backward(ffn_kept, ffn_got, cross_terms, grad, part, params, normed, spread, qkv,
                  qkv_w, out_w, ids_col, ids_row, text, context, tile):
    tokens, width = grad.shape
    here = out_w.shape[0]
    tiles = tokens // tile
    size = width // 16
    third = 2 * here // 3
    ffn_cols = ffn_kept[0].shape[2]
    self_cols = 4 * here // 3
    dhb_two, cross_ctx, y_one, dq_cross = cross_terms
    begin = 2
    after_self = begin + tiles
    steps = after_self + 4
    ffn = [Stream(size, ffn_cols, order) for order in ORDERS]
    cross = [Stream(size, third, order, 0, 0) for order in ORDERS]
    self_streams = [Stream(size, self_cols, order) for order in ORDERS]

    def body(*refs):
        ffn_refs, refs = refs[:6], refs[6:]
        (l0_ref, r0_ref, l1_ref, r1_ref, g_ref, part_ref, mine_ref, pr_ref, n_ref, r_ref, q_ref,
         w_ref, o_ref, ic_ref, ir_ref, x_ref, c_ref) = refs[:17]
        keep_ref, send_ref, sum_ref, ffn_ref = refs[17:21]
        self_out, cross_out, rest = refs[21:27], refs[27:33], refs[33:]
        (lt, acc, wt, ot, other, dq_all, dhb_all, full, part_sems) = rest[:9]
        ffn_local, ffn_sems, rest = rest[9:15], rest[15], rest[16:]
        for which, stream in enumerate(ffn):
            rest = stream.bind(rest, 1)
            stream.pairs[0] = (None, ffn_local[2 * which])
            stream.got[0] = ffn_local[2 * which + 1]
        for stream in cross:
            rest = stream.bind(rest, 0)
        at = pl.program_id(0)
        side = lax.axis_index("mp")
        loads = [
            pltpu.make_async_copy(ffn_refs[i], ffn_local[i], ffn_sems.at[i]) for i in range(6)
        ]
        part_copy = remote(part_ref, other, part_sems.at[0], part_sems.at[1], None)

        @pl.when(at == 0)
        def _():
            greet(LINKS)
            for load in loads:
                load.start()
            lt[...] = l0_ref[...].T
            sum_ref[...] = jnp.zeros_like(sum_ref)
            met(LINKS)
            part_copy.start()
            for which, stream in enumerate(ffn):
                loads[2 * which].wait()
                loads[2 * which + 1].wait()
                stream.fold(0, stream.pairs[1])
                stream.start(1)
            acc[...] = nn(lt[...], r0_ref[...])
            full[:, :here] = acc[...].astype(BF)

        @pl.when(at == 1)
        def _():
            lt[...] = l1_ref[...].T
            acc[...] = nn(lt[...], r1_ref[...])
            full[:, here : 2 * here] = acc[...].astype(BF)
            for which, stream in enumerate(cross):
                split_shards(full, slice(which * third, (which + 1) * third), stream.pairs[0],
                             stream.order[0], size)
                stream.start(0)
            for s in range(3):
                wt[s * here : (s + 1) * here, :] = w_ref[s].T
            ot[...] = o_ref[...].T
            part_copy.wait()

        def between(pair):
            for t, (step, place) in enumerate(FFN_STEPS):
                if pair != place:
                    continue

                @pl.when(at == begin + step)
                def _(t=t):
                    for stream in ffn:
                        stream.advance(t + 1)

        @pl.when((at >= begin) & (at < after_self))
        def _():
            i = at - begin
            dhb, dqkv = self_tile(
                g_ref[...], mine_ref[...], other[i], pr_ref, n_ref[...], r_ref[...], q_ref,
                wt, ot, ic_ref[...] == ir_ref[0], sum_ref, keep_ref, send_ref, side == 0, here,
                between,
            )
            for j in range(tiles):
                @pl.when(i == j)
                def _(j=j):
                    dq_all[j * tile : (j + 1) * tile, :] = dqkv
                    dhb_all[j * tile : (j + 1) * tile, :] = dhb

        for j in range(4):
            @pl.when(at == after_self + j)
            def _(j=j):
                if j == 0:
                    lt[...] = x_ref[...].T
                if j == 3:
                    lt[...] = dhb_all[...].T
                right = c_ref[...] if j == 3 else dq_all[:, j * here : (j + 1) * here]
                acc[...] = nn(lt[...], right)
                full[:, j * here : (j + 1) * here] = acc[...].astype(BF)
                if j == 3:
                    for which, stream in enumerate(self_streams):
                        split_shards(
                            full, slice(which * self_cols, (which + 1) * self_cols),
                            self_out[2 * which : 2 * which + 2], stream.order[0], size,
                        )
                    for which, stream in enumerate(cross):
                        stream.copy(0).wait()
                        stream.fold(0, cross_out[2 * which : 2 * which + 2])
                    for which, stream in enumerate(ffn):
                        ffn_ref[:, which * ffn_cols : (which + 1) * ffn_cols] = stream.finish()

    anywhere = pl.BlockSpec(memory_space=pl.ANY)

    def rows(columns):
        return pl.BlockSpec((tile, columns), lambda i: (jnp.clip(i - begin, 0, tiles - 1), 0))

    ids_spec = pl.BlockSpec((1, 1, tile), lambda i: (jnp.clip(i - begin, 0, tiles - 1), 0, 0))
    ffn_arrays = [a for pair in zip(ffn_kept, ffn_got) for a in pair]
    operands = ffn_arrays + [
        dhb_two, cross_ctx, y_one, dq_cross, grad, part.reshape(tiles, tile, width), part, params,
        normed, spread, qkv, qkv_w, out_w, ids_col, ids_row, text, context,
    ]
    ins = [anywhere] * 6 + [
        whole(dhb_two.shape), whole(cross_ctx.shape), whole(y_one.shape), whole(dq_cross.shape),
        rows(width), anywhere, rows(width), whole(params.shape), rows(width), rows(1),
        rows(3 * here), whole(qkv_w.shape), whole(out_w.shape), rows(1), ids_spec,
        whole(text.shape), whole(context.shape),
    ]
    outs = [
        ((tokens, here), F32, rows(here)),
        ((tokens, here), BF, rows(here)),
        small_out((8, width)),
        small_out((size, 3 * ffn_cols)),
    ]
    outs += [small_out(self_streams[0].shape(0), BF)] * 6
    outs += [small_out(cross[0].shape(1), BF)] * 6
    scratch = [
        pltpu.VMEM((width, tokens), BF),
        pltpu.VMEM((width, here), F32),
        pltpu.VMEM((3 * here, width), BF),
        pltpu.VMEM((width, here), BF),
        pltpu.VMEM((tiles, tile, width), BF),
        pltpu.VMEM((tokens, 3 * here), BF),
        pltpu.VMEM((tokens, width), BF),
        pltpu.VMEM((width, 4 * here), BF),
        pltpu.SemaphoreType.DMA((2,)),
    ]
    scratch += [pltpu.VMEM(ffn[0].shape(0), BF)] * 6 + [pltpu.SemaphoreType.DMA((6,))]
    for stream in ffn:
        stream.first = 1
        scratch += stream.scratch(1)
    for stream in cross:
        scratch += stream.scratch(0)
    made = call(
        body, "rows_backward", steps, ins, outs, scratch,
        2 * tokens * width * 10 * here, tokens * width * 30, collective=1,
    )(*operands)
    return made[:4], [made[4 + 2 * i : 6 + 2 * i] for i in range(3)], [
        made[10 + 2 * i : 12 + 2 * i] for i in range(3)]


def patch_backward(patches, pair, cross_kv, cross_pairs, self_pairs, sums, padded):
    images, count, visual = patches.shape
    width = cross_kv.shape[2]
    half = visual // 2
    wide = 2 * width
    size = visual // 16
    group = 5
    steps = images // group
    small = cross_pairs[0][0].shape[1]
    third = wide // 3
    self_cols = self_pairs[0][0].shape[2]
    cross = [Stream(small, third, order, 1) for order in ORDERS]
    selves = [Stream(small, self_cols, order) for order in ORDERS]
    kvs = [Stream(size, third, order) for order in ORDERS]
    given = list(cross_pairs) + list(self_pairs)

    def body(p_ref, g_ref, w_ref, s1_ref, s2_ref, s3_ref, *refs):
        firsts = [refs[2 * i : 2 * i + 2] for i in range(6)]
        out_ref, cross_ref, self_ref, kv_ref, sum_ref = refs[12:17]
        rows, acc, wt, send, got, send_sem, got_sem, sum_now, sum_got, sum_sems = refs[17:27]
        p_all, g_all, load_sems, out_sems = refs[27:31]
        rest = refs[31:]
        for which, stream in enumerate(cross):
            rest = stream.bind(rest, 2, firsts[which])
        for which, stream in enumerate(selves):
            rest = stream.bind(rest, 1, firsts[3 + which])
        for stream in kvs:
            rest = stream.bind(rest, 0)
        side = lax.axis_index("mp")
        at = pl.program_id(0)

        def patch_copy(tile):
            return remote(send.at[tile], got.at[tile], send_sem.at[tile], got_sem.at[tile], None)

        def loads(tile):
            images_at = pl.ds(tile * group, group)
            rows_at = pl.ds(pl.multiple_of(tile * group * padded, 16), group * padded)
            return (
                pltpu.make_async_copy(p_ref.at[images_at], p_all.at[tile], load_sems.at[2 * tile]),
                pltpu.make_async_copy(g_ref.at[rows_at], g_all.at[tile], load_sems.at[2 * tile + 1]),
            )

        def store(tile):
            images_at = pl.ds(tile * group, group)
            return pltpu.make_async_copy(send.at[tile], out_ref.at[images_at], out_sems.at[tile])

        def sum_copy(bit):
            return remote(sum_now.at[bit], sum_got.at[bit], sum_sems.at[bit],
                          sum_sems.at[4 + bit], bit)

        @pl.when(at == 0)
        def _():
            greet(LINKS)
            for tile in range(steps):
                for load in loads(tile):
                    load.start(priority=1)
            rows[...] = jnp.zeros_like(rows)
            sum_now[0, :8] = s3_ref[...]
            sum_now[0, 8:12] = s1_ref[0:4]
            sum_now[0, 12:16] = s2_ref[0:4]
            met(LINKS)
            sum_copy(0).start()
            for stream in selves:
                stream.start(0)
            for stream in cross:
                stream.start(1)
            wt[:width, :] = w_ref[0].T
            wt[width:, :] = w_ref[1].T

        def sum_next(bit):
            sum_copy(bit).wait()
            sum_now[bit + 1] = sum_now[bit] + sum_got[bit]
            sum_copy(bit + 1).start()

        def advance(streams, t):
            for stream in streams:
                stream.advance(t)

        @pl.when(at == steps - 1)
        def _():
            sum_next(0)
            advance(selves, 0)
            advance(cross, 1)

        @pl.when(at == steps + 1)
        def _():
            sum_next(1)
            advance(selves, 1)
            for stream in kvs:
                stream.start(0)
            advance(cross, 2)

        @pl.when(at == steps + 3)
        def _():
            sum_next(2)
            advance(selves, 2)

        for step in range(3):
            @pl.when(at == 2 * steps + (1, 3, 4)[step])
            def _(step=step):
                advance(kvs, step)

        @pl.when(at < steps)
        def _():
            for load in loads(at):
                load.wait()
            for i in range(group):
                rows[padded * i : padded * i + count, :] = p_all[at, i]
            new = tn(rows[...], g_all[at])

            @pl.when(at == 0)
            def _():
                acc[...] = new

            @pl.when(at > 0)
            def _():
                acc[...] += new

            @pl.when(at == steps - 1)
            def _():
                for which, stream in enumerate(kvs):
                    split_shards(acc, slice(which * third, (which + 1) * third), stream.pairs[0],
                                 stream.order[0], size)

        def product(tile, half_at):
            lanes = pl.ds(pl.multiple_of(half_at * half, 128), half)
            return nn(g_all[tile], wt[:, lanes])

        @pl.when((at >= steps) & (at < 2 * steps))
        def _():
            tile = at - steps
            out = product(tile, 1 - side)
            for i in range(group):
                send[tile, i] = out[padded * i : padded * i + count].astype(BF)
            patch_copy(tile).start()

        @pl.when(at >= 2 * steps)
        def _():
            tile = at - 2 * steps
            out = product(tile, side)
            patch_copy(tile).wait()
            for i in range(group):
                mine = out[padded * i : padded * i + count]
                send[tile, i] = (mine + got[tile, i].astype(F32)).astype(BF)
            store(tile).start(priority=1)

        @pl.when(at == 3 * steps - 1)
        def _():
            sum_copy(3).wait()
            sum_ref[...] = sum_now[3] + sum_got[3]
            for target, streams in ((cross_ref, cross), (self_ref, selves), (kv_ref, kvs)):
                for which, stream in enumerate(streams):
                    lo = which * stream.columns
                    target[:, lo : lo + stream.columns] = stream.finish()
            for tile in range(steps):
                store(tile).wait()

    anywhere = pl.BlockSpec(memory_space=pl.ANY)
    ins = [
        anywhere,
        anywhere,
        whole(cross_kv.shape),
    ] + [whole(s.shape) for s in sums]
    operands = [patches, pair, cross_kv, *sums]
    for sent, kept in given:
        ins += [anywhere, whole(kept.shape)]
        operands += [sent, kept]
    scratch = [
        pltpu.VMEM((group * padded, visual), BF),
        pltpu.VMEM((visual, wide), F32),
        pltpu.VMEM((wide, visual), BF),
        pltpu.VMEM((steps, group, count, half), BF),
        pltpu.VMEM((steps, group, count, half), BF),
        pltpu.SemaphoreType.DMA((steps,)),
        pltpu.SemaphoreType.DMA((steps,)),
        pltpu.VMEM((4, 16, wide), F32),
        pltpu.VMEM((4, 16, wide), F32),
        pltpu.SemaphoreType.DMA((8,)),
        pltpu.VMEM((steps, group, count, visual), BF),
        pltpu.VMEM((steps, group * padded, wide), BF),
        pltpu.SemaphoreType.DMA((2 * steps,)),
        pltpu.SemaphoreType.DMA((steps,)),
    ]
    for stream in cross:
        scratch += stream.scratch(2)
    for stream in selves:
        scratch += stream.scratch(1)
    for stream in kvs:
        scratch += stream.scratch(0)
    return call(
        body,
        "patch_backward",
        3 * steps,
        ins,
        [
            ((images, count, half), BF, anywhere),
            small_out((small, wide)),
            small_out((small, 3 * self_cols)),
            small_out((size, wide)),
            small_out((16, wide)),
        ],
        scratch,
        2 * images * padded * visual * wide * 2,
        patches.size * 2 + pair.size * 6 + images * count * half * 4,
        collective=2,
    )(*operands)


def finish(side, patch, text_keep, text_other, ffn, cross, self_sum, kv, sums):
    images, count, half = patch.shape
    tokens, here = text_keep.shape
    block = ffn.shape[0]
    hidden = ffn.shape[1] // 2
    steps = 5
    tile = tokens // steps
    group = images // steps

    def body(side_ref, p_ref, k_ref, t_ref, f_ref, c_ref, s_ref, v_ref, m_ref,
             patch_out, text_out, qkv_out, so_out, cq_out, kv_out, co_out, fi_out, fo_out,
             sb_out, cb_out, fb_out, br_out, ga_out, sh_out):
        patch_out[...] = p_ref[...].astype(F32)
        text_out[...] = k_ref[...] + t_ref[...].astype(F32)

        @pl.when(pl.program_id(0) == 0)
        def _():
            for i in range(3):
                qkv_out[i] = s_ref[:, i * here : (i + 1) * here]
            so_out[...] = s_ref[:, 3 * here :]
            cq_out[...] = c_ref[:, here:]
            co_out[...] = c_ref[:, :here]
            fi_out[...] = f_ref[:, hidden:]
            fo_out[...] = f_ref[:, :hidden]
            for i in range(2):
                kv_out[i] = v_ref[:, i * here : (i + 1) * here]
                sb_out[i : i + 1, :] = m_ref[11:12, i * here : (i + 1) * here]
                cb_out[i : i + 1, :] = m_ref[15:16, i * here : (i + 1) * here]
                fb_out[:, 2 * i * here : 2 * (i + 1) * here] = m_ref[4 + i : 5 + i, :]
            first = side_ref[0] == 0
            for out, at in ((ga_out, 0), (sh_out, 1), (br_out, 2)):
                for i, row in enumerate((8 + at, 12 + at, at)):
                    out[i : i + 1, :] = jnp.where(
                        first, m_ref[row : row + 1, :here], m_ref[row : row + 1, here:]
                    )

    rows = tiled((tile, here))
    blocks = tiled((group, count, half))
    return call(
        body,
        "finish",
        steps,
        [blocks, rows, rows] + [whole(a.shape) for a in (ffn, cross, self_sum, kv, sums)],
        [
            (patch.shape, F32, blocks),
            (text_keep.shape, F32, rows),
            small_out((3, block, here)),
            small_out((block, here)),
            small_out((block, here)),
            small_out((2, kv.shape[0], here)),
            small_out((block, here)),
            small_out((block, hidden)),
            small_out((block, hidden)),
            small_out((2, here)),
            small_out((2, here)),
            small_out((1, hidden)),
            small_out((3, here)),
            small_out((3, here)),
            small_out((3, here)),
        ],
        [],
        images * count * half,
        images * count * half * 6,
        scalars=1,
    )(side, patch, text_keep, text_other, ffn, cross, self_sum, kv, sums)


def swap_dp(value, bit, shards):
    return lax.ppermute(value, "dp", [(i, i ^ (1 << bit)) for i in range(shards)])


def add_pair(keep, arrived):
    return keep.astype(F32) + arrived.astype(F32)


def split_next(total, position, mine):
    lead = total.shape[0]
    inner = 1 << position
    view = total.reshape((lead // (2 * inner), 2, inner) + total.shape[1:])
    send = lax.dynamic_index_in_dim(view, 1 - mine, 1, keepdims=False)
    keep = lax.dynamic_index_in_dim(view, mine, 1, keepdims=False)
    shape = (lead // 2,) + total.shape[1:]
    return send.reshape(shape).astype(BF), keep.reshape(shape).astype(BF)


class Sum:
    def __init__(self, first, second, join, bits, shards):
        self.bits, self.shards, self.join = bits, shards, join
        self.keep = [first[1], second[1]]
        self.sent = [swap_dp(first[0], 0, shards), swap_dp(second[0], 1, shards)]
        self.bit = 1

    def step(self, *behind):
        arrived = after(self.sent, behind)
        totals = [add_pair(k, a) for k, a in zip(self.keep, arrived)]
        bit, bits, shards = self.bit, self.bits, self.shards
        if bit == 1:
            pairs = [split_next(t, 0, bits[b]) for t, b in zip(totals, (1, 0))]
            self.keep = [keep for _, keep in pairs]
            self.sent = [swap_dp(send, b, shards) for (send, _), b in zip(pairs, (1, 0))]
        else:
            total = totals[0]
            if bit == 2:
                total = jnp.concatenate(totals, axis=self.join)
            if total.shape[0] == 1:
                return total[0]
            send, keep = split_next(total, 0, bits[bit])
            self.keep, self.sent = [keep], [swap_dp(send, bit, shards)]
        self.bit += 1
        return None

    def finish(self):
        done = None
        while done is None:
            done = self.step()
        return done


def after(values, behind):
    if not behind:
        return values
    return lax.optimization_barrier((values, behind))[0]


def sum_dp(value, shards):
    bit = 0
    while (1 << bit) < shards:
        value = value + swap_dp(value, bit, shards)
        bit += 1
    return value


def swap_mp(value):
    return lax.ppermute(value, "mp", [(0, 1), (1, 0)])


def local(
    shards,
    text,
    patches,
    segment_ids,
    row_image,
    self_qkv,
    self_bias,
    self_out,
    cross_query,
    cross_bias,
    cross_kv,
    cross_out,
    ffn_in,
    ffn_in_bias,
    ffn_out,
    branch_bias,
    norm_gain,
    norm_bias,
    cotangent,
):
    rows, length = segment_ids.shape
    images, count, visual = patches.shape
    tokens, here = text.shape
    padded = -(-count // 32) * 32
    tile = 5 * length
    hidden = ffn_in.shape[1]
    dp_at = lax.axis_index("dp")
    mp_at = lax.axis_index("mp")
    side = mp_at.reshape(1).astype(jnp.int32)
    bit_count = max(2, shards.bit_length() - 1)
    bits = (dp_at >> jnp.arange(bit_count, dtype=jnp.int32)) & 1
    bits = bits.astype(jnp.int32)
    bit_at = [(dp_at >> b) & 1 for b in range(bit_count)]

    def both(own):
        other = swap_mp(own)
        return jnp.where(
            mp_at == 0,
            jnp.concatenate((own, other), axis=1),
            jnp.concatenate((other, own), axis=1),
        )

    params = both(jnp.concatenate((branch_bias, norm_gain, norm_bias), axis=0)).astype(F32)
    cot_full = both(cotangent)

    picks = (row_image - dp_at * images).astype(jnp.int32)
    ids = segment_ids + 32 * (jnp.arange(rows, dtype=jnp.int32) % (tile // length))[:, None]
    ids_col = ids.reshape(tokens, 1)
    ids_row = ids.reshape(tokens // tile, 1, tile)
    zero = jnp.zeros((here,), F32)
    qkv_b = jnp.concatenate((self_bias[0].astype(F32), zero, self_bias[1].astype(F32)))[None]

    keys, values = project_patches(patches, cross_kv, cross_bias, padded)
    keys, cot_full = lax.optimization_barrier((keys, cot_full))
    qkv, context, part_one, text_full = self_forward(
        side, text, swap_mp(text), self_qkv, qkv_b, self_out, ids_col, ids_row, tile
    )
    n_one, r_one, y_one, query, cross_ctx, part_two, other_two = cross_forward(
        picks, text_full, part_one, swap_mp(part_one), params, cross_query, cross_bias,
        keys, values, cross_out, tile, length, count, padded,
    )
    n_two, r_two, y_two, act, slope, part_three, other_three = ffn_forward(
        n_one, part_two, other_two.reshape(tokens, -1), params, ffn_in, ffn_in_bias[None], ffn_out, tile
    )
    joined, dh_three, dhb_three, du, part_four, sums_three = ffn_backward(
        side, n_two, part_three, other_three.reshape(tokens, -1), params, cot_full, slope, ffn_in, ffn_out,
        tile,
    )
    other_four = swap_mp(part_four)
    quick = shards == 16
    if quick:
        most, few = 2 * hidden // 3, hidden // 3
        ffn_groups = grad_weight(
            bits,
            [
                (0, [(dhb_three, act, 0, most)]),
                (1, [(dhb_three, act, most, few), (y_two, du, 0, few)]),
                (2, [(y_two, du, few, most)]),
            ],
            shards, "grad_ffn", few,
        )
        ffn_got = [swap_dp(g[0], b, shards) for b, g in enumerate(ffn_groups)]
        part_four, _ = after([part_four, other_four], tuple(g[0] for g in ffn_groups))
        dh_two, dhb_two, dq_cross, part_five, pair, sums_two = cross_backward(
            picks, dh_three, part_four, other_four, params, n_two, r_two, query, keys, values,
            cross_query, cross_out, tile, length, count, padded,
        )
        ffn_got = after(ffn_got, (part_five,))
        (text_keep, text_send, sums_one, ffn_shard), self_pairs, cross_pairs = rows_backward(
            [g[1] for g in ffn_groups], ffn_got, (dhb_two, cross_ctx, y_one, dq_cross), dh_two,
            part_five, params, n_one, r_one, qkv, self_qkv, self_out, ids_col, ids_row,
            text_full, context, tile,
        )
        text_other = swap_mp(text_send)
        patch, cross_shard, self_shard, kv_shard, sums = patch_backward(
            patches, pair, cross_kv, cross_pairs, self_pairs, (sums_one, sums_two, sums_three),
            padded,
        )
        (patch_grad, text_grad, g_qkv, g_so, g_cq, g_kv, g_co, g_fi, g_fo, g_sb, g_cb, g_fb, g_br,
         g_ga, g_sh) = finish(
            side, patch, text_keep, text_other, ffn_shard, cross_shard, self_shard, kv_shard, sums
        )
        return (joined, text_grad, patch_grad, g_qkv, g_sb, g_so.T, g_cq, g_cb, g_kv, g_co.T, g_fi,
                g_fb.reshape(-1), g_fo.T, g_br, g_ga, g_sh)
    ffn_groups = grad_weight(
        bits,
        [(0, [(dhb_three, act, 0, hidden)]), (1, [(y_two, du, 0, hidden)])],
        shards, "grad_ffn", 512,
    )
    ffn_sum = Sum(*ffn_groups, 2, bit_at, shards)

    part_four, _ = after([part_four, other_four], tuple(g[0] for g in ffn_groups))
    dh_two, dhb_two, dq_cross, part_five, pair, sums_two = cross_backward(
        picks, dh_three, part_four, other_four, params, n_two, r_two, query, keys, values,
        cross_query, cross_out, tile, length, count, padded,
    )
    other_five = swap_mp(part_five)
    ffn_sum.step(part_five)
    (out_pair,) = grad_weight(
        bits,
        [(0, [(dhb_two, cross_ctx, 0, here), (y_one, dq_cross, 0, here)])],
        shards, "grad_cross", here,
    )
    kv_pair = grad_weight_patches(bits, patches, pair, padded, shards, 1)
    cross_sum = Sum(out_pair, kv_pair, 1, bit_at, shards)
    ffn_sum.step(kv_pair[0])

    part_five, _ = after([part_five, other_five], (kv_pair[0],))
    dhb_one, dqkv, text_keep, text_send, sums_one = self_backward(
        side, dh_two, part_five, other_five, params, n_one, r_one, qkv, self_qkv, self_out,
        ids_col, ids_row, tile,
    )
    text_other = swap_mp(text_send)
    cross_sum.step(dhb_one)
    ffn_sum.step(dhb_one)
    self_groups = grad_weight(
        bits,
        [
            (0, [(text_full, dqkv, 0, 2 * here)]),
            (1, [(text_full, dqkv, 2 * here, here), (dhb_one, context, 0, here)]),
        ],
        shards, "grad_self", here,
    )
    self_sum = Sum(*self_groups, 2, bit_at, shards)
    cross_sum.step(self_groups[0][0])
    sent = patch_send(side, after([pair], (self_groups[0][0],))[0], cross_kv, images, count, padded)
    ffn_shard = ffn_sum.finish()
    arrived = swap_mp(sent)
    self_sum.step(sent)
    patch_grad = patch_keep(side, pair, cross_kv, arrived, padded)
    cross_shard = cross_sum.finish()
    self_shard = self_sum.finish()
    text_grad = text_keep + text_other.astype(F32)

    def mine(block):
        return jnp.where(mp_at == 0, block[:, :here], block[:, here:])

    smalls = jnp.concatenate(
        (
            mine(sums_one[:3]),
            mine(sums_two[:3]),
            mine(sums_three[:3]),
            sums_one[3].reshape(2, here),
            sums_two[3].reshape(2, here),
            sums_three[4:6].reshape(-1, here),
        ),
        axis=0,
    )
    smalls = sum_dp(smalls, shards)
    block = self_shard.shape[0]
    self_grad = jnp.stack([self_shard[:, i * here : (i + 1) * here] for i in range(3)])
    return (
        joined,
        text_grad,
        patch_grad,
        self_grad,
        smalls[9:11],
        self_shard[:, 3 * here :].T,
        cross_shard[:block, here:],
        smalls[11:13],
        jnp.stack((cross_shard[block:, :here], cross_shard[block:, here:])),
        cross_shard[:block, :here].T,
        ffn_shard[:, hidden:],
        smalls[13:].reshape(-1),
        ffn_shard[:, :hidden].T,
        jnp.stack((smalls[2], smalls[5], smalls[8])),
        jnp.stack((smalls[0], smalls[3], smalls[6])),
        jnp.stack((smalls[1], smalls[4], smalls[7])),
    )


def solution(mesh):
    return jax.shard_map(
        partial(local, mesh.shape["dp"]),
        mesh=mesh,
        in_specs=(
            P("dp", "mp"),
            P("dp", None, None),
            P("dp", None),
            P("dp"),
            P(None, None, "mp"),
            P(None, "mp"),
            P("mp", None),
            P(None, "mp"),
            P(None, "mp"),
            P(None, None, "mp"),
            P("mp", None),
            P(None, "mp"),
            P("mp"),
            P("mp", None),
            P(None, "mp"),
            P(None, "mp"),
            P(None, "mp"),
            P("dp", "mp"),
        ),
        out_specs=(
            P("dp", "mp"),
            P("dp", "mp"),
            P("dp", None, "mp"),
            P(None, "dp", "mp"),
            P(None, "mp"),
            P("mp", "dp"),
            P("dp", "mp"),
            P(None, "mp"),
            P(None, "dp", "mp"),
            P("mp", "dp"),
            P("dp", "mp"),
            P("mp"),
            P("mp", "dp"),
            P(None, "mp"),
            P(None, "mp"),
            P(None, "mp"),
        ),
        check_vma=False,
    )
```
